512 devices in a mesh: row: 32 (over x, z), col: 16 (over y, core).
Axes of the slice: x: 4, y: 8, z: 8, core: 2. Of those that a mesh axis runs over, the one named last changes fastest.
Arguments:
- charges: float32 [524288], P(('row', 'col')), may hold values from -0.5 to 1.5
- structure_id: int32 [524288], P(('row', 'col')), may hold values from 0 to 4095, as said below
- live_count: int32 [512], P(('row', 'col')), may hold values from 512 to 1024, as said below
- cell_index: int32 [3, 524288], P(None, ('row', 'col')), may hold values from 0 to 255, as said below
- fraction: float32 [3, 524288], P(None, ('row', 'col')), may hold values from 0 to 1
- influence: float32 [256, 256, 256], P('col', 'row'), may hold values from 0.1 to 10
Outputs:
- forces: float32 [3, 524288], P(None, ('row', 'col'))
- atom_energy: float32 [524288], P(('row', 'col'))
The draws below stay inside these ranges and needn't reach their ends.
Inputs may be any that keep to these rules, and one draw needn't show every extreme that they name: `structure_id`: devices are numbered row-major over (row, col). Slots 0 to 7 of device d are live and belong to fragments d * 8 to d * 8 + 7, so every fragment has a live atom; every other slot names a fragment of its own device, of one of the four devices beside it along row or col (wrapping around), or of the device whose number is d plus half the number of devices (wrapping around). Device d's live atoms are its first live_count[d] slots; the count reaches 1024 on some device in every draw. `cell_index`: the atom slots of the device at (row r, col c) lie in its mesh block: first index from r * 8 to r * 8 + 7, second from c * 16 to c * 16 + 15; the third is anywhere.
All inputs are finite; a program needn't handle non-finite values.
Results may differ from the reference program's by a relative error of at most 0.000065.
Values sent between devices are 32-bit elements; how exact they have to be, the bound alone decides.
No kernel may reach another device: no remote copies, remote signals or barrier semaphores. Data moves between devices by JAX's collectives and lax.ppermute only.
A program may use at most 64 MiB of HBM per device.

```python
import math
import jax
import jax.numpy as jnp
from jax import lax

CX = 8
CY = 16
NZ = 256
ATOM_DEV = 1024
S_DEV = 8
NX = 256
NY = 256
ATOMS = 524288
STRUCTS = 4096
N_ROW = 32
N_COL = 16
DEVICES = 512


def draw_structure_id(key, part):
    key_side, key_pick = jax.random.split(jax.random.fold_in(key, 5))
    atom_slot = lax.iota(jnp.int32, ATOMS)
    device = atom_slot // ATOM_DEV
    within = atom_slot % ATOM_DEV
    row_place = device // N_COL
    col_place = device % N_COL
    side = jax.random.randint(key_side, (ATOMS,), 0, 6)
    row_step = jnp.where(side == 1, 1, jnp.where(side == 2, -1, 0))
    col_step = jnp.where(side == 3, 1, jnp.where(side == 4, -1, 0))
    owner = (row_place + row_step + N_ROW) % N_ROW * N_COL + (col_place + col_step + N_COL) % N_COL
    far_owner = (device + DEVICES // 2) % DEVICES
    owner = jnp.where(side == 5, far_owner, owner)
    nearby = owner * S_DEV + jax.random.randint(key_pick, (ATOMS,), 0, S_DEV)
    return jnp.where(within < S_DEV, device * S_DEV + within, nearby).astype(jnp.int32)


def draw_live_count(key, part):
    key_counts, key_fullest = jax.random.split(jax.random.fold_in(key, 7))
    least_live = max(S_DEV, ATOM_DEV // 2)
    counts = jax.random.randint(key_counts, (DEVICES,), least_live, ATOM_DEV + 1)
    fullest = jax.random.randint(key_fullest, (), 0, DEVICES)
    return jnp.where(lax.iota(jnp.int32, DEVICES) == fullest, ATOM_DEV, counts).astype(jnp.int32)


def draw_cell_index(key, part):
    key_x, key_y, key_z = jax.random.split(jax.random.fold_in(key, 11), 3)
    atom_slot = lax.iota(jnp.int32, ATOMS)
    device = atom_slot // ATOM_DEV
    row_place = device // N_COL
    col_place = device % N_COL
    cell_x = row_place * CX + jax.random.randint(key_x, (ATOMS,), 0, CX)
    cell_y = col_place * CY + jax.random.randint(key_y, (ATOMS,), 0, CY)
    cell_z = jax.random.randint(key_z, (ATOMS,), 0, NZ)
    return jnp.stack([cell_x, cell_y, cell_z]).astype(jnp.int32)


def block_levels(key, dims, shards, smallest, high):
    def one(dim, shards_of):
        draws = jax.random.uniform(jax.random.fold_in(jax.random.fold_in(key, 6), dim), (shards_of,), jnp.float32, smallest / len(shards), high / len(shards))
        return jnp.repeat(jnp.exp(draws), dims[dim] // shards_of).reshape((-1,) + (1,) * (len(dims) - dim - 1))

    level = one(*shards[0])
    for cut in shards[1:]:
        level = level * one(*cut)
    return level


def setup_inputs(seed: int = 0) -> dict:
    key_of = jax.random.split(jax.random.key(seed), 7)
    return {
        "charges": jnp.clip(-0.5 + 2.0 * jax.random.uniform(key_of[0], (ATOMS,), jnp.float32) ** block_levels(key_of[0], (ATOMS,), ((0, 512),), -0.2, 0.2), -0.5, 1.5),
        "structure_id": draw_structure_id(jax.random.fold_in(key_of[6], 71), 0),
        "live_count": draw_live_count(jax.random.fold_in(key_of[6], 71), 0),
        "cell_index": draw_cell_index(jax.random.fold_in(key_of[6], 71), 0),
        "fraction": jnp.clip(1.0 * jax.random.uniform(key_of[4], (3, ATOMS), jnp.float32) ** block_levels(key_of[4], (3, ATOMS), ((1, 512),), -0.2, 0.2), 0.0, 1.0),
        "influence": jnp.clip(jnp.exp(math.log(10.0) - 4.6051702 * jax.random.uniform(key_of[5], (NZ, NY, NX), jnp.float32) ** block_levels(key_of[5], (NZ, NY, NX), ((0, 16), (1, 32)), -0.2, 0.2)), 0.1, 10.0),
    }


def spline_weights(fraction):
    remain = 1.0 - fraction
    square = fraction * fraction
    cubic_term = square * fraction
    values = [remain * remain * remain / 6.0, (3.0 * cubic_term - 6.0 * square + 4.0) / 6.0,
              (-3.0 * cubic_term + 3.0 * square + 3.0 * fraction + 1.0) / 6.0, cubic_term / 6.0]
    slopes = [-0.5 * remain * remain, 0.5 * (3.0 * square - 4.0 * fraction),
              0.5 * (-3.0 * square + 2.0 * fraction + 1.0), 0.5 * square]
    return values, slopes


def reference(charges, structure_id, live_count, cell_index, fraction, influence):
    atom_slot = jnp.arange(ATOMS, dtype=jnp.int32)
    live = ((atom_slot % ATOM_DEV) < live_count[atom_slot // ATOM_DEV]).astype(jnp.float32)
    totals = jax.ops.segment_sum(charges * live, structure_id, num_segments=STRUCTS)
    counts = jax.ops.segment_sum(live, structure_id, num_segments=STRUCTS)
    neutral = (charges - (totals / counts)[structure_id]) * live
    wx_val, wx_slope = spline_weights(fraction[0])
    wy_val, wy_slope = spline_weights(fraction[1])
    wz_val, wz_slope = spline_weights(fraction[2])
    density = jnp.zeros((NX, NY, NZ), jnp.float32)
    for first in range(4):
        cell_x = (cell_index[0] + first) % NX
        for second in range(4):
            cell_y = (cell_index[1] + second) % NY
            partial_xy = neutral * wx_val[first] * wy_val[second]
            for third in range(4):
                cell_z = (cell_index[2] + third) % NZ
                density = density.at[cell_x, cell_y, cell_z].add(partial_xy * wz_val[third])
    spectrum = jnp.fft.fftn(density)
    kernel = jnp.transpose(influence, (2, 1, 0))
    potential = jnp.real(jnp.fft.ifftn(spectrum * kernel))
    value = jnp.zeros_like(charges)
    grad_x = jnp.zeros_like(charges)
    grad_y = jnp.zeros_like(charges)
    grad_z = jnp.zeros_like(charges)
    for first in range(4):
        cell_x = (cell_index[0] + first) % NX
        for second in range(4):
            cell_y = (cell_index[1] + second) % NY
            for third in range(4):
                cell_z = (cell_index[2] + third) % NZ
                sample = potential[cell_x, cell_y, cell_z]
                value = value + wx_val[first] * wy_val[second] * wz_val[third] * sample
                grad_x = grad_x + wx_slope[first] * wy_val[second] * wz_val[third] * sample
                grad_y = grad_y + wx_val[first] * wy_slope[second] * wz_val[third] * sample
                grad_z = grad_z + wx_val[first] * wy_val[second] * wz_slope[third] * sample
    atom_energy = 0.5 * neutral * value
    forces = -neutral[None, :] * jnp.stack([grad_x, grad_y, grad_z])
    return forces, atom_energy
```

```python
import functools

import jax
import jax.numpy as jnp
import numpy as np
from jax import lax
from jax.experimental import pallas as pl
from jax.experimental.pallas import tpu as pltpu
from jax.sharding import Mesh
from jax.sharding import PartitionSpec as P

N_ROW = 32
N_COL = 16
DEV = N_ROW * N_COL
CX = 8
CY = 16
N = 256
ATOMS = 1024
FRAG = 8
NK = 9
XI = CX + 3
PACK = 14
LANES = 128
ROW = ("row_0", "row_1")
COL = ("col_0", "col_1")
ALL = ROW + COL
MAIN = XI * CY
PLANE = MAIN + XI * 8
f32 = jnp.float32
bf16 = jnp.bfloat16


def kz_of(c, slot):
    if slot == 8 and c >= 8:
        return None
    return 16 * c + slot


def halves(table):
    high = table.astype(np.float32).astype(bf16)
    low = (table - high.astype(np.float64)).astype(np.float32).astype(bf16)
    return high, low


def z_lane(c, part):
    if c < PACK:
        return part * LANES + NK * c
    return 2 * LANES + NK * (2 * part + c - PACK)


@functools.cache
def z_table():
    table = np.zeros((N, 3 * LANES))
    z = np.arange(N)
    for c in range(N_COL):
        for slot in range(NK):
            kz = kz_of(c, slot)
            if kz is None:
                continue
            angle = 2.0 * np.pi * (kz * z % N) / N
            table[:, z_lane(c, 0) + slot] = np.cos(angle)
            table[:, z_lane(c, 1) + slot] = -np.sin(angle)
    return np.stack(halves(table))


@functools.cache
def y_table():
    table = np.zeros((2, N, N_COL, 40))
    ky = np.arange(N)
    for c in range(N_COL):
        for row in range(40):
            if row < 16:
                part, j = 0, row
            elif row < 24:
                part, j = (row - 16) // 4, 16 + row % 4
                if j == 19:
                    continue
            else:
                part, j = 1, row - 24
            angle = 2.0 * np.pi * (ky * (CY * c + j) % N) / N
            if part == 0:
                table[0, :, c, row] = np.cos(angle)
                table[1, :, c, row] = -np.sin(angle)
            else:
                table[0, :, c, row] = np.sin(angle)
                table[1, :, c, row] = np.cos(angle)
    return table.reshape(2 * N, N_COL * 40)


@functools.cache
def y_forward():
    return np.concatenate(halves(y_table()), axis=0)


@functools.cache
def y_back():
    return np.concatenate(halves(y_table().T.copy()), axis=0)


@functools.cache
def x_tables():
    twiddle = np.zeros((N_ROW, 2, LANES))
    k1 = np.arange(N_ROW)
    mix = np.zeros((2, LANES, 2, LANES))
    for i in range(XI):
        angle = 2.0 * np.pi * (i * k1 % N) / N
        for slot in range(NK):
            twiddle[:, 0, i * NK + slot] = np.cos(angle)
            twiddle[:, 1, i * NK + slot] = -np.sin(angle)
            for k2 in range(8):
                a = 2.0 * np.pi * (i * k2 % 8) / 8
                src, dst = i * NK + slot, slot * 8 + k2
                mix[0, src, 0, dst] = np.cos(a)
                mix[0, src, 1, dst] = -np.sin(a)
                mix[1, src, 0, dst] = np.sin(a)
                mix[1, src, 1, dst] = np.cos(a)
    return twiddle.astype(np.float32), np.stack(halves(mix.reshape(2 * LANES, 2 * LANES)))


def split(x):
    high = x.astype(bf16)
    low = (x - high.astype(f32)).astype(bf16)
    return high, low


def dot(a, b, dims=(((1,), (0,)), ((), ()))):
    return lax.dot_general(a, b, dims, preferred_element_type=f32)


NT = (((1,), (1,)), ((), ()))


def spline_values(fraction):
    remain = 1.0 - fraction
    square = fraction * fraction
    cubic = square * fraction
    return (
        remain * remain * remain * (1.0 / 6.0),
        (3.0 * cubic - 6.0 * square + 4.0) * (1.0 / 6.0),
        (-3.0 * cubic + 3.0 * square + 3.0 * fraction + 1.0) * (1.0 / 6.0),
        cubic * (1.0 / 6.0),
    )


def spline_slopes(fraction):
    remain = 1.0 - fraction
    square = fraction * fraction
    return (
        -0.5 * remain * remain,
        0.5 * (3.0 * square - 4.0 * fraction),
        0.5 * (-3.0 * square + 2.0 * fraction + 1.0),
        0.5 * square,
    )


def place(cell, weights, number):
    out = jnp.zeros(number.shape, f32)
    for offset in range(4):
        out = jnp.where(number == cell + offset, weights[offset], out)
    return out


def place_periodic(cell, weights):
    number = lax.broadcasted_iota(jnp.int32, (N, ATOMS), 0)
    out = jnp.zeros((N, ATOMS), f32)
    for offset in range(4):
        out = jnp.where(number == (cell + offset) % N, weights[offset], out)
    return out


def y_halo_rows(cell, weights):
    row = lax.broadcasted_iota(jnp.int32, (8, ATOMS), 0)
    return place(cell, weights, CY + row % 4)


def owners(device):
    row = device // N_COL
    col = device % N_COL
    return (
        device,
        (row + 1) % N_ROW * N_COL + col,
        (row + N_ROW - 1) % N_ROW * N_COL + col,
        row * N_COL + (col + 1) % N_COL,
        row * N_COL + (col + N_COL - 1) % N_COL,
        (device + DEV // 2) % DEV,
    )


def member_masks(device, live, sid):
    row = lax.broadcasted_iota(jnp.int32, (8, ATOMS), 0)
    lane = lax.broadcasted_iota(jnp.int32, (8, ATOMS), 1)
    alive = lane < live
    return [(sid == row + owner * FRAG) & alive for owner in owners(device)]


def partial_sums(device, live, sid, charges):
    out = []
    for mask in member_masks(device, live, sid):
        total = jnp.sum(jnp.where(mask, charges, 0.0), axis=1, keepdims=True)
        count = jnp.sum(jnp.where(mask, 1.0, 0.0), axis=1, keepdims=True)
        total = jnp.broadcast_to(total, (8, LANES))
        count = jnp.broadcast_to(count, (8, LANES))
        out.append(jnp.concatenate([total, count], axis=0))
    return out


def neutral_charges(device, live, sid, charges, means):
    acc = jnp.zeros((8, ATOMS), f32)
    for mask, mean in zip(member_masks(device, live, sid), means):
        acc = acc + jnp.where(mask, mean[:, 0:1], 0.0)
    mean = jnp.sum(acc, axis=0, keepdims=True)
    lane = lax.broadcasted_iota(jnp.int32, (1, ATOMS), 1)
    return jnp.where(lane < live, charges - mean, 0.0)


def lane_iota(rows):
    return lax.broadcasted_iota(jnp.int32, (rows, LANES), 1)


def group_tile(c, part):
    lane = z_lane(c, part)
    return lane // LANES, lane % LANES


def to_messages(wave, roll):
    lanes = lane_iota(16)
    sub = lax.broadcasted_iota(jnp.int32, (8, LANES), 0)
    out = []
    for c in range(N_COL):
        main = [jnp.zeros((16, LANES), f32), jnp.zeros((16, LANES), f32)]
        halo = [jnp.zeros((8, LANES), f32), jnp.zeros((8, LANES), f32)]
        for part in range(2):
            tile, lane = group_tile(c, part)
            cols = slice(tile * LANES, (tile + 1) * LANES)
            for x in range(XI):
                shift = (NK * x - lane) % LANES
                here = (lanes >= NK * x) & (lanes < NK * x + NK)
                piece = wave[x * CY : (x + 1) * CY, cols]
                edge = wave[MAIN + x * 8 : MAIN + (x + 1) * 8, cols]
                if shift:
                    piece = roll(piece, shift, 1)
                    edge = roll(edge, shift, 1)
                main[part] = jnp.where(here, piece, main[part])
                halo[part] = jnp.where(here[:8], edge, halo[part])
        both = jnp.where(sub < 4, halo[0], halo[1])
        out.append(jnp.concatenate([main[0], both, main[1]], axis=0))
    return out


def from_messages(message, roll):
    lanes = lane_iota(16)
    sub = lax.broadcasted_iota(jnp.int32, (8, LANES), 0)
    main = []
    halo = []
    for x in range(XI):
        wide = [jnp.zeros((16, LANES), f32) for _ in range(3)]
        edges = [jnp.zeros((8, LANES), f32) for _ in range(3)]
        for c in range(N_COL):
            block = message(c)
            for part in range(2):
                tile, lane = group_tile(c, part)
                shift = (lane - NK * x) % LANES
                here = (lanes >= lane) & (lanes < lane + NK)
                piece = block[0:16] if part == 0 else block[24:40]
                edge = block[16:24]
                if shift:
                    piece = roll(piece, shift, 1)
                    edge = roll(edge, shift, 1)
                wide[tile] = jnp.where(here, piece, wide[tile])
                own = sub < 4 if part == 0 else sub >= 4
                edges[tile] = jnp.where(here[:8] & own, edge, edges[tile])
        main.append(jnp.concatenate(wide, axis=1))
        halo.append(jnp.concatenate(edges, axis=1))
    return jnp.concatenate(main + halo, axis=0)


def spread_to_z(neutral, cell_x, cell_y, cell_z, fraction, table, roll):
    weights = spline_values(fraction)
    wx = [w[0:1] for w in weights]
    wy = [w[1:2] for w in weights]
    wz = [w[2:3] * neutral for w in weights]
    z_rows = place_periodic(cell_z, wz)
    x_rows = place(cell_x, wx, lax.broadcasted_iota(jnp.int32, (16, ATOMS), 0))
    y_rows = place(cell_y, wy, lax.broadcasted_iota(jnp.int32, (16, ATOMS), 0))
    y_edge = y_halo_rows(cell_y, wy)
    plane = jnp.concatenate(
        [y_rows * x_rows[x : x + 1] for x in range(XI)]
        + [y_edge * x_rows[x : x + 1] for x in range(XI)],
        axis=0,
    )
    plane_high, plane_low = split(plane)
    z_high, z_low = split(z_rows)
    grid = dot(plane_high, z_high, NT) + (dot(plane_low, z_high, NT) + dot(plane_high, z_low, NT))
    grid_high, grid_low = split(grid)
    wave = dot(grid_high, table[0]) + (dot(grid_low, table[0]) + dot(grid_high, table[1]))
    return to_messages(wave, roll)


def y_stage(x, table):
    high, low = split(x)
    half = table.shape[0] // 2
    both = dot(table, jnp.concatenate([high, low], axis=1))
    return both[:half, :LANES] + (both[:half, LANES:] + both[half:, :LANES])


def fft(values, sign):
    count = len(values)
    if count == 1:
        return values
    even = fft(values[0::2], sign)
    odd = fft(values[1::2], sign)
    out = [None] * count
    for k in range(count // 2):
        re, im = odd[k]
        if k == 0:
            pass
        elif 4 * k == count:
            re, im = (-sign * im, sign * re)
        else:
            angle = 2.0 * np.pi * k / count
            c, s = float(np.cos(angle)), float(sign * np.sin(angle))
            re, im = (re * c - im * s, re * s + im * c)
        er, ei = even[k]
        out[k] = (er + re, ei + im)
        out[k + count // 2] = (er - re, ei - im)
    return out


def x_forward(values, twiddle):
    out = []
    for k1, (re, im) in enumerate(fft(values, -1.0)):
        cos, sin = twiddle(k1)
        out.append(jnp.concatenate([re * cos - im * sin, re * sin + im * cos], axis=1))
    return jnp.concatenate(out, axis=0)


def x_mix(wave, gain, mix):
    high, low = split(wave)
    spectrum = dot(high, mix[0]) + (dot(low, mix[0]) + dot(high, mix[1]))
    spectrum = spectrum * gain
    high, low = split(spectrum)
    return dot(high, mix[0], NT) + (dot(low, mix[0], NT) + dot(high, mix[1], NT))


def x_back(wave, twiddle):
    values = []
    for k1 in range(N_ROW):
        re = wave[k1 * 8 : (k1 + 1) * 8, :LANES]
        im = wave[k1 * 8 : (k1 + 1) * 8, LANES:]
        cos, sin = twiddle(k1)
        values.append((re * cos + im * sin, im * cos - re * sin))
    return fft(values, 1.0)


def gain_table(device, own, mirror, edge, roll):
    col = device % N_COL
    r = lax.broadcasted_iota(jnp.int32, (72, 128), 0)
    k = lax.broadcasted_iota(jnp.int32, (72, 128), 1)
    take_own = (k == r).astype(bf16)
    r = lax.broadcasted_iota(jnp.int32, (72, 64), 0)
    k = lax.broadcasted_iota(jnp.int32, (72, 64), 1)
    slot, i = r // 8, r % 8
    take_mirror = ((slot > 0) & (i > 0) & (k == (8 - slot) * 8 + 8 - i)).astype(bf16)
    r = lax.broadcasted_iota(jnp.int32, (72, 8), 0)
    k = lax.broadcasted_iota(jnp.int32, (72, 8), 1)
    take_edge = ((r // 8 > 0) & (r % 8 == 0) & (k == 8 - r // 8)).astype(bf16)
    kx = lax.broadcasted_iota(jnp.int32, (N, N), 0)
    lane = lax.broadcasted_iota(jnp.int32, (N, N), 1)
    wave = lane // 8 + 32 * (lane % 8)
    order = (kx == wave).astype(bf16)
    reverse = (kx == (N - wave) % N).astype(bf16)

    def ordered(x, select, permutation):
        high, low = split(x)
        high = dot(select, high).astype(bf16)
        low = dot(select, low).astype(bf16)
        return dot(high, permutation) + dot(low, permutation)

    gain = ordered(own, take_own, order)
    gain = gain + ordered(mirror, take_mirror, reverse) + ordered(edge, take_edge, reverse)
    row = lax.broadcasted_iota(jnp.int32, (72, N), 0)
    gain = jnp.where((row >= 64) & (col >= 8), 0.0, gain) * (1.0 / (N * N * N))
    lanes = lane_iota(8)
    out = []
    for k1 in range(N_ROW):
        tile, lane = (k1 * 8) // LANES, (k1 * 8) % LANES
        acc = jnp.zeros((8, LANES), f32)
        for slot in range(NK):
            piece = gain[slot * 8 : (slot + 1) * 8, tile * LANES : (tile + 1) * LANES]
            shift = (slot * 8 - lane) % LANES
            if shift:
                piece = roll(piece, shift, 1)
            acc = jnp.where((lanes >= slot * 8) & (lanes < slot * 8 + 8), piece, acc)
        out.append(acc)
    return out


def interpolate(wave, neutral, cell_x, cell_y, cell_z, fraction, table):
    weights = spline_values(fraction)
    slopes = spline_slopes(fraction)
    number = lax.broadcasted_iota(jnp.int32, (16, ATOMS), 0)
    x_rows = place(cell_x, [w[0:1] for w in weights], number)
    x_slopes = place(cell_x, [w[0:1] for w in slopes], number)
    wy = [w[1:2] for w in weights]
    vy = [w[1:2] for w in slopes]
    y_rows, y_slopes = place(cell_y, wy, number), place(cell_y, vy, number)
    y_edge, y_edge_slopes = y_halo_rows(cell_y, wy), y_halo_rows(cell_y, vy)
    z_rows = place_periodic(cell_z, [w[2:3] for w in weights])
    z_slopes = place_periodic(cell_z, [w[2:3] for w in slopes])
    high, low = split(wave)
    grid = dot(high, table[0], NT) + (dot(low, table[0], NT) + dot(high, table[1], NT))
    grid_high, grid_low = split(grid)

    def sample(rows):
        high, low = split(rows)
        return dot(grid_high, high) + (dot(grid_low, high) + dot(grid_high, low))

    at = sample(z_rows)
    at_slope = sample(z_slopes)
    value = jnp.zeros((8, ATOMS), f32)
    grad_x, grad_y, grad_z = value, value, value

    def eight(x):
        return x[:8] + x[8:]

    for x in range(XI):
        main = at[x * CY : (x + 1) * CY]
        edge = at[MAIN + x * 8 : MAIN + (x + 1) * 8]
        main_slope = at_slope[x * CY : (x + 1) * CY]
        edge_slope = at_slope[MAIN + x * 8 : MAIN + (x + 1) * 8]
        plain = eight(main * y_rows) + edge * y_edge
        turned = eight(main * y_slopes) + edge * y_edge_slopes
        risen = eight(main_slope * y_rows) + edge_slope * y_edge
        value = value + plain * x_rows[x : x + 1]
        grad_x = grad_x + plain * x_slopes[x : x + 1]
        grad_y = grad_y + turned * x_rows[x : x + 1]
        grad_z = grad_z + risen * x_rows[x : x + 1]

    def total(x):
        return jnp.sum(x, axis=0, keepdims=True)

    energy = 0.5 * neutral * total(value)
    force = [-neutral * total(g) for g in (grad_x, grad_y, grad_z)]
    return energy, force


def partial_kernel(dev, live, sid, charges, *out):
    for ref, x in zip(out, partial_sums(dev[0], live[0], sid[...], charges[...])):
        ref[...] = x


def mean_kernel(own, a, b, c, d, e, mirror, mean, packed):
    total = own[...] + a[...] + b[...] + c[...] + d[...] + e[...]
    result = total[:8] / total[8:]
    mean[...] = result
    packed[0:8, :] = result
    for p in range(8):
        packed[8 + p : 9 + p, :] = mirror[p, 0:1, :LANES]
        packed[16 + p : 17 + p, :] = mirror[p, 0:1, LANES:]


def local_cells(dev, cells):
    return (
        cells[0:1] - dev // N_COL * CX,
        cells[1:2] - dev % N_COL * CY,
        cells[2:3],
    )


def spread_kernel(dev, live, sid, charges, cells, fraction, m0, m1, m2, m3, m4, m5, table, out, neutral_out):
    d = dev[0]
    means = [m0[...], m1[...], m2[0:8, :], m3[...], m4[...], m5[...]]
    neutral = neutral_charges(d, live[0], sid[...], charges[...], means)
    neutral_out[...] = neutral
    x, y, z = local_cells(d, cells[...])
    for c, message in enumerate(spread_to_z(neutral, x, y, z, fraction[...], table, pltpu.roll)):
        out[c] = message


def y_forward_kernel(x, table, out):
    y = y_stage(x[...].reshape(N_COL * 40, LANES), table[...])
    out[:, :, :LANES] = y[:N].reshape(N_ROW, 8, LANES)
    out[:, :, LANES:] = y[N:].reshape(N_ROW, 8, LANES)


def y_back_kernel(x, table, out):
    re = x[:, :, :LANES].reshape(N, LANES)
    im = x[:, :, LANES:].reshape(N, LANES)
    y = y_stage(jnp.concatenate([re, im], axis=0), table[...])
    out[...] = y.reshape(N_COL, 40, LANES)


def gain_kernel(dev, own, mirror, packed, out):
    edge = jnp.concatenate([packed[8:16, :], packed[16:24, :]], axis=1)
    flat = own[...].reshape(128, N)
    pieces = gain_table(dev[0], flat, mirror[...].reshape(64, N), edge, pltpu.roll)
    for k1, piece in enumerate(pieces):
        out[k1 * 8 : (k1 + 1) * 8, :LANES] = piece
        out[k1 * 8 : (k1 + 1) * 8, LANES:] = piece


def x_kernel(x, gain, twiddle, mix, out):
    def factor(k1):
        return twiddle[k1, 0:1, :], twiddle[k1, 1:2, :]

    values = [(x[r, :, :LANES], x[r, :, LANES:]) for r in range(N_ROW)]
    wave = x_mix(x_forward(values, factor), gain[...], mix)
    for r, (re, im) in enumerate(x_back(wave, factor)):
        out[r, :, :LANES] = re
        out[r, :, LANES:] = im


def atom_kernel(dev, message, neutral, cells, fraction, table, force, energy):
    wave = from_messages(lambda c: message[c], pltpu.roll)
    x, y, z = local_cells(dev[0], cells[...])
    e, g = interpolate(wave, neutral[...], x, y, z, fraction[...], table)
    energy[...] = e
    for d in range(3):
        force[d : d + 1, :] = g[d]


def call(kernel, shapes, scalars, *args):
    smem = pl.BlockSpec(memory_space=pltpu.SMEM)
    vmem = pl.BlockSpec(memory_space=pltpu.VMEM)
    many = len(shapes) > 1
    out_shape = [jax.ShapeDtypeStruct(s, f32) for s in shapes]
    return pl.pallas_call(
        kernel,
        out_shape=out_shape if many else out_shape[0],
        in_specs=[smem] * scalars + [vmem] * (len(args) - scalars),
        out_specs=[vmem] * len(shapes) if many else vmem,
        compiler_params=pltpu.CompilerParams(vmem_limit_bytes=48 << 20),
    )(*args)


def shifted(x, axis, distance):
    count = lax.axis_size(axis)
    return lax.ppermute(x, axis, [(i, (i + distance) % count) for i in range(count)])


def swap(x, axis):
    return lax.all_to_all(x, axis, split_axis=0, concat_axis=0, tiled=True)


def body(charges, structure_id, live_count, cells, fraction, influence):
    dev = lax.axis_index(ALL).astype(jnp.int32).reshape(1)
    charges = charges.reshape(1, ATOMS)
    sid = structure_id.reshape(1, ATOMS)
    mirror = lax.ppermute(influence[8:], ALL, [(i, DEV - 1 - i) for i in range(DEV)])
    parts = call(partial_kernel, [(16, LANES)] * 6, 2, dev, live_count, sid, charges)
    mean, packed = call(
        mean_kernel,
        [(8, LANES), (24, LANES)],
        0,
        parts[0],
        shifted(parts[1], ROW, 1),
        shifted(parts[2], ROW, -1),
        shifted(parts[3], COL, 1),
        shifted(parts[4], COL, -1),
        shifted(parts[5], ALL, DEV // 2),
        mirror,
    )
    packed = shifted(packed, ROW, 1)
    after_row = shifted(mean, ROW, -1)
    after_col = shifted(mean, COL, -1)
    before_col = shifted(mean, COL, 1)
    far = shifted(mean, ALL, DEV // 2)
    messages, neutral = call(
        spread_kernel,
        [(N_COL, 40, LANES), (1, ATOMS)],
        2,
        dev, live_count, sid, charges, cells, fraction,
        mean, after_row, packed, after_col, before_col, far,
        z_table(),
    )
    gain = call(gain_kernel, [(N, 2 * LANES)], 1, dev, influence, mirror, packed)
    twiddle, mix = x_tables()
    columns = swap(messages, COL)
    rows = call(y_forward_kernel, [(N_ROW, 8, 2 * LANES)], 0, columns, y_forward())
    rows = swap(rows, ROW)
    rows = call(x_kernel, [(N_ROW, 8, 2 * LANES)], 0, rows, gain, twiddle, mix)
    rows = swap(rows, ROW)
    columns = call(y_back_kernel, [(N_COL, 40, LANES)], 0, rows, y_back())
    columns = swap(columns, COL)
    forces, energy = call(
        atom_kernel,
        [(3, ATOMS), (1, ATOMS)],
        1,
        dev, columns, neutral, cells, fraction, z_table(),
    )
    return forces, energy.reshape(ATOMS)


def solution(mesh):
    torus = Mesh(mesh.devices.reshape(4, 8, 8, 2), ALL)
    placed = (P(ALL), P(ALL), P(ALL), P(None, ALL), P(None, ALL), P(COL, ROW, None))
    return jax.shard_map(
        body, mesh=torus, in_specs=placed, out_specs=(P(None, ALL), P(ALL)), check_vma=False
    )
```

```python
import functools

import jax
import jax.numpy as jnp
import numpy as np
from jax import lax
from jax.experimental import pallas as pl
from jax.experimental.pallas import tpu as pltpu
from jax.sharding import Mesh
from jax.sharding import PartitionSpec as P

N_ROW = 32
N_COL = 16
DEV = N_ROW * N_COL
CX = 8
CY = 16
N = 256
ATOMS = 1024
FRAG = 8
NK = 9
XI = CX + 3
PACK = 14
LANES = 128
ROW = ("row_0", "row_1")
COL = ("col_0", "col_1")
ALL = ROW + COL
MAIN = XI * CY
PLANE = MAIN + XI * 8
f32 = jnp.float32
bf16 = jnp.bfloat16


def kz_of(c, slot):
    if slot == 8 and c >= 8:
        return None
    return 16 * c + slot


def halves(table):
    high = table.astype(np.float32).astype(bf16)
    low = (table - high.astype(np.float64)).astype(np.float32).astype(bf16)
    return high, low


def z_lane(c, part):
    if c < PACK:
        return part * LANES + NK * c
    return 2 * LANES + NK * (2 * part + c - PACK)


@functools.cache
def z_table():
    table = np.zeros((N, 3 * LANES))
    z = np.arange(N)
    for c in range(N_COL):
        for slot in range(NK):
            kz = kz_of(c, slot)
            if kz is None:
                continue
            angle = 2.0 * np.pi * (kz * z % N) / N
            table[:, z_lane(c, 0) + slot] = np.cos(angle)
            table[:, z_lane(c, 1) + slot] = -np.sin(angle)
    return np.stack(halves(table))


@functools.cache
def y_table():
    table = np.zeros((2, N, N_COL, 40))
    ky = np.arange(N)
    for c in range(N_COL):
        for row in range(40):
            if row < 16:
                part, j = 0, row
            elif row < 24:
                part, j = (row - 16) // 4, 16 + row % 4
                if j == 19:
                    continue
            else:
                part, j = 1, row - 24
            angle = 2.0 * np.pi * (ky * (CY * c + j) % N) / N
            if part == 0:
                table[0, :, c, row] = np.cos(angle)
                table[1, :, c, row] = -np.sin(angle)
            else:
                table[0, :, c, row] = np.sin(angle)
                table[1, :, c, row] = np.cos(angle)
    return table.reshape(2 * N, N_COL * 40)


@functools.cache
def y_forward():
    return np.concatenate(halves(y_table()), axis=0)


@functools.cache
def x_tables():
    twiddle = np.zeros((N_ROW, 2, LANES))
    k1 = np.arange(N_ROW)
    mix = np.zeros((2, LANES, 2, LANES))
    for i in range(XI):
        angle = 2.0 * np.pi * (i * k1 % N) / N
        for slot in range(NK):
            twiddle[:, 0, i * NK + slot] = np.cos(angle)
            twiddle[:, 1, i * NK + slot] = -np.sin(angle)
            for k2 in range(8):
                a = 2.0 * np.pi * (i * k2 % 8) / 8
                src, dst = i * NK + slot, slot * 8 + k2
                mix[0, src, 0, dst] = np.cos(a)
                mix[0, src, 1, dst] = -np.sin(a)
                mix[1, src, 0, dst] = np.sin(a)
                mix[1, src, 1, dst] = np.cos(a)
    return twiddle.astype(np.float32), np.stack(halves(mix.reshape(2 * LANES, 2 * LANES)))


def split(x):
    high = x.astype(bf16)
    low = (x - high.astype(f32)).astype(bf16)
    return high, low


def dot(a, b, dims=(((1,), (0,)), ((), ()))):
    return lax.dot_general(a, b, dims, preferred_element_type=f32)


NT = (((1,), (1,)), ((), ()))


def spline_values(fraction):
    remain = 1.0 - fraction
    square = fraction * fraction
    cubic = square * fraction
    return (
        remain * remain * remain * (1.0 / 6.0),
        (3.0 * cubic - 6.0 * square + 4.0) * (1.0 / 6.0),
        (-3.0 * cubic + 3.0 * square + 3.0 * fraction + 1.0) * (1.0 / 6.0),
        cubic * (1.0 / 6.0),
    )


def spline_slopes(fraction):
    remain = 1.0 - fraction
    square = fraction * fraction
    return (
        -0.5 * remain * remain,
        0.5 * (3.0 * square - 4.0 * fraction),
        0.5 * (-3.0 * square + 2.0 * fraction + 1.0),
        0.5 * square,
    )


def place(cell, weights, number):
    out = jnp.zeros(number.shape, f32)
    for offset in range(4):
        out = jnp.where(number == cell + offset, weights[offset], out)
    return out


def place_periodic(cell, weights):
    number = lax.broadcasted_iota(jnp.int32, (N, ATOMS), 0)
    out = jnp.zeros((N, ATOMS), f32)
    for offset in range(4):
        out = jnp.where(number == (cell + offset) % N, weights[offset], out)
    return out


def y_halo_rows(cell, weights):
    row = lax.broadcasted_iota(jnp.int32, (8, ATOMS), 0)
    return place(cell, weights, CY + row % 4)


def owners(device):
    row = device // N_COL
    col = device % N_COL
    return (
        device,
        (row + 1) % N_ROW * N_COL + col,
        (row + N_ROW - 1) % N_ROW * N_COL + col,
        row * N_COL + (col + 1) % N_COL,
        row * N_COL + (col + N_COL - 1) % N_COL,
        (device + DEV // 2) % DEV,
    )


def member_masks(device, live, sid):
    row = lax.broadcasted_iota(jnp.int32, (8, ATOMS), 0)
    lane = lax.broadcasted_iota(jnp.int32, (8, ATOMS), 1)
    alive = lane < live
    return [(sid == row + owner * FRAG) & alive for owner in owners(device)]


def partial_sums(device, live, sid, charges):
    row = lax.broadcasted_iota(jnp.int32, (8, LANES), 0)
    lane = lax.broadcasted_iota(jnp.int32, (8, LANES), 1)
    acc = jnp.zeros((8, LANES), f32)
    for slot, mask in enumerate(member_masks(device, live, sid)):
        total = jnp.sum(jnp.where(mask, charges, 0.0), axis=1, keepdims=True)
        count = jnp.sum(jnp.where(mask, 1.0, 0.0), axis=1, keepdims=True)
        acc = jnp.where(lane == 16 * slot + row, total, acc)
        acc = jnp.where(lane == 16 * slot + 8 + row, count, acc)
    return jnp.sum(acc, axis=0, keepdims=True)


def fragment_means(device, sums, roll):
    row = lax.broadcasted_iota(jnp.int32, (8, LANES), 0)
    lane = lax.broadcasted_iota(jnp.int32, (8, LANES), 1)
    means = []
    for owner in owners(device):
        around = owners(owner)
        total = jnp.zeros((1, LANES), f32)
        for slot, source in enumerate((0, 2, 1, 4, 3, 5)):
            part = sums(around[source])
            total = total + (roll(part, LANES - 16 * slot, 1) if slot else part)
        mean = total / roll(total, LANES - 8, 1)
        mean = jnp.where(lane == row, jnp.broadcast_to(mean, (8, LANES)), 0.0)
        means.append(jnp.sum(mean, axis=1, keepdims=True))
    return means


def neutral_charges(device, live, sid, charges, means):
    acc = jnp.zeros((8, ATOMS), f32)
    for mask, mean in zip(member_masks(device, live, sid), means):
        acc = acc + jnp.where(mask, mean, 0.0)
    mean = jnp.sum(acc, axis=0, keepdims=True)
    lane = lax.broadcasted_iota(jnp.int32, (1, ATOMS), 1)
    return jnp.where(lane < live, charges - mean, 0.0)


def lane_iota(rows):
    return lax.broadcasted_iota(jnp.int32, (rows, LANES), 1)


def group_tile(c, part):
    lane = z_lane(c, part)
    return lane // LANES, lane % LANES


def to_messages(wave, roll):
    lanes = lane_iota(16)
    sub = lax.broadcasted_iota(jnp.int32, (8, LANES), 0)
    out = []
    for c in range(N_COL):
        main = [jnp.zeros((16, LANES), f32), jnp.zeros((16, LANES), f32)]
        halo = [jnp.zeros((8, LANES), f32), jnp.zeros((8, LANES), f32)]
        for part in range(2):
            tile, lane = group_tile(c, part)
            cols = slice(tile * LANES, (tile + 1) * LANES)
            for x in range(XI):
                shift = (NK * x - lane) % LANES
                here = (lanes >= NK * x) & (lanes < NK * x + NK)
                piece = wave[x * CY : (x + 1) * CY, cols]
                edge = wave[MAIN + x * 8 : MAIN + (x + 1) * 8, cols]
                if shift:
                    piece = roll(piece, shift, 1)
                    edge = roll(edge, shift, 1)
                main[part] = jnp.where(here, piece, main[part])
                halo[part] = jnp.where(here[:8], edge, halo[part])
        both = jnp.where(sub < 4, halo[0], halo[1])
        out.append(jnp.concatenate([main[0], both, main[1]], axis=0))
    return out


def from_messages(message, roll):
    lanes = lane_iota(16)
    sub = lax.broadcasted_iota(jnp.int32, (8, LANES), 0)
    main = []
    halo = []
    for x in range(XI):
        wide = [jnp.zeros((16, LANES), f32) for _ in range(3)]
        edges = [jnp.zeros((8, LANES), f32) for _ in range(3)]
        for c in range(N_COL):
            block = message(c)
            for part in range(2):
                tile, lane = group_tile(c, part)
                shift = (lane - NK * x) % LANES
                here = (lanes >= lane) & (lanes < lane + NK)
                piece = block[0:16] if part == 0 else block[24:40]
                edge = block[16:24]
                if shift:
                    piece = roll(piece, shift, 1)
                    edge = roll(edge, shift, 1)
                wide[tile] = jnp.where(here, piece, wide[tile])
                own = sub < 4 if part == 0 else sub >= 4
                edges[tile] = jnp.where(here[:8] & own, edge, edges[tile])
        main.append(jnp.concatenate(wide, axis=1))
        halo.append(jnp.concatenate(edges, axis=1))
    return jnp.concatenate(main + halo, axis=0)


def spread_to_z(neutral, cell_x, cell_y, fraction, z_high, z_low, table, roll):
    weights = spline_values(fraction)
    wx = [w[0:1] * neutral for w in weights]
    wy = [w[1:2] for w in weights]
    x_rows = place(cell_x, wx, lax.broadcasted_iota(jnp.int32, (16, ATOMS), 0))
    y_rows = place(cell_y, wy, lax.broadcasted_iota(jnp.int32, (16, ATOMS), 0))
    y_edge = y_halo_rows(cell_y, wy)
    plane = jnp.concatenate(
        [y_rows * x_rows[x : x + 1] for x in range(XI)]
        + [y_edge * x_rows[x : x + 1] for x in range(XI)],
        axis=0,
    )
    plane_high, plane_low = split(plane)
    grid = dot(plane_high, z_high, NT) + (dot(plane_low, z_high, NT) + dot(plane_high, z_low, NT))
    grid_high, grid_low = split(grid)
    wave = dot(grid_high, table[0]) + (dot(grid_low, table[0]) + dot(grid_high, table[1]))
    return to_messages(wave, roll)


def z_parts(cell_z, fraction):
    z = fraction[2:3]
    return split(place_periodic(cell_z, spline_values(z))) + split(
        place_periodic(cell_z, spline_slopes(z))
    )


def y_stage(x, table):
    high, low = split(x)
    half = table.shape[0] // 2
    both = dot(table, jnp.concatenate([high, low], axis=1))
    return both[:half, :LANES] + (both[:half, LANES:] + both[half:, :LANES])


def y_adjoint(re, im, table):
    x = jnp.concatenate([re.T, im.T], axis=1)
    high, low = split(x)
    both = dot(jnp.concatenate([high, low], axis=0), table[: 2 * N])
    y = both[:LANES] + (both[LANES:] + dot(high, table[2 * N :]))
    return y.T


def fft(values, sign):
    count = len(values)
    if count == 1:
        return values
    even = fft(values[0::2], sign)
    odd = fft(values[1::2], sign)
    out = [None] * count
    for k in range(count // 2):
        re, im = odd[k]
        if k == 0:
            pass
        elif 4 * k == count:
            re, im = (-sign * im, sign * re)
        else:
            angle = 2.0 * np.pi * k / count
            c, s = float(np.cos(angle)), float(sign * np.sin(angle))
            re, im = (re * c - im * s, re * s + im * c)
        er, ei = even[k]
        out[k] = (er + re, ei + im)
        out[k + count // 2] = (er - re, ei - im)
    return out


def x_forward(values, twiddle):
    out = []
    for k1, (re, im) in enumerate(fft(values, -1.0)):
        cos, sin = twiddle(k1)
        out.append(jnp.concatenate([re * cos - im * sin, re * sin + im * cos], axis=1))
    return jnp.concatenate(out, axis=0)


def x_mix(wave, gain, mix):
    high, low = split(wave)
    spectrum = dot(high, mix[0]) + (dot(low, mix[0]) + dot(high, mix[1]))
    spectrum = spectrum * gain
    high, low = split(spectrum)
    return dot(high, mix[0], NT) + (dot(low, mix[0], NT) + dot(high, mix[1], NT))


def x_back(wave, twiddle):
    values = []
    for k1 in range(N_ROW):
        re = wave[k1 * 8 : (k1 + 1) * 8, :LANES]
        im = wave[k1 * 8 : (k1 + 1) * 8, LANES:]
        cos, sin = twiddle(k1)
        values.append((re * cos + im * sin, im * cos - re * sin))
    return fft(values, 1.0)


def gain_table(device, own, mirror, edge, roll):
    col = device % N_COL
    r = lax.broadcasted_iota(jnp.int32, (72, 128), 0)
    k = lax.broadcasted_iota(jnp.int32, (72, 128), 1)
    take_own = (k == r).astype(bf16)
    r = lax.broadcasted_iota(jnp.int32, (72, 64), 0)
    k = lax.broadcasted_iota(jnp.int32, (72, 64), 1)
    slot, i = r // 8, r % 8
    take_mirror = ((slot > 0) & (i > 0) & (k == (8 - slot) * 8 + 8 - i)).astype(bf16)
    r = lax.broadcasted_iota(jnp.int32, (72, 8), 0)
    k = lax.broadcasted_iota(jnp.int32, (72, 8), 1)
    take_edge = ((r // 8 > 0) & (r % 8 == 0) & (k == 8 - r // 8)).astype(bf16)
    kx = lax.broadcasted_iota(jnp.int32, (N, N), 0)
    lane = lax.broadcasted_iota(jnp.int32, (N, N), 1)
    wave = lane // 8 + 32 * (lane % 8)
    order = (kx == wave).astype(bf16)
    reverse = (kx == (N - wave) % N).astype(bf16)

    def ordered(x, select, permutation):
        high, low = split(x)
        high = dot(select, high).astype(bf16)
        low = dot(select, low).astype(bf16)
        return dot(high, permutation) + dot(low, permutation)

    gain = ordered(own, take_own, order)
    gain = gain + ordered(mirror, take_mirror, reverse) + ordered(edge, take_edge, reverse)
    row = lax.broadcasted_iota(jnp.int32, (72, N), 0)
    gain = jnp.where((row >= 64) & (col >= 8), 0.0, gain) * (1.0 / (N * N * N))
    lanes = lane_iota(8)
    out = []
    for k1 in range(N_ROW):
        tile, lane = (k1 * 8) // LANES, (k1 * 8) % LANES
        acc = jnp.zeros((8, LANES), f32)
        for slot in range(NK):
            piece = gain[slot * 8 : (slot + 1) * 8, tile * LANES : (tile + 1) * LANES]
            shift = (slot * 8 - lane) % LANES
            if shift:
                piece = roll(piece, shift, 1)
            acc = jnp.where((lanes >= slot * 8) & (lanes < slot * 8 + 8), piece, acc)
        out.append(acc)
    return out


def interpolate(wave, neutral, cell_x, cell_y, fraction, z_rows, z_slopes, table):
    weights = spline_values(fraction)
    slopes = spline_slopes(fraction)
    number = lax.broadcasted_iota(jnp.int32, (16, ATOMS), 0)
    x_rows = place(cell_x, [w[0:1] for w in weights], number)
    x_slopes = place(cell_x, [w[0:1] for w in slopes], number)
    wy = [w[1:2] for w in weights]
    vy = [w[1:2] for w in slopes]
    y_rows, y_slopes = place(cell_y, wy, number), place(cell_y, vy, number)
    y_edge, y_edge_slopes = y_halo_rows(cell_y, wy), y_halo_rows(cell_y, vy)
    high, low = split(wave)
    grid = dot(high, table[0], NT) + (dot(low, table[0], NT) + dot(high, table[1], NT))
    grid_high, grid_low = split(grid)

    def sample(high, low):
        return dot(grid_high, high) + (dot(grid_low, high) + dot(grid_high, low))

    at = sample(*z_rows)
    at_slope = sample(*z_slopes)
    value = jnp.zeros((8, ATOMS), f32)
    grad_x, grad_y, grad_z = value, value, value

    def eight(x):
        return x[:8] + x[8:]

    for x in range(XI):
        main = at[x * CY : (x + 1) * CY]
        edge = at[MAIN + x * 8 : MAIN + (x + 1) * 8]
        main_slope = at_slope[x * CY : (x + 1) * CY]
        edge_slope = at_slope[MAIN + x * 8 : MAIN + (x + 1) * 8]
        plain = eight(main * y_rows) + edge * y_edge
        turned = eight(main * y_slopes) + edge * y_edge_slopes
        risen = eight(main_slope * y_rows) + edge_slope * y_edge
        value = value + plain * x_rows[x : x + 1]
        grad_x = grad_x + plain * x_slopes[x : x + 1]
        grad_y = grad_y + turned * x_rows[x : x + 1]
        grad_z = grad_z + risen * x_rows[x : x + 1]

    def total(x):
        return jnp.sum(x, axis=0, keepdims=True)

    energy = 0.5 * neutral * total(value)
    force = [-neutral * total(g) for g in (grad_x, grad_y, grad_z)]
    return energy, force


def partial_kernel(dev, live, sid_hbm, charges_hbm, out, sid, charges, sems):
    copies = [
        pltpu.make_async_copy(sid_hbm, sid, sems.at[0]),
        pltpu.make_async_copy(charges_hbm, charges, sems.at[1]),
    ]
    for copy in copies:
        copy.start()
    for copy in copies:
        copy.wait()
    row = partial_sums(dev[0], live[0], sid[...], charges[...])
    out[...] = jnp.broadcast_to(row, (DEV, LANES))


def prefetch_kernel(cells_hbm, fraction_hbm, influence, z_tab, y_tab, mix_tab, turn_tab, *refs):
    cells, fraction, mirror, edge, z, y, mix, turn = refs[:8]
    parts, sems = refs[8:12], refs[12]
    pairs = [
        (cells_hbm, cells),
        (fraction_hbm, fraction),
        (influence.at[8:16], mirror),
        (influence.at[8:16, 0], edge),
        (z_tab, z),
        (y_tab, y),
        (mix_tab, mix),
        (turn_tab, turn),
    ]
    copies = [pltpu.make_async_copy(a, b, sems.at[i]) for i, (a, b) in enumerate(pairs)]
    for copy in copies:
        copy.start()
    copies[0].wait()
    copies[1].wait()
    for ref, x in zip(parts, z_parts(cells[2:3], fraction[...])):
        ref[...] = x
    for copy in copies[2:]:
        copy.wait()


def local_cells(dev, cells):
    return (
        cells[0:1] - dev // N_COL * CX,
        cells[1:2] - dev % N_COL * CY,
        cells[2:3],
    )


def spread_kernel(dev, live, sums, sid, charges, cells, fraction, z_high, z_low, table, out, neutral_out):
    d = dev[0]
    means = fragment_means(d, lambda s: sums[pl.ds(s, 1), :], pltpu.roll)
    neutral = neutral_charges(d, live[0], sid[...], charges[...], means)
    neutral_out[...] = neutral
    x, y, _ = local_cells(d, cells[...])
    messages = spread_to_z(
        neutral, x, y, fraction[...], z_high[...], z_low[...], table, pltpu.roll
    )
    for c, message in enumerate(messages):
        out[c] = message


def y_forward_kernel(x, table, out):
    y = y_stage(x[...].reshape(N_COL * 40, LANES), table[...])
    out[:, :, :LANES] = y[:N].reshape(N_ROW, 8, LANES)
    out[:, :, LANES:] = y[N:].reshape(N_ROW, 8, LANES)


def y_back_kernel(x, table, out):
    re = x[:, :, :LANES].reshape(N, LANES)
    im = x[:, :, LANES:].reshape(N, LANES)
    out[...] = y_adjoint(re, im, table).reshape(N_COL, 40, LANES)


def gain_kernel(dev, influence, mirror, edge, out, own, sem):
    copy = pltpu.make_async_copy(influence, own, sem)
    copy.start()
    copy.wait()
    flat = own[...].reshape(128, N)
    pieces = gain_table(dev[0], flat, mirror[...].reshape(64, N), edge[...], pltpu.roll)
    for k1, piece in enumerate(pieces):
        out[k1 * 8 : (k1 + 1) * 8, :LANES] = piece
        out[k1 * 8 : (k1 + 1) * 8, LANES:] = piece


def x_kernel(x, gain, twiddle, mix, out):
    def factor(k1):
        return twiddle[k1, 0:1, :], twiddle[k1, 1:2, :]

    values = [(x[r, :, :LANES], x[r, :, LANES:]) for r in range(N_ROW)]
    wave = x_mix(x_forward(values, factor), gain[...], mix)
    for r, (re, im) in enumerate(x_back(wave, factor)):
        out[r, :, :LANES] = re
        out[r, :, LANES:] = im


def atom_kernel(dev, message, neutral, cells, fraction, zh, zl, vh, vl, table, force, energy):
    wave = from_messages(lambda c: message[c], pltpu.roll)
    x, y, _ = local_cells(dev[0], cells[...])
    e, g = interpolate(
        wave, neutral[...], x, y, fraction[...], (zh[...], zl[...]), (vh[...], vl[...]), table
    )
    energy[...] = e
    for d in range(3):
        force[d : d + 1, :] = g[d]


def call(kernel, outs, spaces, args, scratch=()):
    kinds = {
        "s": pl.BlockSpec(memory_space=pltpu.SMEM),
        "v": pl.BlockSpec(memory_space=pltpu.VMEM),
        "h": pl.BlockSpec(memory_space=pl.ANY),
    }
    shapes = [jax.ShapeDtypeStruct(o[0], o[1]) if isinstance(o[0], tuple) else jax.ShapeDtypeStruct(o, f32) for o in outs]
    many = len(shapes) > 1
    return pl.pallas_call(
        kernel,
        out_shape=shapes if many else shapes[0],
        in_specs=[kinds[k] for k in spaces],
        out_specs=[kinds["v"]] * len(shapes) if many else kinds["v"],
        scratch_shapes=list(scratch),
        compiler_params=pltpu.CompilerParams(vmem_limit_bytes=48 << 20),
    )(*args)


def swap(x, axis):
    return lax.all_to_all(x, axis, split_axis=0, concat_axis=0, tiled=True)


def body(charges, structure_id, live_count, cells, fraction, influence):
    dev = lax.axis_index(ALL).astype(jnp.int32).reshape(1)
    charges = charges.reshape(1, ATOMS)
    sid = structure_id.reshape(1, ATOMS)
    sums = call(
        partial_kernel,
        [(DEV, LANES)],
        "sshh",
        (dev, live_count, sid, charges),
        [
            pltpu.VMEM((1, ATOMS), jnp.int32),
            pltpu.VMEM((1, ATOMS), f32),
            pltpu.SemaphoreType.DMA((2,)),
        ],
    )
    sums = swap(sums.reshape(DEV, 1, LANES), ALL).reshape(DEV, LANES)
    twiddle, mix = x_tables()
    half = ((N, ATOMS), bf16)
    cells, fraction, mirror, edge, z_tab, y_tab, mix, twiddle, zh, zl, vh, vl = call(
        prefetch_kernel,
        [
            ((3, ATOMS), jnp.int32),
            (3, ATOMS),
            (8, 8, N),
            (8, N),
            ((2, N, 3 * LANES), bf16),
            ((4 * N, 40 * N_COL), bf16),
            ((2, 2 * LANES, 2 * LANES), bf16),
            (N_ROW, 2, LANES),
            half,
            half,
            half,
            half,
        ],
        "hhhhhhh",
        (cells, fraction, influence, z_table(), y_forward(), mix, twiddle),
        [pltpu.SemaphoreType.DMA((8,))],
    )
    mirror = lax.ppermute(mirror, ALL, [(i, DEV - 1 - i) for i in range(DEV)])
    edge = lax.ppermute(
        edge,
        ALL,
        [(i, (N_ROW - i // N_COL) % N_ROW * N_COL + N_COL - 1 - i % N_COL) for i in range(DEV)],
    )
    gain = call(
        gain_kernel,
        [(N, 2 * LANES)],
        "shvv",
        (dev, influence, mirror, edge),
        [pltpu.VMEM((16, 8, N), f32), pltpu.SemaphoreType.DMA(())],
    )
    messages, neutral = call(
        spread_kernel,
        [(N_COL, 40, LANES), (1, ATOMS)],
        "ssvvvvvvvv",
        (dev, live_count, sums, sid, charges, cells, fraction, zh, zl, z_tab),
    )
    columns = swap(messages, COL)
    rows = call(y_forward_kernel, [(N_ROW, 8, 2 * LANES)], "vv", (columns, y_tab))
    rows = swap(rows, ROW)
    rows = call(x_kernel, [(N_ROW, 8, 2 * LANES)], "vvvv", (rows, gain, twiddle, mix))
    rows = swap(rows, ROW)
    columns = call(y_back_kernel, [(N_COL, 40, LANES)], "vv", (rows, y_tab))
    columns = swap(columns, COL)
    forces, energy = call(
        atom_kernel,
        [(3, ATOMS), (1, ATOMS)],
        "svvvvvvvvv",
        (dev, columns, neutral, cells, fraction, zh, zl, vh, vl, z_tab),
    )
    return forces, energy.reshape(ATOMS)


def solution(mesh):
    torus = Mesh(mesh.devices.reshape(4, 8, 8, 2), ALL)
    placed = (P(ALL), P(ALL), P(ALL), P(None, ALL), P(None, ALL), P(COL, ROW, None))
    return jax.shard_map(
        body, mesh=torus, in_specs=placed, out_specs=(P(None, ALL), P(ALL)), check_vma=False
    )
```

```python
import functools

import jax
import jax.numpy as jnp
import numpy as np
from jax import lax
from jax.experimental import pallas as pl
from jax.experimental.pallas import tpu as pltpu
from jax.sharding import Mesh
from jax.sharding import PartitionSpec as P

N_ROW = 32
N_COL = 16
DEV = N_ROW * N_COL
CX = 8
CY = 16
N = 256
ATOMS = 1024
FRAG = 8
NK = 9
XI = CX + 3
PACK = 14
LANES = 128
ROW = ("row_0", "row_1")
COL = ("col_0", "col_1")
ALL = ROW + COL
MAIN = XI * CY
PLANE = MAIN + 3 * CY
GROUPS = XI + 3
ROWS = 2 * CY
f32 = jnp.float32
bf16 = jnp.bfloat16


def kz_of(c, slot):
    if slot == 8 and c >= 8:
        return None
    return 16 * c + slot


def halves(table):
    high = table.astype(np.float32).astype(bf16)
    low = (table - high.astype(np.float64)).astype(np.float32).astype(bf16)
    return high, low


def z_lane(c, part):
    if c < PACK:
        return part * LANES + NK * c
    return 2 * LANES + NK * (2 * part + c - PACK)


@functools.cache
def z_table():
    table = np.zeros((N, 3 * LANES))
    z = np.arange(N)
    for c in range(N_COL):
        for slot in range(NK):
            kz = kz_of(c, slot)
            if kz is None:
                continue
            angle = 2.0 * np.pi * (kz * z % N) / N
            table[:, z_lane(c, 0) + slot] = np.cos(angle)
            table[:, z_lane(c, 1) + slot] = -np.sin(angle)
    return np.stack(halves(table))


@functools.cache
def y_table():
    k = np.arange(N)
    angle = (2.0 * np.pi / N) * (k[:, None] * k[None, :] % N)
    cos = np.cos(angle).reshape(N, N_COL, CY)
    sin = np.sin(angle).reshape(N, N_COL, CY)
    table = np.zeros((2, N, N_COL, 2, CY))
    table[0, :, :, 0] = cos
    table[0, :, :, 1] = sin
    table[1, :, :, 0] = -sin
    table[1, :, :, 1] = cos
    return np.concatenate(halves(table.reshape(2 * N, 2 * N)), axis=0)


@functools.cache
def x_tables():
    twiddle = np.zeros((N_ROW, 2, LANES))
    k1 = np.arange(N_ROW)
    mix = np.zeros((2, LANES, 2, LANES))
    for i in range(XI):
        angle = 2.0 * np.pi * (i * k1 % N) / N
        for slot in range(NK):
            twiddle[:, 0, i * NK + slot] = np.cos(angle)
            twiddle[:, 1, i * NK + slot] = -np.sin(angle)
            for k2 in range(8):
                a = 2.0 * np.pi * (i * k2 % 8) / 8
                src, dst = i * NK + slot, slot * 8 + k2
                mix[0, src, 0, dst] = np.cos(a)
                mix[0, src, 1, dst] = -np.sin(a)
                mix[1, src, 0, dst] = np.sin(a)
                mix[1, src, 1, dst] = np.cos(a)
    return twiddle.astype(np.float32), np.stack(halves(mix.reshape(2 * LANES, 2 * LANES)))


def split(x):
    high = x.astype(bf16)
    low = (x - high.astype(f32)).astype(bf16)
    return high, low


def dot(a, b, dims=(((1,), (0,)), ((), ()))):
    return lax.dot_general(a, b, dims, preferred_element_type=f32)


NT = (((1,), (1,)), ((), ()))


def spline_values(fraction):
    remain = 1.0 - fraction
    square = fraction * fraction
    cubic = square * fraction
    return (
        remain * remain * remain * (1.0 / 6.0),
        (3.0 * cubic - 6.0 * square + 4.0) * (1.0 / 6.0),
        (-3.0 * cubic + 3.0 * square + 3.0 * fraction + 1.0) * (1.0 / 6.0),
        cubic * (1.0 / 6.0),
    )


def spline_slopes(fraction):
    remain = 1.0 - fraction
    square = fraction * fraction
    return (
        -0.5 * remain * remain,
        0.5 * (3.0 * square - 4.0 * fraction),
        0.5 * (-3.0 * square + 2.0 * fraction + 1.0),
        0.5 * square,
    )


def place(cell, weights, number):
    out = jnp.zeros(number.shape, f32)
    for offset in range(4):
        out = jnp.where(number == cell + offset, weights[offset], out)
    return out


def place_periodic(cell, weights):
    number = lax.broadcasted_iota(jnp.int32, (N, ATOMS), 0)
    out = jnp.zeros((N, ATOMS), f32)
    for offset in range(4):
        out = jnp.where(number == (cell + offset) % N, weights[offset], out)
    return out


def y_halo_rows(cell, weights):
    return place(cell, weights, CY + lax.broadcasted_iota(jnp.int32, (8, ATOMS), 0))


def owners(device):
    row = device // N_COL
    col = device % N_COL
    return (
        device,
        (row + 1) % N_ROW * N_COL + col,
        (row + N_ROW - 1) % N_ROW * N_COL + col,
        row * N_COL + (col + 1) % N_COL,
        row * N_COL + (col + N_COL - 1) % N_COL,
        (device + DEV // 2) % DEV,
    )


def member_masks(device, live, sid):
    row = lax.broadcasted_iota(jnp.int32, (8, ATOMS), 0)
    lane = lax.broadcasted_iota(jnp.int32, (8, ATOMS), 1)
    alive = lane < live
    return [(sid == row + owner * FRAG) & alive for owner in owners(device)]


def partial_sums(device, live, sid, charges):
    row = lax.broadcasted_iota(jnp.int32, (8, LANES), 0)
    lane = lax.broadcasted_iota(jnp.int32, (8, LANES), 1)
    acc = jnp.zeros((8, LANES), f32)
    for slot, mask in enumerate(member_masks(device, live, sid)):
        total = jnp.sum(jnp.where(mask, charges, 0.0), axis=1, keepdims=True)
        count = jnp.sum(jnp.where(mask, 1.0, 0.0), axis=1, keepdims=True)
        acc = jnp.where(lane == 16 * slot + row, total, acc)
        acc = jnp.where(lane == 16 * slot + 8 + row, count, acc)
    return jnp.sum(acc, axis=0, keepdims=True)


def fragment_means(device, sums, roll):
    row = lax.broadcasted_iota(jnp.int32, (8, LANES), 0)
    lane = lax.broadcasted_iota(jnp.int32, (8, LANES), 1)
    means = []
    for owner in owners(device):
        around = owners(owner)
        total = jnp.zeros((1, LANES), f32)
        for slot, source in enumerate((0, 2, 1, 4, 3, 5)):
            part = sums(around[source])
            total = total + (roll(part, LANES - 16 * slot, 1) if slot else part)
        mean = total / roll(total, LANES - 8, 1)
        mean = jnp.where(lane == row, jnp.broadcast_to(mean, (8, LANES)), 0.0)
        means.append(jnp.sum(mean, axis=1, keepdims=True))
    return means


def neutral_charges(device, live, sid, charges, means):
    acc = jnp.zeros((8, ATOMS), f32)
    for mask, mean in zip(member_masks(device, live, sid), means):
        acc = acc + jnp.where(mask, mean, 0.0)
    mean = jnp.sum(acc, axis=0, keepdims=True)
    lane = lax.broadcasted_iota(jnp.int32, (1, ATOMS), 1)
    return jnp.where(lane < live, charges - mean, 0.0)


def lane_iota(rows):
    return lax.broadcasted_iota(jnp.int32, (rows, LANES), 1)


def group_tile(c, part):
    lane = z_lane(c, part)
    return lane // LANES, lane % LANES


def to_messages(wave, roll):
    lanes = lane_iota(CY)
    out = []
    for c in range(N_COL):
        parts = []
        for part in range(2):
            tile, lane = group_tile(c, part)
            acc = jnp.zeros((CY, LANES), f32)
            for g in range(GROUPS):
                piece = wave[g * CY : (g + 1) * CY, tile * LANES : (tile + 1) * LANES]
                shift = (NK * g - lane) % LANES
                if shift:
                    piece = roll(piece, shift, 1)
                acc = jnp.where((lanes >= NK * g) & (lanes < NK * g + NK), piece, acc)
            parts.append(acc)
        out.append(jnp.concatenate(parts, axis=0))
    return out


def from_messages(message, roll):
    lanes = lane_iota(CY)
    out = []
    for g in range(GROUPS):
        wide = [jnp.zeros((CY, LANES), f32) for _ in range(3)]
        for c in range(N_COL):
            block = message(c)
            for part in range(2):
                tile, lane = group_tile(c, part)
                piece = block[part * CY : (part + 1) * CY]
                shift = (lane - NK * g) % LANES
                if shift:
                    piece = roll(piece, shift, 1)
                wide[tile] = jnp.where((lanes >= lane) & (lanes < lane + NK), piece, wide[tile])
        out.append(jnp.concatenate(wide, axis=1))
    return jnp.concatenate(out, axis=0)


def add_halo(blocks, roll, slant):
    lane = lane_iota(8)
    row = lax.broadcasted_iota(jnp.int32, (8, LANES), 0)
    out = [None] * N_COL
    for c in range(N_COL):
        after = (c + 1) % N_COL
        pair = []
        for part in range(2):
            low = slant(blocks[c][part][:8], 0)
            high = slant(roll(blocks[c][part][8:], 8 * NK, 1), 0)
            lines = jnp.zeros((8, LANES), f32)
            for h in range(3):
                first = NK * (XI + 2 - h) + NK * row
                take_low = (lane - first + 2 * LANES) % LANES < NK
                take_high = ((lane - first - 8 * NK + 3 * LANES) % LANES < NK) & (row < XI - 8)
                line = jnp.where(take_low, low, 0.0) + jnp.where(take_high, high, 0.0)
                lines = jnp.where(row == h, jnp.sum(line, axis=0, keepdims=True), lines)
            lines = slant(lines, LANES - NK * (XI + 2))
            main = blocks[after][part]
            pair.append(jnp.concatenate([main[:8] + lines, main[8:]], axis=0))
        out[after] = pair
    return out


def copy_halo(blocks, roll, slant):
    lane = lane_iota(8)
    out = []
    for c in range(N_COL):
        after = (c + 1) % N_COL
        pair = []
        for part in range(2):
            low, high = blocks[c][part][:8], blocks[c][part][8:]
            for h in range(3):
                line = jnp.broadcast_to(blocks[after][part][h : h + 1], (8, LANES))
                group = NK * (XI + 2 - h)
                here = (lane >= group) & (lane < group + NK)
                base = group - 15 * NK
                low = jnp.where(here, slant(roll(line, base % LANES, 1), 0), low)
                high = jnp.where(here, slant(line, base + 8 * NK), high)
            pair.append(jnp.concatenate([low, high], axis=0))
        out.append(pair)
    return out


def spread_to_z(neutral, cell_x, cell_y, fraction, z_high, z_low, table, roll):
    weights = spline_values(fraction)
    wx = [w[0:1] * neutral for w in weights]
    wy = [w[1:2] for w in weights]
    x_rows = place(cell_x, wx, lax.broadcasted_iota(jnp.int32, (16, ATOMS), 0))
    y_rows = place(cell_y, wy, lax.broadcasted_iota(jnp.int32, (16, ATOMS), 0))
    y_edge = y_halo_rows(cell_y, wy)
    plane = jnp.concatenate(
        [y_rows * x_rows[x : x + 1] for x in range(XI)]
        + [x_rows * y_edge[h : h + 1] for h in (2, 1, 0)],
        axis=0,
    )
    plane_high, plane_low = split(plane)
    grid = dot(plane_high, z_high, NT) + (dot(plane_low, z_high, NT) + dot(plane_high, z_low, NT))
    grid_high, grid_low = split(grid)
    wave = dot(grid_high, table[0]) + (dot(grid_low, table[0]) + dot(grid_high, table[1]))
    return to_messages(wave, roll)


def z_parts(cell_z, fraction):
    z = fraction[2:3]
    return split(place_periodic(cell_z, spline_values(z))) + split(
        place_periodic(cell_z, spline_slopes(z))
    )


def y_stage(x, table):
    high, low = split(x)
    half = table.shape[0] // 2
    both = dot(table, jnp.concatenate([high, low], axis=1))
    return both[:half, :LANES] + (both[:half, LANES:] + both[half:, :LANES])


def fft(values, sign):
    count = len(values)
    if count == 1:
        return values
    even = fft(values[0::2], sign)
    odd = fft(values[1::2], sign)
    out = [None] * count
    for k in range(count // 2):
        re, im = odd[k]
        if k == 0:
            pass
        elif 4 * k == count:
            re, im = (-sign * im, sign * re)
        else:
            angle = 2.0 * np.pi * k / count
            c, s = float(np.cos(angle)), float(sign * np.sin(angle))
            re, im = (re * c - im * s, re * s + im * c)
        er, ei = even[k]
        out[k] = (er + re, ei + im)
        out[k + count // 2] = (er - re, ei - im)
    return out


def x_forward(values, twiddle):
    out = []
    for k1, (re, im) in enumerate(fft(values, -1.0)):
        cos, sin = twiddle(k1)
        out.append(jnp.concatenate([re * cos - im * sin, re * sin + im * cos], axis=1))
    return jnp.concatenate(out, axis=0)


def x_mix(wave, gain, mix):
    high, low = split(wave)
    spectrum = dot(high, mix[0]) + (dot(low, mix[0]) + dot(high, mix[1]))
    spectrum = spectrum * gain
    high, low = split(spectrum)
    return dot(high, mix[0], NT) + (dot(low, mix[0], NT) + dot(high, mix[1], NT))


def x_back(wave, twiddle):
    values = []
    for k1 in range(N_ROW):
        re = wave[k1 * 8 : (k1 + 1) * 8, :LANES]
        im = wave[k1 * 8 : (k1 + 1) * 8, LANES:]
        cos, sin = twiddle(k1)
        values.append((re * cos + im * sin, im * cos - re * sin))
    return fft(values, 1.0)


def gain_table(device, own, mirror, edge, roll):
    col = device % N_COL
    r = lax.broadcasted_iota(jnp.int32, (72, 128), 0)
    k = lax.broadcasted_iota(jnp.int32, (72, 128), 1)
    take_own = (k == r).astype(bf16)
    r = lax.broadcasted_iota(jnp.int32, (72, 64), 0)
    k = lax.broadcasted_iota(jnp.int32, (72, 64), 1)
    slot, i = r // 8, r % 8
    take_mirror = ((slot > 0) & (i > 0) & (k == (8 - slot) * 8 + 8 - i)).astype(bf16)
    r = lax.broadcasted_iota(jnp.int32, (72, 8), 0)
    k = lax.broadcasted_iota(jnp.int32, (72, 8), 1)
    take_edge = ((r // 8 > 0) & (r % 8 == 0) & (k == 8 - r // 8)).astype(bf16)
    kx = lax.broadcasted_iota(jnp.int32, (N, N), 0)
    lane = lax.broadcasted_iota(jnp.int32, (N, N), 1)
    wave = lane // 8 + 32 * (lane % 8)
    order = (kx == wave).astype(bf16)
    reverse = (kx == (N - wave) % N).astype(bf16)

    def ordered(x, select, permutation):
        high, low = split(x)
        high = dot(select, high).astype(bf16)
        low = dot(select, low).astype(bf16)
        return dot(high, permutation) + dot(low, permutation)

    gain = ordered(own, take_own, order)
    gain = gain + ordered(mirror, take_mirror, reverse) + ordered(edge, take_edge, reverse)
    row = lax.broadcasted_iota(jnp.int32, (72, N), 0)
    gain = jnp.where((row >= 64) & (col >= 8), 0.0, gain) * (1.0 / (N * N * N))
    lanes = lane_iota(8)
    out = []
    for k1 in range(N_ROW):
        tile, lane = (k1 * 8) // LANES, (k1 * 8) % LANES
        acc = jnp.zeros((8, LANES), f32)
        for slot in range(NK):
            piece = gain[slot * 8 : (slot + 1) * 8, tile * LANES : (tile + 1) * LANES]
            shift = (slot * 8 - lane) % LANES
            if shift:
                piece = roll(piece, shift, 1)
            acc = jnp.where((lanes >= slot * 8) & (lanes < slot * 8 + 8), piece, acc)
        out.append(acc)
    return out


def interpolate(wave, neutral, cell_x, cell_y, fraction, z_rows, z_slopes, table):
    weights = spline_values(fraction)
    slopes = spline_slopes(fraction)
    number = lax.broadcasted_iota(jnp.int32, (16, ATOMS), 0)
    x_rows = place(cell_x, [w[0:1] for w in weights], number)
    x_slopes = place(cell_x, [w[0:1] for w in slopes], number)
    wy = [w[1:2] for w in weights]
    vy = [w[1:2] for w in slopes]
    y_rows, y_slopes = place(cell_y, wy, number), place(cell_y, vy, number)
    x_back = place(cell_x, [w[0:1] for w in weights], 15 - number)
    x_back_slopes = place(cell_x, [w[0:1] for w in slopes], 15 - number)
    y_edge, y_edge_slopes = y_halo_rows(cell_y, wy), y_halo_rows(cell_y, vy)
    high, low = split(wave)
    grid = dot(high, table[0], NT) + (dot(low, table[0], NT) + dot(high, table[1], NT))
    grid_high, grid_low = split(grid)

    def sample(high, low):
        return dot(grid_high, high) + (dot(grid_low, high) + dot(grid_high, low))

    at = sample(*z_rows)
    at_slope = sample(*z_slopes)
    value = jnp.zeros((8, ATOMS), f32)
    grad_x, grad_y, grad_z = value, value, value

    def eight(x):
        return x[:8] + x[8:]

    for x in range(XI):
        main = at[x * CY : (x + 1) * CY]
        plain = eight(main * y_rows)
        turned = eight(main * y_slopes)
        risen = eight(at_slope[x * CY : (x + 1) * CY] * y_rows)
        value = value + plain * x_rows[x : x + 1]
        grad_x = grad_x + plain * x_slopes[x : x + 1]
        grad_y = grad_y + turned * x_rows[x : x + 1]
        grad_z = grad_z + risen * x_rows[x : x + 1]
    for h in range(3):
        rows = slice(MAIN + (2 - h) * CY, MAIN + (3 - h) * CY)
        plain = eight(at[rows] * x_back)
        weight = y_edge[h : h + 1]
        value = value + plain * weight
        grad_x = grad_x + eight(at[rows] * x_back_slopes) * weight
        grad_y = grad_y + plain * y_edge_slopes[h : h + 1]
        grad_z = grad_z + eight(at_slope[rows] * x_back) * weight

    def total(x):
        return jnp.sum(x, axis=0, keepdims=True)

    energy = 0.5 * neutral * total(value)
    force = [-neutral * total(g) for g in (grad_x, grad_y, grad_z)]
    return energy, force


def run_copies(pairs, sems):
    copies = [pltpu.make_async_copy(a, b, sems.at[i]) for i, (a, b) in enumerate(pairs)]
    for copy in copies:
        copy.start()
    return copies


def partial_kernel(dev, live, sid_hbm, charges_hbm, influence, out, sid, charges, mirror, edge, sems):
    copies = run_copies(
        [
            (sid_hbm, sid),
            (charges_hbm, charges),
            (influence.at[8:16], mirror),
            (influence.at[8:16, 0], edge),
        ],
        sems,
    )
    copies[0].wait()
    copies[1].wait()
    row = partial_sums(dev[0], live[0], sid[...], charges[...])
    out[...] = jnp.broadcast_to(row, (N_COL, 8, LANES))
    copies[2].wait()
    copies[3].wait()


def relay_kernel(dev, sums, out):
    col = dev[0] % N_COL
    row = lax.broadcasted_iota(jnp.int32, (8, LANES), 0)
    acc = jnp.zeros((8, LANES), f32)
    for k in range(5):
        acc = jnp.where(row == k, sums[(col + N_COL + k - 2) % N_COL, 0:1, :], acc)
    out[...] = jnp.broadcast_to(acc, (N_ROW, 8, LANES))


def prefetch_kernel(cells_hbm, fraction_hbm, influence, z_tab, y_tab, mix_tab, turn_tab, *refs):
    cells, fraction, own, z, y, mix, turn = refs[:7]
    parts, sems = refs[7:11], refs[11]
    copies = run_copies(
        [
            (cells_hbm, cells),
            (fraction_hbm, fraction),
            (influence, own),
            (z_tab, z),
            (y_tab, y),
            (mix_tab, mix),
            (turn_tab, turn),
        ],
        sems,
    )
    copies[0].wait()
    copies[1].wait()
    for ref, x in zip(parts, z_parts(cells[2:3], fraction[...])):
        ref[...] = x
    for copy in copies[2:]:
        copy.wait()


def local_cells(dev, cells):
    return (
        cells[0:1] - dev // N_COL * CX,
        cells[1:2] - dev % N_COL * CY,
        cells[2:3],
    )


def spread_kernel(dev, live, sums, sid, charges, cells, fraction, z_high, z_low, table, out, neutral_out):
    d = dev[0]
    col = d % N_COL

    def row_of(s):
        return sums[s // N_COL, pl.ds((s % N_COL - col + N_COL + 2) % N_COL, 1), :]

    means = fragment_means(d, row_of, pltpu.roll)
    neutral = neutral_charges(d, live[0], sid[...], charges[...], means)
    neutral_out[...] = neutral
    x, y, _ = local_cells(d, cells[...])
    messages = spread_to_z(
        neutral, x, y, fraction[...], z_high[...], z_low[...], table, pltpu.roll
    )
    for c, message in enumerate(messages):
        out[c] = message


def slant(x, shift):
    return pltpu.roll(x, shift, 1, stride=NK, stride_axis=0)


def pairs_of(x):
    return [[x[c, :CY], x[c, CY:]] for c in range(N_COL)]


def y_forward_kernel(x, table, out):
    blocks = add_halo(pairs_of(x), pltpu.roll, slant)
    y = y_stage(jnp.concatenate([b for pair in blocks for b in pair], axis=0), table[...])
    out[:, :, :LANES] = y[:N].reshape(N_ROW, 8, LANES)
    out[:, :, LANES:] = y[N:].reshape(N_ROW, 8, LANES)


def y_back_kernel(x, table, out):
    pieces = []
    for r in range(0, N_ROW, 2):
        pieces += [x[r, :, :LANES], x[r + 1, :, :LANES], -x[r, :, LANES:], -x[r + 1, :, LANES:]]
    y = y_stage(jnp.concatenate(pieces, axis=0), table[...])
    blocks = [
        [y[c * CY : (c + 1) * CY], -y[N + c * CY : N + (c + 1) * CY]] for c in range(N_COL)
    ]
    for c, (re, im) in enumerate(copy_halo(blocks, pltpu.roll, slant)):
        out[c, :CY] = re
        out[c, CY:] = im


def gain_kernel(dev, own, mirror, edge, out):
    flat = own[...].reshape(128, N)
    pieces = gain_table(dev[0], flat, mirror[...].reshape(64, N), edge[...], pltpu.roll)
    for k1, piece in enumerate(pieces):
        out[k1 * 8 : (k1 + 1) * 8, :LANES] = piece
        out[k1 * 8 : (k1 + 1) * 8, LANES:] = piece


def x_kernel(x, gain, twiddle, mix, out):
    def factor(k1):
        return twiddle[k1, 0:1, :], twiddle[k1, 1:2, :]

    values = [(x[r, :, :LANES], x[r, :, LANES:]) for r in range(N_ROW)]
    wave = x_mix(x_forward(values, factor), gain[...], mix)
    for r, (re, im) in enumerate(x_back(wave, factor)):
        out[r, :, :LANES] = re
        out[r, :, LANES:] = im


def atom_kernel(dev, message, neutral, cells, fraction, zh, zl, vh, vl, table, force, energy):
    wave = from_messages(lambda c: message[c], pltpu.roll)
    x, y, _ = local_cells(dev[0], cells[...])
    e, g = interpolate(
        wave, neutral[...], x, y, fraction[...], (zh[...], zl[...]), (vh[...], vl[...]), table
    )
    energy[...] = e
    for d in range(3):
        force[d : d + 1, :] = g[d]


def call(kernel, outs, spaces, args, scratch=()):
    kinds = {
        "s": pl.BlockSpec(memory_space=pltpu.SMEM),
        "v": pl.BlockSpec(memory_space=pltpu.VMEM),
        "h": pl.BlockSpec(memory_space=pltpu.HBM),
    }
    shapes = [jax.ShapeDtypeStruct(o[0], o[1]) if isinstance(o[0], tuple) else jax.ShapeDtypeStruct(o, f32) for o in outs]
    many = len(shapes) > 1
    args = [
        pltpu.with_memory_space_constraint(x, pltpu.HBM) if k == "h" else x
        for k, x in zip(spaces, args)
    ]
    return pl.pallas_call(
        kernel,
        out_shape=shapes if many else shapes[0],
        in_specs=[kinds[k] for k in spaces],
        out_specs=[kinds["v"]] * len(shapes) if many else kinds["v"],
        scratch_shapes=list(scratch),
        compiler_params=pltpu.CompilerParams(vmem_limit_bytes=16 << 20),
    )(*args)


def swap(x, axis):
    return lax.all_to_all(x, axis, split_axis=0, concat_axis=0, tiled=True)


def body(charges, structure_id, live_count, cells, fraction, influence):
    dev = lax.axis_index(ALL).astype(jnp.int32).reshape(1)
    charges = charges.reshape(1, ATOMS)
    sid = structure_id.reshape(1, ATOMS)
    sums, sid, charges, mirror, edge = call(
        partial_kernel,
        [(N_COL, 8, LANES), ((1, ATOMS), jnp.int32), (1, ATOMS), (8, 8, N), (8, N)],
        "sshhh",
        (dev, live_count, sid, charges, influence),
        [pltpu.SemaphoreType.DMA((4,))],
    )
    mirror = lax.ppermute(mirror, ALL, [(i, DEV - 1 - i) for i in range(DEV)])
    edge = lax.ppermute(
        edge,
        ALL,
        [(i, (N_ROW - i // N_COL) % N_ROW * N_COL + N_COL - 1 - i % N_COL) for i in range(DEV)],
    )
    sums = swap(sums, COL)
    sums, mirror, edge = lax.optimization_barrier((sums, mirror, edge))
    sums = call(relay_kernel, [(N_ROW, 8, LANES)], "sv", (dev, sums))
    sums = swap(sums, ROW)
    twiddle, mix = x_tables()
    half = ((N, ATOMS), bf16)
    cells, fraction, own, z_tab, y_tab, mix, twiddle, zh, zl, vh, vl = call(
        prefetch_kernel,
        [
            ((3, ATOMS), jnp.int32),
            (3, ATOMS),
            (16, 8, N),
            ((2, N, 3 * LANES), bf16),
            ((4 * N, 2 * N), bf16),
            ((2, 2 * LANES, 2 * LANES), bf16),
            (N_ROW, 2, LANES),
            half,
            half,
            half,
            half,
        ],
        "hhhhhhh",
        (cells, fraction, influence, z_table(), y_table(), mix, twiddle),
        [pltpu.SemaphoreType.DMA((7,))],
    )
    gain = call(gain_kernel, [(N, 2 * LANES)], "svvv", (dev, own, mirror, edge))
    zh, gain = lax.optimization_barrier((zh, gain))
    messages, neutral = call(
        spread_kernel,
        [(N_COL, ROWS, LANES), (1, ATOMS)],
        "ssvvvvvvvv",
        (dev, live_count, sums, sid, charges, cells, fraction, zh, zl, z_tab),
    )
    columns = swap(messages, COL)
    rows = call(y_forward_kernel, [(N_ROW, 8, 2 * LANES)], "vv", (columns, y_tab))
    rows = swap(rows, ROW)
    rows = call(x_kernel, [(N_ROW, 8, 2 * LANES)], "vvvv", (rows, gain, twiddle, mix))
    rows = swap(rows, ROW)
    columns = call(y_back_kernel, [(N_COL, ROWS, LANES)], "vv", (rows, y_tab))
    columns = swap(columns, COL)
    forces, energy = call(
        atom_kernel,
        [(3, ATOMS), (1, ATOMS)],
        "svvvvvvvvv",
        (dev, columns, neutral, cells, fraction, zh, zl, vh, vl, z_tab),
    )
    return forces, energy.reshape(ATOMS)


def solution(mesh):
    torus = Mesh(mesh.devices.reshape(4, 8, 8, 2), ALL)
    placed = (P(ALL), P(ALL), P(ALL), P(None, ALL), P(None, ALL), P(COL, ROW, None))
    return jax.shard_map(
        body, mesh=torus, in_specs=placed, out_specs=(P(None, ALL), P(ALL)), check_vma=False
    )
```

```python
import functools

import jax
import jax.numpy as jnp
import numpy as np
from jax import lax
from jax.experimental import pallas as pl
from jax.experimental.pallas import tpu as pltpu
from jax.sharding import Mesh
from jax.sharding import PartitionSpec as P

N_ROW = 32
N_COL = 16
DEV = N_ROW * N_COL
CX = 8
CY = 16
N = 256
ATOMS = 1024
FRAG = 8
NK = 9
XI = CX + 3
PACK = 14
LANES = 128
ROW = ("row_0", "row_1")
COL = ("col_0", "col_1")
ALL = ROW + COL
MAIN = XI * CY
PLANE = MAIN + 3 * CY
GROUPS = XI + 3
ROWS = 2 * CY
f32 = jnp.float32
bf16 = jnp.bfloat16


def kz_of(c, slot):
    if slot == 8 and c >= 8:
        return None
    return 16 * c + slot


def halves(table):
    high = table.astype(np.float32).astype(bf16)
    low = (table - high.astype(np.float64)).astype(np.float32).astype(bf16)
    return high, low


def z_lane(c, part):
    if c < PACK:
        return part * LANES + NK * c
    return 2 * LANES + NK * (2 * part + c - PACK)


@functools.cache
def z_table():
    table = np.zeros((N, 3 * LANES))
    z = np.arange(N)
    for c in range(N_COL):
        for slot in range(NK):
            kz = kz_of(c, slot)
            if kz is None:
                continue
            angle = 2.0 * np.pi * (kz * z % N) / N
            table[:, z_lane(c, 0) + slot] = np.cos(angle)
            table[:, z_lane(c, 1) + slot] = -np.sin(angle)
    return np.stack(halves(table))


@functools.cache
def y_table():
    k = np.arange(N)
    angle = (2.0 * np.pi / N) * (k[:, None] * k[None, :] % N)
    cos = np.cos(angle).reshape(N, N_COL, CY)
    sin = np.sin(angle).reshape(N, N_COL, CY)
    table = np.zeros((2, N, N_COL, 2, CY))
    table[0, :, :, 0] = cos
    table[0, :, :, 1] = sin
    table[1, :, :, 0] = -sin
    table[1, :, :, 1] = cos
    return np.concatenate(halves(table.reshape(2 * N, 2 * N)), axis=0)


@functools.cache
def x_tables():
    twiddle = np.zeros((N_ROW, 2, LANES))
    k1 = np.arange(N_ROW)
    mix = np.zeros((2, LANES, 2, LANES))
    for i in range(XI):
        angle = 2.0 * np.pi * (i * k1 % N) / N
        for slot in range(NK):
            twiddle[:, 0, i * NK + slot] = np.cos(angle)
            twiddle[:, 1, i * NK + slot] = -np.sin(angle)
            for k2 in range(8):
                a = 2.0 * np.pi * (i * k2 % 8) / 8
                src, dst = i * NK + slot, slot * 8 + k2
                mix[0, src, 0, dst] = np.cos(a)
                mix[0, src, 1, dst] = -np.sin(a)
                mix[1, src, 0, dst] = np.sin(a)
                mix[1, src, 1, dst] = np.cos(a)
    return twiddle.astype(np.float32), np.stack(halves(mix.reshape(2 * LANES, 2 * LANES)))


def split(x):
    high = x.astype(bf16)
    low = (x - high.astype(f32)).astype(bf16)
    return high, low


def dot(a, b, dims=(((1,), (0,)), ((), ()))):
    return lax.dot_general(a, b, dims, preferred_element_type=f32)


NT = (((1,), (1,)), ((), ()))


def spline_values(fraction):
    remain = 1.0 - fraction
    square = fraction * fraction
    cubic = square * fraction
    return (
        remain * remain * remain * (1.0 / 6.0),
        (3.0 * cubic - 6.0 * square + 4.0) * (1.0 / 6.0),
        (-3.0 * cubic + 3.0 * square + 3.0 * fraction + 1.0) * (1.0 / 6.0),
        cubic * (1.0 / 6.0),
    )


def spline_slopes(fraction):
    remain = 1.0 - fraction
    square = fraction * fraction
    return (
        -0.5 * remain * remain,
        0.5 * (3.0 * square - 4.0 * fraction),
        0.5 * (-3.0 * square + 2.0 * fraction + 1.0),
        0.5 * square,
    )


def place(cell, weights, number):
    out = jnp.zeros(number.shape, f32)
    for offset in range(4):
        out = jnp.where(number == cell + offset, weights[offset], out)
    return out


def place_periodic(cell, weights):
    number = lax.broadcasted_iota(jnp.int32, (N, ATOMS), 0)
    out = jnp.zeros((N, ATOMS), f32)
    for offset in range(4):
        out = jnp.where(number == (cell + offset) % N, weights[offset], out)
    return out


def y_halo_rows(cell, weights):
    return place(cell, weights, CY + lax.broadcasted_iota(jnp.int32, (8, ATOMS), 0))


STEPS = ((0, 0), (1, 0), (-1, 0), (0, 1), (0, -1), (N_ROW // 2, 0))


def owners(device):
    row = device // N_COL
    col = device % N_COL
    return [
        (row + N_ROW + dr) % N_ROW * N_COL + (col + N_COL + dc) % N_COL for dr, dc in STEPS
    ]


def member_masks(device, live, sid):
    row = lax.broadcasted_iota(jnp.int32, (8, ATOMS), 0)
    lane = lax.broadcasted_iota(jnp.int32, (8, ATOMS), 1)
    alive = lane < live
    return [(sid == row + owner * FRAG) & alive for owner in owners(device)]


def partial_sums(device, live, sid, charges):
    row = lax.broadcasted_iota(jnp.int32, (8, LANES), 0)
    lane = lax.broadcasted_iota(jnp.int32, (8, LANES), 1)
    acc = jnp.zeros((8, LANES), f32)
    for slot, mask in enumerate(member_masks(device, live, sid)):
        total = jnp.sum(jnp.where(mask, charges, 0.0), axis=1, keepdims=True)
        count = jnp.sum(jnp.where(mask, 1.0, 0.0), axis=1, keepdims=True)
        acc = jnp.where(lane == 16 * slot + row, total, acc)
        acc = jnp.where(lane == 16 * slot + 8 + row, count, acc)
    return jnp.sum(acc, axis=0, keepdims=True)


def fragment_means(row_of, roll):
    row = lax.broadcasted_iota(jnp.int32, (8, LANES), 0)
    lane = lax.broadcasted_iota(jnp.int32, (8, LANES), 1)
    means = []
    for owner_row, owner_col in STEPS:
        total = jnp.zeros((1, LANES), f32)
        for slot, (dr, dc) in enumerate(STEPS):
            step = owner_col - dc
            if abs(step) == 2:
                k, start = 1 + step // 2, 96
            else:
                k, start = 1 + step, 16 * slot
            part = row_of(owner_row - dr, k)
            total = total + (roll(part, LANES - start, 1) if start else part)
        mean = total / roll(total, LANES - 8, 1)
        mean = jnp.where(lane == row, jnp.broadcast_to(mean, (8, LANES)), 0.0)
        means.append(jnp.sum(mean, axis=1, keepdims=True))
    return means


def relay_rows(col, sums, roll):
    row = lax.broadcasted_iota(jnp.int32, (8, LANES), 0)
    lane = lax.broadcasted_iota(jnp.int32, (8, LANES), 1)
    near = [sums((col + N_COL + k) % N_COL) for k in (-2, -1, 0, 1, 2)]
    first = jnp.where(lane < 96, near[1], roll(near[0], 48, 1))
    last = jnp.where(lane < 96, near[3], roll(near[4], 32, 1))
    out = jnp.where(row % 4 == 0, first, last)
    return jnp.where(row % 4 == 1, near[2], out)


def neutral_charges(device, live, sid, charges, means):
    acc = jnp.zeros((8, ATOMS), f32)
    for mask, mean in zip(member_masks(device, live, sid), means):
        acc = acc + jnp.where(mask, mean, 0.0)
    mean = jnp.sum(acc, axis=0, keepdims=True)
    lane = lax.broadcasted_iota(jnp.int32, (1, ATOMS), 1)
    return jnp.where(lane < live, charges - mean, 0.0)


def lane_iota(rows):
    return lax.broadcasted_iota(jnp.int32, (rows, LANES), 1)


def group_tile(c, part):
    lane = z_lane(c, part)
    return lane // LANES, lane % LANES


def to_messages(wave, roll):
    lanes = lane_iota(CY)
    here = [(lanes >= NK * g) & (lanes < NK * g + NK) for g in range(GROUPS)]
    out = []
    for c in range(N_COL):
        parts = []
        for part in range(2):
            tile, lane = group_tile(c, part)
            acc = jnp.zeros((CY, LANES), f32)
            for g in range(GROUPS):
                piece = wave[g * CY : (g + 1) * CY, tile * LANES : (tile + 1) * LANES]
                shift = (NK * g - lane) % LANES
                if shift:
                    piece = roll(piece, shift, 1)
                acc = jnp.where(here[g], piece, acc)
            parts.append(acc)
        out.append(jnp.concatenate(parts, axis=0))
    return out


def from_messages(message, roll):
    lanes = lane_iota(CY)
    here = [(lanes >= NK * g) & (lanes < NK * g + NK) for g in range(GROUPS)]
    out = []
    for g in range(GROUPS):
        wide = [jnp.zeros((CY, LANES), f32) for _ in range(3)]
        for c in range(N_COL):
            block = message(c)
            for part in range(2):
                tile, lane = group_tile(c, part)
                piece = block[part * CY : (part + 1) * CY]
                shift = (lane - NK * g) % LANES
                if shift:
                    piece = roll(piece, shift, 1)
                wide[tile] = jnp.where(here[lane // NK], piece, wide[tile])
        out.append(jnp.concatenate(wide, axis=1))
    return jnp.concatenate(out, axis=0)


def add_halo(blocks, roll, slant):
    lane = lane_iota(8)
    row = lax.broadcasted_iota(jnp.int32, (8, LANES), 0)
    out = [None] * N_COL
    for c in range(N_COL):
        after = (c + 1) % N_COL
        pair = []
        for part in range(2):
            low = slant(blocks[c][part][:8], 0)
            high = slant(roll(blocks[c][part][8:], 8 * NK, 1), 0)
            lines = jnp.zeros((8, LANES), f32)
            for h in range(3):
                first = NK * (XI + 2 - h) + NK * row
                take_low = (lane - first + 2 * LANES) % LANES < NK
                take_high = ((lane - first - 8 * NK + 3 * LANES) % LANES < NK) & (row < XI - 8)
                line = jnp.where(take_low, low, 0.0) + jnp.where(take_high, high, 0.0)
                lines = jnp.where(row == h, jnp.sum(line, axis=0, keepdims=True), lines)
            lines = slant(lines, LANES - NK * (XI + 2))
            main = blocks[after][part]
            pair.append(jnp.concatenate([main[:8] + lines, main[8:]], axis=0))
        out[after] = pair
    return out


def copy_halo(blocks, roll, slant):
    lane = lane_iota(8)
    out = []
    for c in range(N_COL):
        after = (c + 1) % N_COL
        pair = []
        for part in range(2):
            low, high = blocks[c][part][:8], blocks[c][part][8:]
            for h in range(3):
                line = jnp.broadcast_to(blocks[after][part][h : h + 1], (8, LANES))
                group = NK * (XI + 2 - h)
                here = (lane >= group) & (lane < group + NK)
                base = group - 15 * NK
                low = jnp.where(here, slant(roll(line, base % LANES, 1), 0), low)
                high = jnp.where(here, slant(line, base + 8 * NK), high)
            pair.append(jnp.concatenate([low, high], axis=0))
        out.append(pair)
    return out


def spread_to_z(neutral, cell_x, cell_y, fraction, z_high, z_low, table, roll):
    weights = spline_values(fraction)
    wx = [w[0:1] * neutral for w in weights]
    wy = [w[1:2] for w in weights]
    x_rows = place(cell_x, wx, lax.broadcasted_iota(jnp.int32, (16, ATOMS), 0))
    y_rows = place(cell_y, wy, lax.broadcasted_iota(jnp.int32, (16, ATOMS), 0))
    y_edge = y_halo_rows(cell_y, wy)
    plane = jnp.concatenate(
        [y_rows * x_rows[x : x + 1] for x in range(XI)]
        + [x_rows * y_edge[h : h + 1] for h in (2, 1, 0)],
        axis=0,
    )
    plane_high, plane_low = split(plane)
    grid = dot(plane_high, z_high, NT) + (dot(plane_low, z_high, NT) + dot(plane_high, z_low, NT))
    grid_high, grid_low = split(grid)
    wave = dot(grid_high, table[0]) + (dot(grid_low, table[0]) + dot(grid_high, table[1]))
    return to_messages(wave, roll)


def z_parts(cell_z, fraction):
    z = fraction[2:3]
    return split(place_periodic(cell_z, spline_values(z))) + split(
        place_periodic(cell_z, spline_slopes(z))
    )


def y_stage(x, table):
    high, low = split(x)
    half = table.shape[0] // 2
    both = dot(table, jnp.concatenate([high, low], axis=1))
    return both[:half, :LANES] + (both[:half, LANES:] + both[half:, :LANES])


def fft(values, sign):
    count = len(values)
    if count == 1:
        return values
    even = fft(values[0::2], sign)
    odd = fft(values[1::2], sign)
    out = [None] * count
    for k in range(count // 2):
        re, im = odd[k]
        if k == 0:
            pass
        elif 4 * k == count:
            re, im = (-sign * im, sign * re)
        else:
            angle = 2.0 * np.pi * k / count
            c, s = float(np.cos(angle)), float(sign * np.sin(angle))
            re, im = (re * c - im * s, re * s + im * c)
        er, ei = even[k]
        out[k] = (er + re, ei + im)
        out[k + count // 2] = (er - re, ei - im)
    return out


def x_turn(values, twiddle):
    out = []
    for k1, (re, im) in enumerate(values):
        cos, sin = twiddle(k1)
        out.append(jnp.concatenate([re * cos - im * sin, re * sin + im * cos], axis=1))
    return jnp.concatenate(out, axis=0)


def x_mix(wave, gain, mix):
    high, low = split(wave)
    spectrum = dot(high, mix[0]) + (dot(low, mix[0]) + dot(high, mix[1]))
    spectrum = spectrum * gain
    high, low = split(spectrum)
    return dot(high, mix[0], NT) + (dot(low, mix[0], NT) + dot(high, mix[1], NT))


def x_back(wave, twiddle):
    values = []
    for k1 in range(N_ROW):
        re = wave[k1 * 8 : (k1 + 1) * 8, :LANES]
        im = wave[k1 * 8 : (k1 + 1) * 8, LANES:]
        cos, sin = twiddle(k1)
        values.append((re * cos + im * sin, im * cos - re * sin))
    return fft(values, 1.0)


def gain_table(device, own, mirror, edge, roll):
    col = device % N_COL
    r = lax.broadcasted_iota(jnp.int32, (72, 128), 0)
    k = lax.broadcasted_iota(jnp.int32, (72, 128), 1)
    take_own = (k == r).astype(bf16)
    r = lax.broadcasted_iota(jnp.int32, (72, 64), 0)
    k = lax.broadcasted_iota(jnp.int32, (72, 64), 1)
    slot, i = r // 8, r % 8
    take_mirror = ((slot > 0) & (i > 0) & (k == (8 - slot) * 8 + 8 - i)).astype(bf16)
    r = lax.broadcasted_iota(jnp.int32, (72, 8), 0)
    k = lax.broadcasted_iota(jnp.int32, (72, 8), 1)
    take_edge = ((r // 8 > 0) & (r % 8 == 0) & (k == 8 - r // 8)).astype(bf16)
    kx = lax.broadcasted_iota(jnp.int32, (N, N), 0)
    lane = lax.broadcasted_iota(jnp.int32, (N, N), 1)
    wave = lane // 8 + 32 * (lane % 8)
    order = (kx == wave).astype(bf16)
    reverse = (kx == (N - wave) % N).astype(bf16)

    def ordered(x, select, permutation):
        high, low = split(x)
        high = dot(select, high).astype(bf16)
        low = dot(select, low).astype(bf16)
        return dot(high, permutation) + dot(low, permutation)

    gain = ordered(own, take_own, order)
    gain = gain + ordered(mirror, take_mirror, reverse) + ordered(edge, take_edge, reverse)
    row = lax.broadcasted_iota(jnp.int32, (72, N), 0)
    gain = jnp.where((row >= 64) & (col >= 8), 0.0, gain) * (1.0 / (N * N * N))
    lanes = lane_iota(8)
    out = []
    for k1 in range(N_ROW):
        tile, lane = (k1 * 8) // LANES, (k1 * 8) % LANES
        acc = jnp.zeros((8, LANES), f32)
        for slot in range(NK):
            piece = gain[slot * 8 : (slot + 1) * 8, tile * LANES : (tile + 1) * LANES]
            shift = (slot * 8 - lane) % LANES
            if shift:
                piece = roll(piece, shift, 1)
            acc = jnp.where((lanes >= slot * 8) & (lanes < slot * 8 + 8), piece, acc)
        out.append(acc)
    return out


def interpolate(wave, neutral, cell_x, cell_y, fraction, z_rows, z_slopes, table):
    weights = spline_values(fraction)
    slopes = spline_slopes(fraction)
    number = lax.broadcasted_iota(jnp.int32, (16, ATOMS), 0)
    x_rows = place(cell_x, [w[0:1] for w in weights], number)
    x_slopes = place(cell_x, [w[0:1] for w in slopes], number)
    wy = [w[1:2] for w in weights]
    vy = [w[1:2] for w in slopes]
    y_rows, y_slopes = place(cell_y, wy, number), place(cell_y, vy, number)
    x_back = place(cell_x, [w[0:1] for w in weights], 15 - number)
    x_back_slopes = place(cell_x, [w[0:1] for w in slopes], 15 - number)
    y_edge, y_edge_slopes = y_halo_rows(cell_y, wy), y_halo_rows(cell_y, vy)
    high, low = split(wave)
    grid = dot(high, table[0], NT) + (dot(low, table[0], NT) + dot(high, table[1], NT))
    grid_high, grid_low = split(grid)

    def sample(high, low):
        return dot(grid_high, high) + (dot(grid_low, high) + dot(grid_high, low))

    at = sample(*z_rows)
    at_slope = sample(*z_slopes)
    value = jnp.zeros((8, ATOMS), f32)
    grad_x, grad_y, grad_z = value, value, value

    def eight(x):
        return x[:8] + x[8:]

    for x in range(XI):
        main = at[x * CY : (x + 1) * CY]
        plain = eight(main * y_rows)
        turned = eight(main * y_slopes)
        risen = eight(at_slope[x * CY : (x + 1) * CY] * y_rows)
        value = value + plain * x_rows[x : x + 1]
        grad_x = grad_x + plain * x_slopes[x : x + 1]
        grad_y = grad_y + turned * x_rows[x : x + 1]
        grad_z = grad_z + risen * x_rows[x : x + 1]
    for h in range(3):
        rows = slice(MAIN + (2 - h) * CY, MAIN + (3 - h) * CY)
        plain = eight(at[rows] * x_back)
        weight = y_edge[h : h + 1]
        value = value + plain * weight
        grad_x = grad_x + eight(at[rows] * x_back_slopes) * weight
        grad_y = grad_y + plain * y_edge_slopes[h : h + 1]
        grad_z = grad_z + eight(at_slope[rows] * x_back) * weight

    def total(x):
        return jnp.sum(x, axis=0, keepdims=True)

    energy = 0.5 * neutral * total(value)
    force = [-neutral * total(g) for g in (grad_x, grad_y, grad_z)]
    return energy, force


def run_copies(pairs, sems):
    copies = [pltpu.make_async_copy(a, b, sems.at[i]) for i, (a, b) in enumerate(pairs)]
    for copy in copies:
        copy.start()
    return copies


def partial_kernel(dev, live, sid_hbm, charges_hbm, influence, out, mirror, sid, charges, sems):
    copies = run_copies(
        [(sid_hbm, sid), (charges_hbm, charges), (influence.at[8:16], mirror)], sems
    )
    copies[0].wait()
    copies[1].wait()
    row = partial_sums(dev[0], live[0], sid[...], charges[...])
    out[...] = jnp.broadcast_to(row, (N_COL, LANES))
    copies[2].wait()


def relay_kernel(dev, sums, out):
    rows = relay_rows(dev[0] % N_COL, lambda c: sums[pl.ds(c, 1), :], pltpu.roll)
    for k in range(N_ROW // 2):
        out[k * 8 : (k + 1) * 8, :] = rows


def prefetch_kernel(cells_hbm, fraction_hbm, z_tab, y_tab, *refs):
    z, y = refs[:2]
    parts, cells, fraction, sems = refs[2:6], refs[6], refs[7], refs[8]
    copies = run_copies([(cells_hbm, cells), (fraction_hbm, fraction), (z_tab, z), (y_tab, y)], sems)
    copies[0].wait()
    copies[1].wait()
    for ref, x in zip(parts, z_parts(cells[2:3], fraction[...])):
        ref[...] = x
    for copy in copies[2:]:
        copy.wait()


def local_cells(dev, cells):
    return (
        cells[0:1] - dev // N_COL * CX,
        cells[1:2] - dev % N_COL * CY,
        cells[2:3],
    )


def spread_kernel(
    dev, live, sums, sid_hbm, charges_hbm, cells_hbm, fraction_hbm, influence, z_high, z_low, table,
    out, neutral_out, edge,
    sid, charges, cells, fraction, neutral_buf, buf, sems, out_sems,
):
    copies = run_copies(
        [
            (sid_hbm, sid),
            (charges_hbm, charges),
            (cells_hbm, cells),
            (fraction_hbm, fraction),
            (influence.at[8:16, 0], edge),
        ],
        sems,
    )
    d = dev[0]
    row = d // N_COL

    def row_of(dr, k):
        return sums[pl.ds((row + 2 * N_ROW + dr) % N_ROW * 4 + k, 1), :]

    means = fragment_means(row_of, pltpu.roll)
    for copy in copies[:4]:
        copy.wait()
    neutral = neutral_charges(d, live[0], sid[...], charges[...], means)
    neutral_buf[...] = neutral
    leaving = [pltpu.make_async_copy(neutral_buf, neutral_out, sems.at[5])]
    leaving[0].start()
    x, y, _ = local_cells(d, cells[...])
    messages = spread_to_z(
        neutral, x, y, fraction[...], z_high[...], z_low[...], table, pltpu.roll
    )
    for c, message in enumerate(messages):
        buf[c] = message
        leaving.append(pltpu.make_async_copy(buf.at[c], out.at[c], out_sems.at[c]))
        leaving[-1].start()
    copies[4].wait()
    for copy in leaving:
        copy.wait()


def slant(x, shift):
    return pltpu.roll(x, shift, 1, stride=NK, stride_axis=0)


def pairs_of(x):
    return [[x[c, :CY], x[c, CY:]] for c in range(N_COL)]


def y_forward_kernel(x, table, out):
    blocks = add_halo(pairs_of(x), pltpu.roll, slant)
    y = y_stage(jnp.concatenate([b for pair in blocks for b in pair], axis=0), table[...])
    out[:, :, :LANES] = y[:N].reshape(N_ROW, 8, LANES)
    out[:, :, LANES:] = y[N:].reshape(N_ROW, 8, LANES)


def y_back_kernel(x, table, out):
    pieces = []
    for r in range(0, N_ROW, 2):
        pieces += [x[r, :, :LANES], x[r + 1, :, :LANES], -x[r, :, LANES:], -x[r + 1, :, LANES:]]
    y = y_stage(jnp.concatenate(pieces, axis=0), table[...])
    blocks = [
        [y[c * CY : (c + 1) * CY], -y[N + c * CY : N + (c + 1) * CY]] for c in range(N_COL)
    ]
    for c, (re, im) in enumerate(copy_halo(blocks, pltpu.roll, slant)):
        out[c, :CY] = re
        out[c, CY:] = im


def gain_kernel(dev, own_hbm, mirror_hbm, edge_hbm, out, own, mirror, edge, sems):
    for copy in run_copies([(own_hbm, own), (mirror_hbm, mirror), (edge_hbm, edge)], sems):
        copy.wait()
    flat = own[...].reshape(128, N)
    pieces = gain_table(dev[0], flat, mirror[...].reshape(64, N), edge[...], pltpu.roll)
    for k1, piece in enumerate(pieces):
        out[k1 * 8 : (k1 + 1) * 8, :LANES] = piece
        out[k1 * 8 : (k1 + 1) * 8, LANES:] = piece


def x_kernel(x, gain, twiddle_hbm, mix_hbm, out, twiddle, mix, sems):
    copies = run_copies([(twiddle_hbm, twiddle), (mix_hbm, mix)], sems)

    def factor(k1):
        return twiddle[k1, 0:1, :], twiddle[k1, 1:2, :]

    values = fft([(x[r, :, :LANES], x[r, :, LANES:]) for r in range(N_ROW)], -1.0)
    for copy in copies:
        copy.wait()
    wave = x_mix(x_turn(values, factor), gain[...], mix)
    for r, (re, im) in enumerate(x_back(wave, factor)):
        out[r, :, :LANES] = re
        out[r, :, LANES:] = im


def atom_kernel(
    dev, message, neutral_hbm, cells_hbm, fraction_hbm, zh, zl, vh, vl, table,
    force, energy,
    neutral, cells, fraction, sems,
):
    copies = run_copies(
        [(neutral_hbm, neutral), (cells_hbm, cells), (fraction_hbm, fraction)], sems
    )
    wave = from_messages(lambda c: message[c], pltpu.roll)
    for copy in copies:
        copy.wait()
    x, y, _ = local_cells(dev[0], cells[...])
    e, g = interpolate(
        wave, neutral[...], x, y, fraction[...], (zh[...], zl[...]), (vh[...], vl[...]), table
    )
    energy[...] = e
    for d in range(3):
        force[d : d + 1, :] = g[d]


KINDS = {"s": pltpu.SMEM, "v": pltpu.VMEM, "h": pltpu.HBM}


def call(kernel, outs, spaces, args, scratch=()):
    args = [
        pltpu.with_memory_space_constraint(x, pltpu.HBM) if k == "h" else x
        for k, x in zip(spaces, args)
    ]
    result = pl.pallas_call(
        kernel,
        out_shape=[
            pltpu.HBM(shape, dtype) if k == "h" else jax.ShapeDtypeStruct(shape, dtype)
            for k, shape, dtype in outs
        ],
        in_specs=[pl.BlockSpec(memory_space=KINDS[k]) for k in spaces],
        out_specs=[pl.BlockSpec(memory_space=KINDS[k]) for k, _, _ in outs],
        scratch_shapes=list(scratch),
        compiler_params=pltpu.CompilerParams(vmem_limit_bytes=16 << 20),
    )(*args)
    return result if len(outs) > 1 else result[0]


def sems(count):
    return pltpu.SemaphoreType.DMA((count,))


def swap(x, axis):
    return lax.all_to_all(x, axis, split_axis=0, concat_axis=0, tiled=True)


def body(charges, structure_id, live_count, cells, fraction, influence):
    dev = lax.axis_index(ALL).astype(jnp.int32).reshape(1)
    charges = charges.reshape(1, ATOMS)
    sid = structure_id.reshape(1, ATOMS)
    sid_buf = pltpu.VMEM((1, ATOMS), jnp.int32)
    row_buf = pltpu.VMEM((1, ATOMS), f32)
    cell_buf = pltpu.VMEM((3, ATOMS), jnp.int32)
    fraction_buf = pltpu.VMEM((3, ATOMS), f32)
    sums, mirror = call(
        partial_kernel,
        [("v", (N_COL, LANES), f32), ("h", (8, 8, N), f32)],
        "sshhh",
        (dev, live_count, sid, charges, influence),
        [sid_buf, row_buf, sems(3)],
    )
    sums = swap(sums.reshape(N_COL, 1, LANES), COL).reshape(N_COL, LANES)
    sums = call(relay_kernel, [("v", (4 * N_ROW, LANES), f32)], "sv", (dev, sums))
    sums, mirror = lax.optimization_barrier((sums, mirror))
    mirror = lax.ppermute(mirror, ALL, [(i, DEV - 1 - i) for i in range(DEV)])
    sums = swap(sums.reshape(N_ROW, 4, LANES), ROW).reshape(4 * N_ROW, LANES)
    twiddle, mix = x_tables()
    z_tab, y_tab, zh, zl, vh, vl = call(
        prefetch_kernel,
        [("v", (2, N, 3 * LANES), bf16), ("v", (4 * N, 2 * N), bf16)]
        + [("v", (N, ATOMS), bf16)] * 4,
        "hhhh",
        (cells, fraction, z_table(), y_table()),
        [cell_buf, fraction_buf, sems(4)],
    )
    sums, mirror, zh = lax.optimization_barrier((sums, mirror, zh))
    messages, neutral, edge = call(
        spread_kernel,
        [("h", (N_COL, ROWS, LANES), f32), ("h", (1, ATOMS), f32), ("h", (8, N), f32)],
        "ssvhhhhhvvv",
        (
            dev, live_count, sums, sid, charges, cells, fraction, influence,
            zh, zl, z_tab,
        ),
        [
            sid_buf, row_buf, cell_buf, fraction_buf, row_buf,
            pltpu.VMEM((N_COL, ROWS, LANES), f32), sems(6), sems(N_COL),
        ],
    )
    edge = lax.ppermute(
        edge,
        ALL,
        [(i, (N_ROW - i // N_COL) % N_ROW * N_COL + N_COL - 1 - i % N_COL) for i in range(DEV)],
    )
    columns = swap(messages, COL)
    gain = call(
        gain_kernel,
        [("v", (N, 2 * LANES), f32)],
        "shhh",
        (dev, influence, mirror, edge),
        [
            pltpu.VMEM((16, 8, N), f32), pltpu.VMEM((8, 8, N), f32), pltpu.VMEM((8, N), f32),
            sems(3),
        ],
    )
    columns, gain = lax.optimization_barrier((columns, gain))
    strip = [("v", (N_ROW, 8, 2 * LANES), f32)]
    rows = call(y_forward_kernel, strip, "vv", (columns, y_tab))
    rows = swap(rows, ROW)
    rows = call(
        x_kernel,
        strip,
        "vvhh",
        (rows, gain, twiddle, mix),
        [
            pltpu.VMEM((N_ROW, 2, LANES), f32),
            pltpu.VMEM((2, 2 * LANES, 2 * LANES), bf16),
            sems(2),
        ],
    )
    rows = swap(rows, ROW)
    columns = call(y_back_kernel, [("v", (N_COL, ROWS, LANES), f32)], "vv", (rows, y_tab))
    columns = swap(columns, COL)
    forces, energy = call(
        atom_kernel,
        [("v", (3, ATOMS), f32), ("v", (1, ATOMS), f32)],
        "svhhhvvvvv",
        (dev, columns, neutral, cells, fraction, zh, zl, vh, vl, z_tab),
        [row_buf, cell_buf, fraction_buf, sems(3)],
    )
    return forces, energy.reshape(ATOMS)


def solution(mesh):
    torus = Mesh(mesh.devices.reshape(4, 8, 8, 2), ALL)
    placed = (P(ALL), P(ALL), P(ALL), P(None, ALL), P(None, ALL), P(COL, ROW, None))
    return jax.shard_map(
        body, mesh=torus, in_specs=placed, out_specs=(P(None, ALL), P(ALL)), check_vma=False
    )
```

```python
import functools

import jax
import jax.numpy as jnp
import numpy as np
from jax import lax
from jax.experimental import pallas as pl
from jax.experimental.pallas import tpu as pltpu
from jax.sharding import Mesh
from jax.sharding import PartitionSpec as P

N_ROW = 32
N_COL = 16
DEV = N_ROW * N_COL
CX = 8
CY = 16
N = 256
ATOMS = 1024
FRAG = 8
NK = 9
XI = CX + 3
PACK = 14
LANES = 128
ROW = ("row_0", "row_1")
COL = ("col_0", "col_1")
ALL = ROW + COL
MAIN = XI * CY
PLANE = MAIN + 3 * CY
GROUPS = XI + 3
ROWS = 2 * CY
f32 = jnp.float32
bf16 = jnp.bfloat16


def kz_of(c, slot):
    if slot == 8 and c >= 8:
        return None
    return 16 * c + slot


def halves(table):
    high = table.astype(np.float32).astype(bf16)
    low = (table - high.astype(np.float64)).astype(np.float32).astype(bf16)
    return high, low


def z_lane(c, part):
    if c < PACK:
        return part * LANES + NK * c
    return 2 * LANES + NK * (2 * part + c - PACK)


@functools.cache
def z_table():
    table = np.zeros((N, 3 * LANES))
    z = np.arange(N)
    for c in range(N_COL):
        for slot in range(NK):
            kz = kz_of(c, slot)
            if kz is None:
                continue
            angle = 2.0 * np.pi * (kz * z % N) / N
            table[:, z_lane(c, 0) + slot] = np.cos(angle)
            table[:, z_lane(c, 1) + slot] = -np.sin(angle)
    return np.stack(halves(table))


@functools.cache
def y_table():
    k = np.arange(N)
    angle = (2.0 * np.pi / N) * (k[:, None] * k[None, :] % N)
    cos = np.cos(angle).reshape(N, N_COL, CY)
    sin = np.sin(angle).reshape(N, N_COL, CY)
    table = np.zeros((2, N, N_COL, 2, CY))
    table[0, :, :, 0] = cos
    table[0, :, :, 1] = sin
    table[1, :, :, 0] = -sin
    table[1, :, :, 1] = cos
    return np.concatenate(halves(table.reshape(2 * N, 2 * N)), axis=0)


@functools.cache
def x_tables():
    twiddle = np.zeros((N_ROW, 2, LANES))
    k1 = np.arange(N_ROW)
    mix = np.zeros((2, LANES, 2, LANES))
    for i in range(XI):
        angle = 2.0 * np.pi * (i * k1 % N) / N
        for slot in range(NK):
            twiddle[:, 0, i * NK + slot] = np.cos(angle)
            twiddle[:, 1, i * NK + slot] = -np.sin(angle)
            for k2 in range(8):
                a = 2.0 * np.pi * (i * k2 % 8) / 8
                src, dst = i * NK + slot, slot * 8 + k2
                mix[0, src, 0, dst] = np.cos(a)
                mix[0, src, 1, dst] = -np.sin(a)
                mix[1, src, 0, dst] = np.sin(a)
                mix[1, src, 1, dst] = np.cos(a)
    return twiddle.astype(np.float32), np.stack(halves(mix.reshape(2 * LANES, 2 * LANES)))


def split(x):
    high = x.astype(bf16)
    low = (x - high.astype(f32)).astype(bf16)
    return high, low


def dot(a, b, dims=(((1,), (0,)), ((), ()))):
    return lax.dot_general(a, b, dims, preferred_element_type=f32)


NT = (((1,), (1,)), ((), ()))


def spline_values(fraction):
    remain = 1.0 - fraction
    square = fraction * fraction
    cubic = square * fraction
    return (
        remain * remain * remain * (1.0 / 6.0),
        (3.0 * cubic - 6.0 * square + 4.0) * (1.0 / 6.0),
        (-3.0 * cubic + 3.0 * square + 3.0 * fraction + 1.0) * (1.0 / 6.0),
        cubic * (1.0 / 6.0),
    )


def spline_slopes(fraction):
    remain = 1.0 - fraction
    square = fraction * fraction
    return (
        -0.5 * remain * remain,
        0.5 * (3.0 * square - 4.0 * fraction),
        0.5 * (-3.0 * square + 2.0 * fraction + 1.0),
        0.5 * square,
    )


def place(cell, weights, number):
    out = jnp.zeros(number.shape, f32)
    for offset in range(4):
        out = jnp.where(number == cell + offset, weights[offset], out)
    return out


def place_periodic(cell, weights):
    number = lax.broadcasted_iota(jnp.int32, (N, ATOMS), 0)
    out = jnp.zeros((N, ATOMS), f32)
    for offset in range(4):
        out = jnp.where(number == (cell + offset) % N, weights[offset], out)
    return out


def y_halo_rows(cell, weights):
    return place(cell, weights, CY + lax.broadcasted_iota(jnp.int32, (8, ATOMS), 0))


STEPS = ((0, 0), (1, 0), (-1, 0), (0, 1), (0, -1), (N_ROW // 2, 0))


def owners(device):
    row = device // N_COL
    col = device % N_COL
    return [
        (row + N_ROW + dr) % N_ROW * N_COL + (col + N_COL + dc) % N_COL for dr, dc in STEPS
    ]


def member_masks(device, live, sid):
    row = lax.broadcasted_iota(jnp.int32, (8, ATOMS), 0)
    lane = lax.broadcasted_iota(jnp.int32, (8, ATOMS), 1)
    alive = lane < live
    return [(sid == row + owner * FRAG) & alive for owner in owners(device)]


def partial_sums(device, live, sid, charges):
    row = lax.broadcasted_iota(jnp.int32, (8, LANES), 0)
    lane = lax.broadcasted_iota(jnp.int32, (8, LANES), 1)
    acc = jnp.zeros((8, LANES), f32)
    for slot, mask in enumerate(member_masks(device, live, sid)):
        total = jnp.sum(jnp.where(mask, charges, 0.0), axis=1, keepdims=True)
        count = jnp.sum(jnp.where(mask, 1.0, 0.0), axis=1, keepdims=True)
        acc = jnp.where(lane == 16 * slot + row, total, acc)
        acc = jnp.where(lane == 16 * slot + 8 + row, count, acc)
    return jnp.sum(acc, axis=0, keepdims=True)


def fragment_means(row_of, roll):
    row = lax.broadcasted_iota(jnp.int32, (8, LANES), 0)
    lane = lax.broadcasted_iota(jnp.int32, (8, LANES), 1)
    means = []
    for owner_row, owner_col in STEPS:
        total = jnp.zeros((1, LANES), f32)
        for slot, (dr, dc) in enumerate(STEPS):
            step = owner_col - dc
            if abs(step) == 2:
                k, start = 1 + step // 2, 96
            else:
                k, start = 1 + step, 16 * slot
            part = row_of(owner_row - dr, k)
            total = total + (roll(part, LANES - start, 1) if start else part)
        mean = total / roll(total, LANES - 8, 1)
        mean = jnp.where(lane == row, jnp.broadcast_to(mean, (8, LANES)), 0.0)
        means.append(jnp.sum(mean, axis=1, keepdims=True))
    return means


def relay_rows(col, sums, roll):
    row = lax.broadcasted_iota(jnp.int32, (8, LANES), 0)
    lane = lax.broadcasted_iota(jnp.int32, (8, LANES), 1)
    near = [sums((col + N_COL + k) % N_COL) for k in (-2, -1, 0, 1, 2)]
    first = jnp.where(lane < 96, near[1], roll(near[0], 48, 1))
    last = jnp.where(lane < 96, near[3], roll(near[4], 32, 1))
    out = jnp.where(row % 4 == 0, first, last)
    return jnp.where(row % 4 == 1, near[2], out)


SPREAD_ROWS = 16 + 16 + 8 + 8 + 48
ATOM_ROWS = 16 * 6 + 8 * 2


def atom_weights(cell_x, cell_y, fraction):
    number = lax.broadcasted_iota(jnp.int32, (16, ATOMS), 0)
    weights = spline_values(fraction)
    slopes = spline_slopes(fraction)
    wx, vx = [w[0:1] for w in weights], [w[0:1] for w in slopes]
    wy, vy = [w[1:2] for w in weights], [w[1:2] for w in slopes]
    return [
        place(cell_x, wx, number),
        place(cell_x, vx, number),
        place(cell_x, wx, 15 - number),
        place(cell_x, vx, 15 - number),
        place(cell_y, wy, number),
        place(cell_y, vy, number),
        y_halo_rows(cell_y, wy),
        y_halo_rows(cell_y, vy),
    ]


def spread_rows(device, live, sid, charges, weights):
    alive = lax.broadcasted_iota(jnp.int32, (8, ATOMS), 1) < live
    row = lax.broadcasted_iota(jnp.int32, (8, ATOMS), 0)
    basis = jnp.where(alive, jnp.where(row == 0, charges, 1.0), 0.0)
    masks = [jnp.where(m, 1.0, 0.0) for m in member_masks(device, live, sid)]
    return [weights[0], weights[4], weights[6], basis] + masks


def neutral_charges(pack, means):
    acc = jnp.zeros((8, ATOMS), f32)
    for slot, mean in enumerate(means):
        acc = acc + pack[48 + 8 * slot : 56 + 8 * slot] * mean
    return pack[40:41] - jnp.sum(acc, axis=0, keepdims=True)


def lane_iota(rows):
    return lax.broadcasted_iota(jnp.int32, (rows, LANES), 1)


def group_tile(c, part):
    lane = z_lane(c, part)
    return lane // LANES, lane % LANES


def to_messages(wave, roll):
    lanes = lane_iota(CY)
    here = [(lanes >= NK * g) & (lanes < NK * g + NK) for g in range(GROUPS)]
    out = []
    for c in range(N_COL):
        parts = []
        for part in range(2):
            tile, lane = group_tile(c, part)
            acc = jnp.zeros((CY, LANES), f32)
            for g in range(GROUPS):
                piece = wave[g * CY : (g + 1) * CY, tile * LANES : (tile + 1) * LANES]
                shift = (NK * g - lane) % LANES
                if shift:
                    piece = roll(piece, shift, 1)
                acc = jnp.where(here[g], piece, acc)
            parts.append(acc)
        out.append(jnp.concatenate(parts, axis=0))
    return out


def from_messages(message, roll):
    lanes = lane_iota(CY)
    here = [(lanes >= NK * g) & (lanes < NK * g + NK) for g in range(GROUPS)]
    out = []
    for g in range(GROUPS):
        wide = [jnp.zeros((CY, LANES), f32) for _ in range(3)]
        for c in range(N_COL):
            block = message(c)
            for part in range(2):
                tile, lane = group_tile(c, part)
                piece = block[part * CY : (part + 1) * CY]
                shift = (lane - NK * g) % LANES
                if shift:
                    piece = roll(piece, shift, 1)
                wide[tile] = jnp.where(here[lane // NK], piece, wide[tile])
        out.append(jnp.concatenate(wide, axis=1))
    return jnp.concatenate(out, axis=0)


def add_halo(blocks, roll, slant):
    lane = lane_iota(8)
    row = lax.broadcasted_iota(jnp.int32, (8, LANES), 0)
    out = [None] * N_COL
    for c in range(N_COL):
        after = (c + 1) % N_COL
        pair = []
        for part in range(2):
            low = slant(blocks[c][part][:8], 0)
            high = slant(roll(blocks[c][part][8:], 8 * NK, 1), 0)
            lines = jnp.zeros((8, LANES), f32)
            for h in range(3):
                first = NK * (XI + 2 - h) + NK * row
                take_low = (lane - first + 2 * LANES) % LANES < NK
                take_high = ((lane - first - 8 * NK + 3 * LANES) % LANES < NK) & (row < XI - 8)
                line = jnp.where(take_low, low, 0.0) + jnp.where(take_high, high, 0.0)
                lines = jnp.where(row == h, jnp.sum(line, axis=0, keepdims=True), lines)
            lines = slant(lines, LANES - NK * (XI + 2))
            main = blocks[after][part]
            pair.append(jnp.concatenate([main[:8] + lines, main[8:]], axis=0))
        out[after] = pair
    return out


def copy_halo(blocks, roll, slant):
    lane = lane_iota(8)
    out = []
    for c in range(N_COL):
        after = (c + 1) % N_COL
        pair = []
        for part in range(2):
            low, high = blocks[c][part][:8], blocks[c][part][8:]
            for h in range(3):
                line = jnp.broadcast_to(blocks[after][part][h : h + 1], (8, LANES))
                group = NK * (XI + 2 - h)
                here = (lane >= group) & (lane < group + NK)
                base = group - 15 * NK
                low = jnp.where(here, slant(roll(line, base % LANES, 1), 0), low)
                high = jnp.where(here, slant(line, base + 8 * NK), high)
            pair.append(jnp.concatenate([low, high], axis=0))
        out.append(pair)
    return out


def spread_to_z(neutral, pack, z_high, z_low, table, roll):
    x_rows = pack[0:16] * neutral
    y_rows = pack[16:32]
    y_edge = pack[32:40]
    plane = jnp.concatenate(
        [y_rows * x_rows[x : x + 1] for x in range(XI)]
        + [x_rows * y_edge[h : h + 1] for h in (2, 1, 0)],
        axis=0,
    )
    plane_high, plane_low = split(plane)
    grid = dot(plane_high, z_high, NT) + (dot(plane_low, z_high, NT) + dot(plane_high, z_low, NT))
    grid_high, grid_low = split(grid)
    wave = dot(grid_high, table[0]) + (dot(grid_low, table[0]) + dot(grid_high, table[1]))
    return to_messages(wave, roll)


def y_stage(x, table):
    high, low = split(x)
    half = table.shape[0] // 2
    both = dot(table, jnp.concatenate([high, low], axis=1))
    return both[:half, :LANES] + (both[:half, LANES:] + both[half:, :LANES])


def fft(values, sign):
    count = len(values)
    if count == 1:
        return values
    even = fft(values[0::2], sign)
    odd = fft(values[1::2], sign)
    out = [None] * count
    for k in range(count // 2):
        re, im = odd[k]
        if k == 0:
            pass
        elif 4 * k == count:
            re, im = (-sign * im, sign * re)
        else:
            angle = 2.0 * np.pi * k / count
            c, s = float(np.cos(angle)), float(sign * np.sin(angle))
            re, im = (re * c - im * s, re * s + im * c)
        er, ei = even[k]
        out[k] = (er + re, ei + im)
        out[k + count // 2] = (er - re, ei - im)
    return out


def x_turn(values, twiddle):
    out = []
    for k1, (re, im) in enumerate(values):
        cos, sin = twiddle(k1)
        out.append(jnp.concatenate([re * cos - im * sin, re * sin + im * cos], axis=1))
    return jnp.concatenate(out, axis=0)


def x_mix(wave, gain, mix):
    high, low = split(wave)
    spectrum = dot(high, mix[0]) + (dot(low, mix[0]) + dot(high, mix[1]))
    spectrum = spectrum * gain
    high, low = split(spectrum)
    return dot(high, mix[0], NT) + (dot(low, mix[0], NT) + dot(high, mix[1], NT))


def x_back(wave, twiddle):
    values = []
    for k1 in range(N_ROW):
        re = wave[k1 * 8 : (k1 + 1) * 8, :LANES]
        im = wave[k1 * 8 : (k1 + 1) * 8, LANES:]
        cos, sin = twiddle(k1)
        values.append((re * cos + im * sin, im * cos - re * sin))
    return fft(values, 1.0)


def gain_table(device, own, mirror, edge, roll):
    col = device % N_COL
    r = lax.broadcasted_iota(jnp.int32, (72, 128), 0)
    k = lax.broadcasted_iota(jnp.int32, (72, 128), 1)
    take_own = ((r % 8 < 7) & (k == r + 1)).astype(bf16)
    r = lax.broadcasted_iota(jnp.int32, (72, 64), 0)
    k = lax.broadcasted_iota(jnp.int32, (72, 64), 1)
    take_mirror = ((r >= 8) & (k == (8 - r // 8) * 8 + 7 - r % 8)).astype(bf16)
    r = lax.broadcasted_iota(jnp.int32, (72, NK), 0)
    k = lax.broadcasted_iota(jnp.int32, (72, NK), 1)
    take_edge = ((r % 8 == 7) & (k == r // 8)).astype(bf16)
    kx = lax.broadcasted_iota(jnp.int32, (N, N), 0)
    lane = lax.broadcasted_iota(jnp.int32, (N, N), 1)
    wave = lane // 8 + 32 * (lane % 8)
    order = (kx == wave).astype(bf16)
    reverse = (kx == (N - wave) % N).astype(bf16)

    def ordered(x, select, permutation):
        high, low = split(x)
        high = dot(select, high).astype(bf16)
        low = dot(select, low).astype(bf16)
        return dot(high, permutation) + dot(low, permutation)

    gain = ordered(own, take_own, order)
    gain = gain + ordered(mirror, take_mirror, reverse) + ordered(edge, take_edge, order)
    row = lax.broadcasted_iota(jnp.int32, (72, N), 0)
    gain = jnp.where((row >= 64) & (col >= 8), 0.0, gain) * (1.0 / (N * N * N))
    lanes = lane_iota(8)
    out = []
    for k1 in range(N_ROW):
        tile, lane = (k1 * 8) // LANES, (k1 * 8) % LANES
        acc = jnp.zeros((8, LANES), f32)
        for slot in range(NK):
            piece = gain[slot * 8 : (slot + 1) * 8, tile * LANES : (tile + 1) * LANES]
            shift = (slot * 8 - lane) % LANES
            if shift:
                piece = roll(piece, shift, 1)
            acc = jnp.where((lanes >= slot * 8) & (lanes < slot * 8 + 8), piece, acc)
        out.append(acc)
    return out


def interpolate(wave, neutral, pack, z_rows, z_slopes, table):
    x_rows, x_slopes, x_back, x_back_slopes, y_rows, y_slopes = [
        pack[16 * k : 16 * (k + 1)] for k in range(6)
    ]
    y_edge, y_edge_slopes = pack[96:104], pack[104:112]
    high, low = split(wave)
    grid = dot(high, table[0], NT) + (dot(low, table[0], NT) + dot(high, table[1], NT))
    grid_high, grid_low = split(grid)

    def sample(high, low):
        return dot(grid_high, high) + (dot(grid_low, high) + dot(grid_high, low))

    at = sample(*z_rows)
    at_slope = sample(*z_slopes)
    value = jnp.zeros((8, ATOMS), f32)
    grad_x, grad_y, grad_z = value, value, value

    def eight(x):
        return x[:8] + x[8:]

    for x in range(XI):
        main = at[x * CY : (x + 1) * CY]
        plain = eight(main * y_rows)
        turned = eight(main * y_slopes)
        risen = eight(at_slope[x * CY : (x + 1) * CY] * y_rows)
        value = value + plain * x_rows[x : x + 1]
        grad_x = grad_x + plain * x_slopes[x : x + 1]
        grad_y = grad_y + turned * x_rows[x : x + 1]
        grad_z = grad_z + risen * x_rows[x : x + 1]
    for h in range(3):
        rows = slice(MAIN + (2 - h) * CY, MAIN + (3 - h) * CY)
        plain = eight(at[rows] * x_back)
        weight = y_edge[h : h + 1]
        value = value + plain * weight
        grad_x = grad_x + eight(at[rows] * x_back_slopes) * weight
        grad_y = grad_y + plain * y_edge_slopes[h : h + 1]
        grad_z = grad_z + eight(at_slope[rows] * x_back) * weight

    def total(x):
        return jnp.sum(x, axis=0, keepdims=True)

    energy = 0.5 * neutral * total(value)
    force = [-neutral * total(g) for g in (grad_x, grad_y, grad_z)]
    return energy, force


def run_copies(pairs, sems):
    copies = [pltpu.make_async_copy(a, b, sems.at[i]) for i, (a, b) in enumerate(pairs)]
    for copy in copies:
        copy.start()
    return copies


def partial_kernel(
    dev, live, sid_hbm, charges_hbm, influence, out, mirror, edge, sid, charges, sems
):
    copies = run_copies(
        [
            (sid_hbm, sid),
            (charges_hbm, charges),
            (influence.at[8:16], mirror),
            (influence.at[0:NK, 0], edge),
        ],
        sems,
    )
    copies[0].wait()
    copies[1].wait()
    row = partial_sums(dev[0], live[0], sid[...], charges[...])
    out[...] = jnp.broadcast_to(row, (N_COL, LANES))
    copies[2].wait()
    copies[3].wait()


def relay_kernel(dev, sums, out):
    rows = relay_rows(dev[0] % N_COL, lambda c: sums[pl.ds(c, 1), :], pltpu.roll)
    for k in range(N_ROW // 2):
        out[k * 8 : (k + 1) * 8, :] = rows


def prefetch_kernel(
    dev, live, cells_hbm, fraction_hbm, sid_hbm, charges_hbm, own_hbm, z_tab, y_tab, turn_tab,
    own, z, y, turn, spread_pack, zh, zl, atom_pack_hbm, vh_hbm, vl_hbm,
    cells, fraction, sid, charges, atom_pack, vh, vl, sems,
):
    copies = run_copies(
        [
            (cells_hbm, cells),
            (fraction_hbm, fraction),
            (sid_hbm, sid),
            (charges_hbm, charges),
            (own_hbm, own),
            (z_tab, z),
            (y_tab, y),
            (turn_tab, turn),
        ],
        sems,
    )
    for copy in copies[:4]:
        copy.wait()
    z_cell = cells[2:3]
    vh[...], vl[...] = split(place_periodic(z_cell, spline_slopes(fraction[2:3])))
    x, y_cell, _ = local_cells(dev[0], cells[...])
    weights = atom_weights(x, y_cell, fraction[...])
    start = 0
    for rows in weights:
        atom_pack[start : start + rows.shape[0], :] = rows
        start += rows.shape[0]
    pairs = [(atom_pack, atom_pack_hbm), (vh, vh_hbm), (vl, vl_hbm)]
    leaving = [pltpu.make_async_copy(a, b, sems.at[8 + i]) for i, (a, b) in enumerate(pairs)]
    for copy in leaving:
        copy.start()
    start = 0
    for rows in spread_rows(dev[0], live[0], sid[...], charges[...], weights):
        spread_pack[start : start + rows.shape[0], :] = rows
        start += rows.shape[0]
    zh[...], zl[...] = split(place_periodic(z_cell, spline_values(fraction[2:3])))
    for copy in copies[4:] + leaving:
        copy.wait()


def local_cells(dev, cells):
    return (
        cells[0:1] - dev // N_COL * CX,
        cells[1:2] - dev % N_COL * CY,
        cells[2:3],
    )


def spread_kernel(dev, sums, pack, z_high, z_low, table, out, neutral_out):
    row = dev[0] // N_COL

    def row_of(dr, k):
        return sums[pl.ds((row + 2 * N_ROW + dr) % N_ROW * 4 + k, 1), :]

    neutral = neutral_charges(pack, fragment_means(row_of, pltpu.roll))
    neutral_out[...] = neutral
    messages = spread_to_z(neutral, pack, z_high[...], z_low[...], table, pltpu.roll)
    for c, message in enumerate(messages):
        out[c] = message


def slant(x, shift):
    return pltpu.roll(x, shift, 1, stride=NK, stride_axis=0)


def pairs_of(x):
    return [[x[c, :CY], x[c, CY:]] for c in range(N_COL)]


def y_forward_kernel(x, table, out):
    blocks = add_halo(pairs_of(x), pltpu.roll, slant)
    y = y_stage(jnp.concatenate([b for pair in blocks for b in pair], axis=0), table[...])
    out[:, :, :LANES] = pltpu.roll(y[:N], N - 1, 0).reshape(N_ROW, 8, LANES)
    out[:, :, LANES:] = pltpu.roll(y[N:], N - 1, 0).reshape(N_ROW, 8, LANES)


def y_back_kernel(x, table, out):
    re = pltpu.roll(x[:, :, :LANES].reshape(N, LANES), 1, 0)
    im = -pltpu.roll(x[:, :, LANES:].reshape(N, LANES), 1, 0)
    pieces = []
    for c in range(N_COL):
        pieces += [re[c * CY : (c + 1) * CY], im[c * CY : (c + 1) * CY]]
    y = y_stage(jnp.concatenate(pieces, axis=0), table[...])
    blocks = [
        [y[c * CY : (c + 1) * CY], -y[N + c * CY : N + (c + 1) * CY]] for c in range(N_COL)
    ]
    for c, (re, im) in enumerate(copy_halo(blocks, pltpu.roll, slant)):
        out[c, :CY] = re
        out[c, CY:] = im


def gain_kernel(dev, own, mirror, edge, out):
    flat = own[...].reshape(128, N)
    pieces = gain_table(dev[0], flat, mirror[...].reshape(64, N), edge[...], pltpu.roll)
    for k1, piece in enumerate(pieces):
        out[k1 * 8 : (k1 + 1) * 8, :LANES] = piece
        out[k1 * 8 : (k1 + 1) * 8, LANES:] = piece


def x_kernel(x, gain, twiddle, mix, out):
    def factor(k1):
        return twiddle[k1, 0:1, :], twiddle[k1, 1:2, :]

    values = fft([(x[r, :, :LANES], x[r, :, LANES:]) for r in range(N_ROW)], -1.0)
    wave = x_mix(x_turn(values, factor), gain[...], mix)
    for r, (re, im) in enumerate(x_back(wave, factor)):
        out[r, :, :LANES] = re
        out[r, :, LANES:] = im


def atom_kernel(message, neutral, pack, zh, zl, vh, vl, table, force, energy):
    wave = from_messages(lambda c: message[c], pltpu.roll)
    e, g = interpolate(
        wave, neutral[...], pack, (zh[...], zl[...]), (vh[...], vl[...]), table
    )
    energy[...] = e
    for d in range(3):
        force[d : d + 1, :] = g[d]


KINDS = {"s": pltpu.SMEM, "v": pltpu.VMEM, "h": pltpu.HBM}


def call(kernel, outs, spaces, args, scratch=()):
    args = [
        pltpu.with_memory_space_constraint(x, pltpu.HBM) if k == "h" else x
        for k, x in zip(spaces, args)
    ]
    result = pl.pallas_call(
        kernel,
        out_shape=[
            pltpu.HBM(shape, dtype) if k == "h" else jax.ShapeDtypeStruct(shape, dtype)
            for k, shape, dtype in outs
        ],
        in_specs=[pl.BlockSpec(memory_space=KINDS[k]) for k in spaces],
        out_specs=[pl.BlockSpec(memory_space=KINDS[k]) for k, _, _ in outs],
        scratch_shapes=list(scratch),
        compiler_params=pltpu.CompilerParams(vmem_limit_bytes=16 << 20),
    )(*args)
    return result if len(outs) > 1 else result[0]


def sems(count):
    return pltpu.SemaphoreType.DMA((count,))


def swap(x, axis):
    return lax.all_to_all(x, axis, split_axis=0, concat_axis=0, tiled=True)


def body(charges, structure_id, live_count, cells, fraction, influence):
    dev = lax.axis_index(ALL).astype(jnp.int32).reshape(1)
    charges = charges.reshape(1, ATOMS)
    sid = structure_id.reshape(1, ATOMS)
    sums, mirror, edge = call(
        partial_kernel,
        [("v", (N_COL, LANES), f32), ("v", (8, 8, N), f32), ("v", (NK, N), f32)],
        "sshhh",
        (dev, live_count, sid, charges, influence),
        [pltpu.VMEM((1, ATOMS), jnp.int32), pltpu.VMEM((1, ATOMS), f32), sems(4)],
    )
    edge = lax.ppermute(edge, ROW, [((i + 1) % N_ROW, i) for i in range(N_ROW)])
    sums = swap(sums.reshape(N_COL, 1, LANES), COL).reshape(N_COL, LANES)
    sums = call(relay_kernel, [("v", (4 * N_ROW, LANES), f32)], "sv", (dev, sums))
    sums, mirror = lax.optimization_barrier((sums, mirror))
    mirror = lax.ppermute(mirror, ALL, [(i, DEV - 1 - i) for i in range(DEV)])
    sums = swap(sums.reshape(N_ROW, 4, LANES), ROW).reshape(4 * N_ROW, LANES)
    twiddle, mix = x_tables()
    sources = (cells, fraction, sid, charges, influence, z_table(), y_table(), twiddle)
    half = ((N, ATOMS), bf16)
    own, z_tab, y_tab, twiddle, spread_pack, zh, zl, atom_pack, vh, vl = call(
        prefetch_kernel,
        [("v", x.shape, x.dtype) for x in sources[4:]]
        + [("v", (SPREAD_ROWS, ATOMS), f32), ("v",) + half, ("v",) + half]
        + [("h", (ATOM_ROWS, ATOMS), f32), ("h",) + half, ("h",) + half],
        "ss" + "h" * len(sources),
        (dev, live_count) + sources,
        [
            pltpu.VMEM((3, ATOMS), jnp.int32), pltpu.VMEM((3, ATOMS), f32),
            pltpu.VMEM((1, ATOMS), jnp.int32), pltpu.VMEM((1, ATOMS), f32),
            pltpu.VMEM((ATOM_ROWS, ATOMS), f32), pltpu.VMEM(*half), pltpu.VMEM(*half), sems(11),
        ],
    )
    gain = call(gain_kernel, [("v", (N, 2 * LANES), f32)], "svvv", (dev, own, mirror, edge))
    zh, gain = lax.optimization_barrier((zh, gain))
    messages, neutral = call(
        spread_kernel,
        [("v", (N_COL, ROWS, LANES), f32), ("v", (1, ATOMS), f32)],
        "svvvvv",
        (dev, sums, spread_pack, zh, zl, z_tab),
    )
    columns = swap(messages, COL)
    strip = [("v", (N_ROW, 8, 2 * LANES), f32)]
    rows = call(y_forward_kernel, strip, "vv", (columns, y_tab))
    rows = swap(rows, ROW)
    rows = call(x_kernel, strip, "vvvv", (rows, gain, twiddle, mix))
    rows = swap(rows, ROW)
    columns = call(y_back_kernel, [("v", (N_COL, ROWS, LANES), f32)], "vv", (rows, y_tab))
    columns = swap(columns, COL)
    forces, energy = call(
        atom_kernel,
        [("v", (3, ATOMS), f32), ("v", (1, ATOMS), f32)],
        "vvvvvvvv",
        (columns, neutral, atom_pack, zh, zl, vh, vl, z_tab),
    )
    return forces, energy.reshape(ATOMS)


def solution(mesh):
    torus = Mesh(mesh.devices.reshape(4, 8, 8, 2), ALL)
    placed = (P(ALL), P(ALL), P(ALL), P(None, ALL), P(None, ALL), P(COL, ROW, None))
    return jax.shard_map(
        body, mesh=torus, in_specs=placed, out_specs=(P(None, ALL), P(ALL)), check_vma=False
    )
```

```python
import functools

import jax
import jax.numpy as jnp
import numpy as np
from jax import lax
from jax.experimental import pallas as pl
from jax.experimental.pallas import tpu as pltpu
from jax.sharding import Mesh
from jax.sharding import PartitionSpec as P

N_ROW = 32
N_COL = 16
DEV = N_ROW * N_COL
CX = 8
CY = 16
N = 256
ATOMS = 1024
FRAG = 8
NK = 9
XI = CX + 3
PACK = 14
LANES = 128
ROW = ("row_0", "row_1")
COL = ("col_0", "col_1")
ALL = ROW + COL
MAIN = XI * CY
PLANE = MAIN + 3 * CY
GROUPS = XI + 3
ROWS = 2 * CY
f32 = jnp.float32
bf16 = jnp.bfloat16


def kz_of(c, slot):
    if slot == 8 and c >= 8:
        return None
    return 16 * c + slot


def halves(table):
    high = table.astype(np.float32).astype(bf16)
    low = (table - high.astype(np.float64)).astype(np.float32).astype(bf16)
    return high, low


def z_lane(c, part):
    if c < PACK:
        return part * LANES + NK * c
    return 2 * LANES + NK * (2 * part + c - PACK)


@functools.cache
def z_table():
    table = np.zeros((N, 3 * LANES))
    z = np.arange(N)
    for c in range(N_COL):
        for slot in range(NK):
            kz = kz_of(c, slot)
            if kz is None:
                continue
            angle = 2.0 * np.pi * (kz * z % N) / N
            table[:, z_lane(c, 0) + slot] = np.cos(angle)
            table[:, z_lane(c, 1) + slot] = -np.sin(angle)
    return np.stack(halves(table))


@functools.cache
def y_table():
    k = np.arange(N)
    angle = (2.0 * np.pi / N) * (k[:, None] * k[None, :] % N)
    cos = np.cos(angle).reshape(N, N_COL, CY)
    sin = np.sin(angle).reshape(N, N_COL, CY)
    table = np.zeros((2, N, N_COL, 2, CY))
    table[0, :, :, 0] = cos
    table[0, :, :, 1] = sin
    table[1, :, :, 0] = -sin
    table[1, :, :, 1] = cos
    return np.concatenate(halves(table.reshape(2 * N, 2 * N)), axis=0)


@functools.cache
def x_tables():
    twiddle = np.zeros((N_ROW, 2, LANES))
    k1 = np.arange(N_ROW)
    mix = np.zeros((2, LANES, 2, LANES))
    for i in range(XI):
        angle = 2.0 * np.pi * (i * k1 % N) / N
        for slot in range(NK):
            twiddle[:, 0, i * NK + slot] = np.cos(angle)
            twiddle[:, 1, i * NK + slot] = -np.sin(angle)
            for k2 in range(8):
                a = 2.0 * np.pi * (i * k2 % 8) / 8
                src, dst = i * NK + slot, slot * 8 + k2
                mix[0, src, 0, dst] = np.cos(a)
                mix[0, src, 1, dst] = -np.sin(a)
                mix[1, src, 0, dst] = np.sin(a)
                mix[1, src, 1, dst] = np.cos(a)
    return twiddle.astype(np.float32), np.stack(halves(mix.reshape(2 * LANES, 2 * LANES)))


def split(x):
    high = x.astype(bf16)
    low = (x - high.astype(f32)).astype(bf16)
    return high, low


def dot(a, b, dims=(((1,), (0,)), ((), ()))):
    return lax.dot_general(a, b, dims, preferred_element_type=f32)


NT = (((1,), (1,)), ((), ()))


def spline_values(fraction):
    remain = 1.0 - fraction
    square = fraction * fraction
    cubic = square * fraction
    return (
        remain * remain * remain * (1.0 / 6.0),
        (3.0 * cubic - 6.0 * square + 4.0) * (1.0 / 6.0),
        (-3.0 * cubic + 3.0 * square + 3.0 * fraction + 1.0) * (1.0 / 6.0),
        cubic * (1.0 / 6.0),
    )


def spline_slopes(fraction):
    remain = 1.0 - fraction
    square = fraction * fraction
    return (
        -0.5 * remain * remain,
        0.5 * (3.0 * square - 4.0 * fraction),
        0.5 * (-3.0 * square + 2.0 * fraction + 1.0),
        0.5 * square,
    )


def place(cell, weights, number):
    out = jnp.zeros(number.shape, f32)
    for offset in range(4):
        out = jnp.where(number == cell + offset, weights[offset], out)
    return out


def place_periodic(cell, weights):
    number = lax.broadcasted_iota(jnp.int32, (N, ATOMS), 0)
    out = jnp.zeros((N, ATOMS), f32)
    for offset in range(4):
        out = jnp.where(number == (cell + offset) % N, weights[offset], out)
    return out


def y_halo_rows(cell, weights):
    return place(cell, weights, CY + lax.broadcasted_iota(jnp.int32, (8, ATOMS), 0))


STEPS = ((0, 0), (1, 0), (-1, 0), (0, 1), (0, -1), (N_ROW // 2, 0))


def owners(device):
    row = device // N_COL
    col = device % N_COL
    return [
        (row + N_ROW + dr) % N_ROW * N_COL + (col + N_COL + dc) % N_COL for dr, dc in STEPS
    ]


def member_masks(device, live, sid):
    row = lax.broadcasted_iota(jnp.int32, (8, ATOMS), 0)
    lane = lax.broadcasted_iota(jnp.int32, (8, ATOMS), 1)
    alive = lane < live
    return [(sid == row + owner * FRAG) & alive for owner in owners(device)]


def partial_sums(device, live, sid, charges):
    row = lax.broadcasted_iota(jnp.int32, (8, LANES), 0)
    lane = lax.broadcasted_iota(jnp.int32, (8, LANES), 1)
    acc = jnp.zeros((8, LANES), f32)
    for slot, mask in enumerate(member_masks(device, live, sid)):
        total = jnp.sum(jnp.where(mask, charges, 0.0), axis=1, keepdims=True)
        count = jnp.sum(jnp.where(mask, 1.0, 0.0), axis=1, keepdims=True)
        acc = jnp.where(lane == 16 * slot + row, total, acc)
        acc = jnp.where(lane == 16 * slot + 8 + row, count, acc)
    return jnp.sum(acc, axis=0, keepdims=True)


def fragment_means(row_of, roll):
    row = lax.broadcasted_iota(jnp.int32, (8, LANES), 0)
    lane = lax.broadcasted_iota(jnp.int32, (8, LANES), 1)
    means = []
    for owner_row, owner_col in STEPS:
        total = jnp.zeros((1, LANES), f32)
        for slot, (dr, dc) in enumerate(STEPS):
            step = owner_col - dc
            if abs(step) == 2:
                k, start = 1 + step // 2, 96
            else:
                k, start = 1 + step, 16 * slot
            part = row_of(owner_row - dr, k)
            total = total + (roll(part, LANES - start, 1) if start else part)
        mean = total / roll(total, LANES - 8, 1)
        mean = jnp.where(lane == row, jnp.broadcast_to(mean, (8, LANES)), 0.0)
        means.append(jnp.sum(mean, axis=1, keepdims=True))
    return means


def relay_rows(col, sums, roll):
    row = lax.broadcasted_iota(jnp.int32, (8, LANES), 0)
    lane = lax.broadcasted_iota(jnp.int32, (8, LANES), 1)
    near = [sums((col + N_COL + k) % N_COL) for k in (-2, -1, 0, 1, 2)]
    first = jnp.where(lane < 96, near[1], roll(near[0], 48, 1))
    last = jnp.where(lane < 96, near[3], roll(near[4], 32, 1))
    out = jnp.where(row % 4 == 0, first, last)
    return jnp.where(row % 4 == 1, near[2], out)


SPREAD_ROWS = 16 + 16 + 8 + 8 + 48
ATOM_ROWS = 16 * 6 + 8 * 2


def atom_weights(cell_x, cell_y, fraction):
    number = lax.broadcasted_iota(jnp.int32, (16, ATOMS), 0)
    weights = spline_values(fraction)
    slopes = spline_slopes(fraction)
    wx, vx = [w[0:1] for w in weights], [w[0:1] for w in slopes]
    wy, vy = [w[1:2] for w in weights], [w[1:2] for w in slopes]
    return [
        place(cell_x, wx, number),
        place(cell_x, vx, number),
        place(cell_x, wx, 15 - number),
        place(cell_x, vx, 15 - number),
        place(cell_y, wy, number),
        place(cell_y, vy, number),
        y_halo_rows(cell_y, wy),
        y_halo_rows(cell_y, vy),
    ]


def spread_rows(device, live, sid, charges, weights):
    alive = lax.broadcasted_iota(jnp.int32, (8, ATOMS), 1) < live
    row = lax.broadcasted_iota(jnp.int32, (8, ATOMS), 0)
    basis = jnp.where(alive, jnp.where(row == 0, charges, 1.0), 0.0)
    masks = [jnp.where(m, 1.0, 0.0) for m in member_masks(device, live, sid)]
    return [weights[0], weights[4], weights[6], basis] + masks


def neutral_charges(pack, means):
    acc = jnp.zeros((8, ATOMS), f32)
    for slot, mean in enumerate(means):
        acc = acc + pack[48 + 8 * slot : 56 + 8 * slot] * mean
    return pack[40:41] - jnp.sum(acc, axis=0, keepdims=True)


def lane_iota(rows):
    return lax.broadcasted_iota(jnp.int32, (rows, LANES), 1)


def group_tile(c, part):
    lane = z_lane(c, part)
    return lane // LANES, lane % LANES


def to_messages(wave, roll):
    lanes = lane_iota(CY)
    here = [(lanes >= NK * g) & (lanes < NK * g + NK) for g in range(GROUPS)]
    out = []
    for c in range(N_COL):
        parts = []
        for part in range(2):
            tile, lane = group_tile(c, part)
            acc = jnp.zeros((CY, LANES), f32)
            for g in range(GROUPS):
                piece = wave[g * CY : (g + 1) * CY, tile * LANES : (tile + 1) * LANES]
                shift = (NK * g - lane) % LANES
                if shift:
                    piece = roll(piece, shift, 1)
                acc = jnp.where(here[g], piece, acc)
            parts.append(acc)
        out.append(jnp.concatenate(parts, axis=0))
    return out


def from_messages(message, roll):
    lanes = lane_iota(CY)
    here = [(lanes >= NK * g) & (lanes < NK * g + NK) for g in range(GROUPS)]
    out = []
    for g in range(GROUPS):
        wide = [jnp.zeros((CY, LANES), f32) for _ in range(3)]
        for c in range(N_COL):
            block = message(c)
            for part in range(2):
                tile, lane = group_tile(c, part)
                piece = block[part * CY : (part + 1) * CY]
                shift = (lane - NK * g) % LANES
                if shift:
                    piece = roll(piece, shift, 1)
                wide[tile] = jnp.where(here[lane // NK], piece, wide[tile])
        out.append(jnp.concatenate(wide, axis=1))
    return jnp.concatenate(out, axis=0)


def add_halo(blocks, roll, slant):
    lane = lane_iota(8)
    row = lax.broadcasted_iota(jnp.int32, (8, LANES), 0)
    out = [None] * N_COL
    for c in range(N_COL):
        after = (c + 1) % N_COL
        pair = []
        for part in range(2):
            low = slant(blocks[c][part][:8], 0)
            high = slant(roll(blocks[c][part][8:], 8 * NK, 1), 0)
            lines = jnp.zeros((8, LANES), f32)
            for h in range(3):
                first = NK * (XI + 2 - h) + NK * row
                take_low = (lane - first + 2 * LANES) % LANES < NK
                take_high = ((lane - first - 8 * NK + 3 * LANES) % LANES < NK) & (row < XI - 8)
                line = jnp.where(take_low, low, 0.0) + jnp.where(take_high, high, 0.0)
                lines = jnp.where(row == h, jnp.sum(line, axis=0, keepdims=True), lines)
            lines = slant(lines, LANES - NK * (XI + 2))
            main = blocks[after][part]
            pair.append(jnp.concatenate([main[:8] + lines, main[8:]], axis=0))
        out[after] = pair
    return out


def copy_halo(blocks, roll, slant):
    lane = lane_iota(8)
    out = []
    for c in range(N_COL):
        after = (c + 1) % N_COL
        pair = []
        for part in range(2):
            low, high = blocks[c][part][:8], blocks[c][part][8:]
            for h in range(3):
                line = jnp.broadcast_to(blocks[after][part][h : h + 1], (8, LANES))
                group = NK * (XI + 2 - h)
                here = (lane >= group) & (lane < group + NK)
                base = group - 15 * NK
                low = jnp.where(here, slant(roll(line, base % LANES, 1), 0), low)
                high = jnp.where(here, slant(line, base + 8 * NK), high)
            pair.append(jnp.concatenate([low, high], axis=0))
        out.append(pair)
    return out


def spread_to_z(neutral, pack, z_high, z_low, table, roll):
    x_rows = pack[0:16] * neutral
    y_rows = pack[16:32]
    y_edge = pack[32:40]
    plane = jnp.concatenate(
        [y_rows * x_rows[x : x + 1] for x in range(XI)]
        + [x_rows * y_edge[h : h + 1] for h in (2, 1, 0)],
        axis=0,
    )
    plane_high, plane_low = split(plane)
    grid = dot(plane_high, z_high, NT) + (dot(plane_low, z_high, NT) + dot(plane_high, z_low, NT))
    grid_high, grid_low = split(grid)
    wave = dot(grid_high, table[0]) + (dot(grid_low, table[0]) + dot(grid_high, table[1]))
    return to_messages(wave, roll)


def y_stage(x, table):
    high, low = split(x)
    half = table.shape[0] // 2
    both = dot(table, jnp.concatenate([high, low], axis=1))
    return both[:half, :LANES] + (both[:half, LANES:] + both[half:, :LANES])


def fft(values, sign):
    count = len(values)
    if count == 1:
        return values
    even = fft(values[0::2], sign)
    odd = fft(values[1::2], sign)
    out = [None] * count
    for k in range(count // 2):
        re, im = odd[k]
        if k == 0:
            pass
        elif 4 * k == count:
            re, im = (-sign * im, sign * re)
        else:
            angle = 2.0 * np.pi * k / count
            c, s = float(np.cos(angle)), float(sign * np.sin(angle))
            re, im = (re * c - im * s, re * s + im * c)
        er, ei = even[k]
        out[k] = (er + re, ei + im)
        out[k + count // 2] = (er - re, ei - im)
    return out


def x_turn(values, twiddle):
    out = []
    for k1, (re, im) in enumerate(values):
        cos, sin = twiddle(k1)
        out.append(jnp.concatenate([re * cos - im * sin, re * sin + im * cos], axis=1))
    return jnp.concatenate(out, axis=0)


def x_mix(wave, gain, mix):
    high, low = split(wave)
    spectrum = dot(high, mix[0]) + (dot(low, mix[0]) + dot(high, mix[1]))
    spectrum = spectrum * gain
    high, low = split(spectrum)
    return dot(high, mix[0], NT) + (dot(low, mix[0], NT) + dot(high, mix[1], NT))


def x_back(wave, twiddle):
    values = []
    for k1 in range(N_ROW):
        re = wave[k1 * 8 : (k1 + 1) * 8, :LANES]
        im = wave[k1 * 8 : (k1 + 1) * 8, LANES:]
        cos, sin = twiddle(k1)
        values.append((re * cos + im * sin, im * cos - re * sin))
    return fft(values, 1.0)


def gain_table(device, own, mirror, edge, roll):
    col = device % N_COL
    r = lax.broadcasted_iota(jnp.int32, (72, 128), 0)
    k = lax.broadcasted_iota(jnp.int32, (72, 128), 1)
    take_own = (k == r).astype(bf16)
    r = lax.broadcasted_iota(jnp.int32, (72, 64), 0)
    k = lax.broadcasted_iota(jnp.int32, (72, 64), 1)
    slot, i = r // 8, r % 8
    take_mirror = ((slot > 0) & (i > 0) & (k == (8 - slot) * 8 + 8 - i)).astype(bf16)
    r = lax.broadcasted_iota(jnp.int32, (72, 8), 0)
    k = lax.broadcasted_iota(jnp.int32, (72, 8), 1)
    take_edge = ((r // 8 > 0) & (r % 8 == 0) & (k == 8 - r // 8)).astype(bf16)
    kx = lax.broadcasted_iota(jnp.int32, (N, N), 0)
    lane = lax.broadcasted_iota(jnp.int32, (N, N), 1)
    wave = lane // 8 + 32 * (lane % 8)
    order = (kx == wave).astype(bf16)
    reverse = (kx == (N - wave) % N).astype(bf16)

    def ordered(x, select, permutation):
        high, low = split(x)
        high = dot(select, high).astype(bf16)
        low = dot(select, low).astype(bf16)
        return dot(high, permutation) + dot(low, permutation)

    gain = ordered(own, take_own, order)
    gain = gain + ordered(mirror, take_mirror, reverse) + ordered(edge, take_edge, reverse)
    row = lax.broadcasted_iota(jnp.int32, (72, N), 0)
    gain = jnp.where((row >= 64) & (col >= 8), 0.0, gain) * (1.0 / (N * N * N))
    lanes = lane_iota(8)
    out = []
    for k1 in range(N_ROW):
        tile, lane = (k1 * 8) // LANES, (k1 * 8) % LANES
        acc = jnp.zeros((8, LANES), f32)
        for slot in range(NK):
            piece = gain[slot * 8 : (slot + 1) * 8, tile * LANES : (tile + 1) * LANES]
            shift = (slot * 8 - lane) % LANES
            if shift:
                piece = roll(piece, shift, 1)
            acc = jnp.where((lanes >= slot * 8) & (lanes < slot * 8 + 8), piece, acc)
        out.append(acc)
    return out


def interpolate(wave, neutral, pack, z_rows, z_slopes, table):
    x_rows, x_slopes, x_back, x_back_slopes, y_rows, y_slopes = [
        pack[16 * k : 16 * (k + 1)] for k in range(6)
    ]
    y_edge, y_edge_slopes = pack[96:104], pack[104:112]
    high, low = split(wave)
    grid = dot(high, table[0], NT) + (dot(low, table[0], NT) + dot(high, table[1], NT))
    grid_high, grid_low = split(grid)

    def sample(high, low):
        return dot(grid_high, high) + (dot(grid_low, high) + dot(grid_high, low))

    at = sample(*z_rows)
    at_slope = sample(*z_slopes)
    value = jnp.zeros((8, ATOMS), f32)
    grad_x, grad_y, grad_z = value, value, value

    def eight(x):
        return x[:8] + x[8:]

    for x in range(XI):
        main = at[x * CY : (x + 1) * CY]
        plain = eight(main * y_rows)
        turned = eight(main * y_slopes)
        risen = eight(at_slope[x * CY : (x + 1) * CY] * y_rows)
        value = value + plain * x_rows[x : x + 1]
        grad_x = grad_x + plain * x_slopes[x : x + 1]
        grad_y = grad_y + turned * x_rows[x : x + 1]
        grad_z = grad_z + risen * x_rows[x : x + 1]
    for h in range(3):
        rows = slice(MAIN + (2 - h) * CY, MAIN + (3 - h) * CY)
        plain = eight(at[rows] * x_back)
        weight = y_edge[h : h + 1]
        value = value + plain * weight
        grad_x = grad_x + eight(at[rows] * x_back_slopes) * weight
        grad_y = grad_y + plain * y_edge_slopes[h : h + 1]
        grad_z = grad_z + eight(at_slope[rows] * x_back) * weight

    def total(x):
        return jnp.sum(x, axis=0, keepdims=True)

    energy = 0.5 * neutral * total(value)
    force = [-neutral * total(g) for g in (grad_x, grad_y, grad_z)]
    return energy, force


def run_copies(pairs, sems):
    copies = [pltpu.make_async_copy(a, b, sems.at[i]) for i, (a, b) in enumerate(pairs)]
    for copy in copies:
        copy.start()
    return copies


def partial_kernel(dev, live, sid_hbm, charges_hbm, out, sid, charges, sems):
    for copy in run_copies([(sid_hbm, sid), (charges_hbm, charges)], sems):
        copy.wait()
    row = partial_sums(dev[0], live[0], sid[...], charges[...])
    out[...] = jnp.broadcast_to(row, (N_COL, LANES))


def relay_kernel(dev, sums, out):
    rows = relay_rows(dev[0] % N_COL, lambda c: sums[pl.ds(c, 1), :], pltpu.roll)
    for k in range(N_ROW // 2):
        out[k * 8 : (k + 1) * 8, :] = rows


def mirror_of(device):
    return DEV - 1 - device


def edge_mirror_of(device):
    return (N_ROW - device // N_COL) % N_ROW * N_COL + N_COL - 1 - device % N_COL


def pairs_by(partner):
    return [[d, partner(d)] for d in range(DEV) if d < partner(d)]


def prefetch_kernel(
    dev, live, cells_hbm, fraction_hbm, sid_hbm, charges_hbm, influence, z_tab, y_tab, turn_tab,
    own, z, y, turn, spread_pack, zh, zl, atom_pack_hbm, vh_hbm, vl_hbm, mirror_hbm, edge_hbm,
    cells, fraction, sid, charges, atom_pack, vh, vl, mirror, edge, sems,
):
    d = dev[0]
    slot = jnp.where(d < mirror_of(d), 8, 0)
    edge_slot = jnp.where(d < edge_mirror_of(d), 8, 0)
    mirror[pl.ds(8 - slot, 8)] = jnp.zeros((8, 8, N), f32)
    edge[pl.ds(pl.multiple_of(8 - edge_slot, 8), 8), :] = jnp.zeros((8, N), f32)
    copies = run_copies(
        [
            (cells_hbm, cells),
            (fraction_hbm, fraction),
            (sid_hbm, sid),
            (charges_hbm, charges),
            (influence.at[8:16], mirror.at[pl.ds(slot, 8)]),
            (influence.at[8:16, 0], edge.at[pl.ds(pl.multiple_of(edge_slot, 8), 8), :]),
            (influence, own),
            (z_tab, z),
            (y_tab, y),
            (turn_tab, turn),
        ],
        sems,
    )
    for copy in copies[:4]:
        copy.wait()
    z_cell = cells[2:3]
    vh[...], vl[...] = split(place_periodic(z_cell, spline_slopes(fraction[2:3])))
    x, y_cell, _ = local_cells(d, cells[...])
    weights = atom_weights(x, y_cell, fraction[...])
    start = 0
    for rows in weights:
        atom_pack[start : start + rows.shape[0], :] = rows
        start += rows.shape[0]
    copies[4].wait()
    copies[5].wait()
    pairs = [
        (mirror, mirror_hbm),
        (edge, edge_hbm),
        (atom_pack, atom_pack_hbm),
        (vh, vh_hbm),
        (vl, vl_hbm),
    ]
    leaving = [pltpu.make_async_copy(a, b, sems.at[10 + i]) for i, (a, b) in enumerate(pairs)]
    for copy in leaving:
        copy.start()
    start = 0
    for rows in spread_rows(d, live[0], sid[...], charges[...], weights):
        spread_pack[start : start + rows.shape[0], :] = rows
        start += rows.shape[0]
    zh[...], zl[...] = split(place_periodic(z_cell, spline_values(fraction[2:3])))
    for copy in copies[6:] + leaving:
        copy.wait()


def local_cells(dev, cells):
    return (
        cells[0:1] - dev // N_COL * CX,
        cells[1:2] - dev % N_COL * CY,
        cells[2:3],
    )


def spread_kernel(dev, sums, pack, z_high, z_low, table, out, neutral_out):
    row = dev[0] // N_COL

    def row_of(dr, k):
        return sums[pl.ds((row + 2 * N_ROW + dr) % N_ROW * 4 + k, 1), :]

    neutral = neutral_charges(pack, fragment_means(row_of, pltpu.roll))
    neutral_out[...] = neutral
    messages = spread_to_z(neutral, pack, z_high[...], z_low[...], table, pltpu.roll)
    for c, message in enumerate(messages):
        out[c] = message


def slant(x, shift):
    return pltpu.roll(x, shift, 1, stride=NK, stride_axis=0)


def pairs_of(x):
    return [[x[c, :CY], x[c, CY:]] for c in range(N_COL)]


def y_forward_kernel(x, table, out):
    blocks = add_halo(pairs_of(x), pltpu.roll, slant)
    y = y_stage(jnp.concatenate([b for pair in blocks for b in pair], axis=0), table[...])
    out[:, :, :LANES] = y[:N].reshape(N_ROW, 8, LANES)
    out[:, :, LANES:] = y[N:].reshape(N_ROW, 8, LANES)


def y_back_kernel(x, table, out):
    re = x[:, :, :LANES].reshape(N, LANES)
    im = -x[:, :, LANES:].reshape(N, LANES)
    pieces = []
    for c in range(N_COL):
        pieces += [re[c * CY : (c + 1) * CY], im[c * CY : (c + 1) * CY]]
    y = y_stage(jnp.concatenate(pieces, axis=0), table[...])
    blocks = [
        [y[c * CY : (c + 1) * CY], -y[N + c * CY : N + (c + 1) * CY]] for c in range(N_COL)
    ]
    for c, (re, im) in enumerate(copy_halo(blocks, pltpu.roll, slant)):
        out[c, :CY] = re
        out[c, CY:] = im


def gain_kernel(dev, own, mirror, edge, out):
    flat = own[...].reshape(128, N)
    pieces = gain_table(dev[0], flat, mirror[...], edge[...], pltpu.roll)
    for k1, piece in enumerate(pieces):
        out[k1 * 8 : (k1 + 1) * 8, :LANES] = piece
        out[k1 * 8 : (k1 + 1) * 8, LANES:] = piece


def x_kernel(x, gain, twiddle, mix, out):
    def factor(k1):
        return twiddle[k1, 0:1, :], twiddle[k1, 1:2, :]

    values = fft([(x[r, :, :LANES], x[r, :, LANES:]) for r in range(N_ROW)], -1.0)
    wave = x_mix(x_turn(values, factor), gain[...], mix)
    for r, (re, im) in enumerate(x_back(wave, factor)):
        out[r, :, :LANES] = re
        out[r, :, LANES:] = im


def atom_kernel(message, neutral, pack, zh, zl, vh, vl, table, force, energy):
    wave = from_messages(lambda c: message[c], pltpu.roll)
    e, g = interpolate(
        wave, neutral[...], pack, (zh[...], zl[...]), (vh[...], vl[...]), table
    )
    energy[...] = e
    for d in range(3):
        force[d : d + 1, :] = g[d]


KINDS = {"s": pltpu.SMEM, "v": pltpu.VMEM, "h": pltpu.HBM}


def call(kernel, outs, spaces, args, scratch=()):
    args = [
        pltpu.with_memory_space_constraint(x, pltpu.HBM) if k == "h" else x
        for k, x in zip(spaces, args)
    ]
    result = pl.pallas_call(
        kernel,
        out_shape=[
            pltpu.HBM(shape, dtype) if k == "h" else jax.ShapeDtypeStruct(shape, dtype)
            for k, shape, dtype in outs
        ],
        in_specs=[pl.BlockSpec(memory_space=KINDS[k]) for k in spaces],
        out_specs=[pl.BlockSpec(memory_space=KINDS[k]) for k, _, _ in outs],
        scratch_shapes=list(scratch),
        compiler_params=pltpu.CompilerParams(vmem_limit_bytes=16 << 20),
    )(*args)
    return result if len(outs) > 1 else result[0]


def sems(count):
    return pltpu.SemaphoreType.DMA((count,))


def swap(x, axis):
    return lax.all_to_all(x, axis, split_axis=0, concat_axis=0, tiled=True)


def body(charges, structure_id, live_count, cells, fraction, influence):
    dev = lax.axis_index(ALL).astype(jnp.int32).reshape(1)
    charges = charges.reshape(1, ATOMS)
    sid = structure_id.reshape(1, ATOMS)
    sums = call(
        partial_kernel,
        [("v", (N_COL, LANES), f32)],
        "sshh",
        (dev, live_count, sid, charges),
        [pltpu.VMEM((1, ATOMS), jnp.int32), pltpu.VMEM((1, ATOMS), f32), sems(2)],
    )
    sums = swap(sums.reshape(N_COL, 1, LANES), COL).reshape(N_COL, LANES)
    sums = call(relay_kernel, [("v", (4 * N_ROW, LANES), f32)], "sv", (dev, sums))
    sums = swap(sums.reshape(N_ROW, 4, LANES), ROW).reshape(4 * N_ROW, LANES)
    twiddle, mix = x_tables()
    sources = (cells, fraction, sid, charges, influence, z_table(), y_table(), twiddle)
    half = ((N, ATOMS), bf16)
    own, z_tab, y_tab, twiddle, spread_pack, zh, zl, atom_pack, vh, vl, mirror, edge = call(
        prefetch_kernel,
        [("v", x.shape, x.dtype) for x in sources[4:]]
        + [("v", (SPREAD_ROWS, ATOMS), f32), ("v",) + half, ("v",) + half]
        + [("h", (ATOM_ROWS, ATOMS), f32), ("h",) + half, ("h",) + half]
        + [("h", (16, 8, N), f32), ("h", (16, N), f32)],
        "ss" + "h" * len(sources),
        (dev, live_count) + sources,
        [
            pltpu.VMEM((3, ATOMS), jnp.int32), pltpu.VMEM((3, ATOMS), f32),
            pltpu.VMEM((1, ATOMS), jnp.int32), pltpu.VMEM((1, ATOMS), f32),
            pltpu.VMEM((ATOM_ROWS, ATOMS), f32), pltpu.VMEM(*half), pltpu.VMEM(*half),
            pltpu.VMEM((16, 8, N), f32), pltpu.VMEM((16, N), f32), sems(15),
        ],
    )
    mirror = lax.psum_scatter(
        mirror.reshape(128, N), ALL, axis_index_groups=pairs_by(mirror_of), tiled=True
    )
    edge = lax.psum_scatter(edge, ALL, axis_index_groups=pairs_by(edge_mirror_of), tiled=True)
    messages, neutral = call(
        spread_kernel,
        [("v", (N_COL, ROWS, LANES), f32), ("v", (1, ATOMS), f32)],
        "svvvvv",
        (dev, sums, spread_pack, zh, zl, z_tab),
    )
    columns = swap(messages, COL)
    gain = call(gain_kernel, [("v", (N, 2 * LANES), f32)], "svvv", (dev, own, mirror, edge))
    columns, gain = lax.optimization_barrier((columns, gain))
    strip = [("v", (N_ROW, 8, 2 * LANES), f32)]
    rows = call(y_forward_kernel, strip, "vv", (columns, y_tab))
    rows = swap(rows, ROW)
    rows = call(x_kernel, strip, "vvvv", (rows, gain, twiddle, mix))
    rows = swap(rows, ROW)
    columns = call(y_back_kernel, [("v", (N_COL, ROWS, LANES), f32)], "vv", (rows, y_tab))
    columns = swap(columns, COL)
    forces, energy = call(
        atom_kernel,
        [("v", (3, ATOMS), f32), ("v", (1, ATOMS), f32)],
        "vvvvvvvv",
        (columns, neutral, atom_pack, zh, zl, vh, vl, z_tab),
    )
    return forces, energy.reshape(ATOMS)


def solution(mesh):
    torus = Mesh(mesh.devices.reshape(4, 8, 8, 2), ALL)
    placed = (P(ALL), P(ALL), P(ALL), P(None, ALL), P(None, ALL), P(COL, ROW, None))
    return jax.shard_map(
        body, mesh=torus, in_specs=placed, out_specs=(P(None, ALL), P(ALL)), check_vma=False
    )
```

```python
import functools

import jax
import jax.numpy as jnp
import numpy as np
from jax import lax
from jax.experimental import pallas as pl
from jax.experimental.pallas import tpu as pltpu
from jax.sharding import Mesh
from jax.sharding import PartitionSpec as P

N_ROW = 32
N_COL = 16
DEV = N_ROW * N_COL
CX = 8
CY = 16
N = 256
ATOMS = 1024
FRAG = 8
NK = 9
XI = CX + 3
PACK = 14
LANES = 128
ROW = ("row_0", "row_1")
COL = ("col_0", "col_1")
ALL = ROW + COL
MAIN = XI * CY
PLANE = MAIN + 3 * CY
GROUPS = XI + 3
ROWS = 2 * CY
RELAY = 24
f32 = jnp.float32
bf16 = jnp.bfloat16


def kz_of(c, slot):
    if slot == 8 and c >= 8:
        return None
    return 16 * c + slot


def halves(table):
    high = table.astype(np.float32).astype(bf16)
    low = (table - high.astype(np.float64)).astype(np.float32).astype(bf16)
    return high, low


def z_lane(c, part):
    if c < PACK:
        return part * LANES + NK * c
    return 2 * LANES + NK * (2 * part + c - PACK)


@functools.cache
def z_table():
    table = np.zeros((N, 3 * LANES))
    z = np.arange(N)
    for c in range(N_COL):
        for slot in range(NK):
            kz = kz_of(c, slot)
            if kz is None:
                continue
            angle = 2.0 * np.pi * (kz * z % N) / N
            table[:, z_lane(c, 0) + slot] = np.cos(angle)
            table[:, z_lane(c, 1) + slot] = -np.sin(angle)
    return np.stack(halves(table))


@functools.cache
def y_table():
    k = np.arange(N)
    angle = (2.0 * np.pi / N) * (k[:, None] * k[None, :] % N)
    cos = np.cos(angle).reshape(N, N_COL, CY)
    sin = np.sin(angle).reshape(N, N_COL, CY)
    table = np.zeros((2, N, N_COL, 2, CY))
    table[0, :, :, 0] = cos
    table[0, :, :, 1] = sin
    table[1, :, :, 0] = -sin
    table[1, :, :, 1] = cos
    return np.concatenate(halves(table.reshape(2 * N, 2 * N)), axis=0)


@functools.cache
def x_tables():
    twiddle = np.zeros((N_ROW, 2, LANES))
    k1 = np.arange(N_ROW)
    mix = np.zeros((2, LANES, 2, LANES))
    for i in range(XI):
        angle = 2.0 * np.pi * (i * k1 % N) / N
        for slot in range(NK):
            twiddle[:, 0, i * NK + slot] = np.cos(angle)
            twiddle[:, 1, i * NK + slot] = -np.sin(angle)
            for k2 in range(8):
                a = 2.0 * np.pi * (i * k2 % 8) / 8
                src, dst = i * NK + slot, slot * 8 + k2
                mix[0, src, 0, dst] = np.cos(a)
                mix[0, src, 1, dst] = -np.sin(a)
                mix[1, src, 0, dst] = np.sin(a)
                mix[1, src, 1, dst] = np.cos(a)
    return twiddle.astype(np.float32), np.stack(halves(mix.reshape(2 * LANES, 2 * LANES)))


def split(x):
    high = x.astype(bf16)
    low = (x - high.astype(f32)).astype(bf16)
    return high, low


def dot(a, b, dims=(((1,), (0,)), ((), ()))):
    return lax.dot_general(a, b, dims, preferred_element_type=f32)


NT = (((1,), (1,)), ((), ()))


def spline_values(fraction):
    remain = 1.0 - fraction
    square = fraction * fraction
    cubic = square * fraction
    return (
        remain * remain * remain * (1.0 / 6.0),
        (3.0 * cubic - 6.0 * square + 4.0) * (1.0 / 6.0),
        (-3.0 * cubic + 3.0 * square + 3.0 * fraction + 1.0) * (1.0 / 6.0),
        cubic * (1.0 / 6.0),
    )


def spline_slopes(fraction):
    remain = 1.0 - fraction
    square = fraction * fraction
    return (
        -0.5 * remain * remain,
        0.5 * (3.0 * square - 4.0 * fraction),
        0.5 * (-3.0 * square + 2.0 * fraction + 1.0),
        0.5 * square,
    )


def place(cell, weights, number):
    out = jnp.zeros(number.shape, f32)
    for offset in range(4):
        out = jnp.where(number == cell + offset, weights[offset], out)
    return out


def place_periodic(cell, weights):
    number = lax.broadcasted_iota(jnp.int32, (N, ATOMS), 0)
    out = jnp.zeros((N, ATOMS), f32)
    for offset in range(4):
        out = jnp.where(number == (cell + offset) % N, weights[offset], out)
    return out


def y_halo_rows(cell, weights):
    return place(cell, weights, CY + lax.broadcasted_iota(jnp.int32, (8, ATOMS), 0))


STEPS = ((0, 0), (1, 0), (-1, 0), (0, 1), (0, -1), (N_ROW // 2, 0))


def owners(device):
    row = device // N_COL
    col = device % N_COL
    return [
        (row + N_ROW + dr) % N_ROW * N_COL + (col + N_COL + dc) % N_COL for dr, dc in STEPS
    ]


def member_masks(device, live, sid):
    row = lax.broadcasted_iota(jnp.int32, (8, ATOMS), 0)
    lane = lax.broadcasted_iota(jnp.int32, (8, ATOMS), 1)
    alive = lane < live
    return [(sid == row + owner * FRAG) & alive for owner in owners(device)]


def partial_sums(device, live, sid, charges):
    row = lax.broadcasted_iota(jnp.int32, (8, LANES), 0)
    lane = lax.broadcasted_iota(jnp.int32, (8, LANES), 1)
    acc = jnp.zeros((8, LANES), f32)
    for slot, mask in enumerate(member_masks(device, live, sid)):
        total = jnp.sum(jnp.where(mask, charges, 0.0), axis=1, keepdims=True)
        count = jnp.sum(jnp.where(mask, 1.0, 0.0), axis=1, keepdims=True)
        acc = jnp.where(lane == 16 * slot + row, total, acc)
        acc = jnp.where(lane == 16 * slot + 8 + row, count, acc)
    return jnp.sum(acc, axis=0, keepdims=True)


def fragment_means(row_of, roll):
    row = lax.broadcasted_iota(jnp.int32, (8, LANES), 0)
    lane = lax.broadcasted_iota(jnp.int32, (8, LANES), 1)
    means = []
    for owner_row, owner_col in STEPS:
        total = jnp.zeros((1, LANES), f32)
        for slot, (dr, dc) in enumerate(STEPS):
            step = owner_col - dc
            if abs(step) == 2:
                k, start = 1 + step // 2, 96
            else:
                k, start = 1 + step, 16 * slot
            part = row_of(owner_row - dr, k)
            total = total + (roll(part, LANES - start, 1) if start else part)
        mean = total / roll(total, LANES - 8, 1)
        mean = jnp.where(lane == row, jnp.broadcast_to(mean, (8, LANES)), 0.0)
        means.append(jnp.sum(mean, axis=1, keepdims=True))
    return means


def relay_rows(col, sums, roll):
    row = lax.broadcasted_iota(jnp.int32, (8, LANES), 0)
    lane = lax.broadcasted_iota(jnp.int32, (8, LANES), 1)
    near = [sums((col + N_COL + k) % N_COL) for k in (-2, -1, 0, 1, 2)]
    first = jnp.where(lane < 96, near[1], roll(near[0], 48, 1))
    last = jnp.where(lane < 96, near[3], roll(near[4], 32, 1))
    out = jnp.where(row % 4 == 0, first, last)
    return jnp.where(row % 4 == 1, near[2], out)


SPREAD_ROWS = 16 + 16 + 8 + 8 + 48
ATOM_ROWS = 16 * 6 + 8 * 2


def atom_weights(cell_x, cell_y, fraction):
    number = lax.broadcasted_iota(jnp.int32, (16, ATOMS), 0)
    weights = spline_values(fraction)
    slopes = spline_slopes(fraction)
    wx, vx = [w[0:1] for w in weights], [w[0:1] for w in slopes]
    wy, vy = [w[1:2] for w in weights], [w[1:2] for w in slopes]
    return [
        place(cell_x, wx, number),
        place(cell_x, vx, number),
        place(cell_x, wx, 15 - number),
        place(cell_x, vx, 15 - number),
        place(cell_y, wy, number),
        place(cell_y, vy, number),
        y_halo_rows(cell_y, wy),
        y_halo_rows(cell_y, vy),
    ]


def spread_rows(device, live, sid, charges, weights):
    alive = lax.broadcasted_iota(jnp.int32, (8, ATOMS), 1) < live
    row = lax.broadcasted_iota(jnp.int32, (8, ATOMS), 0)
    basis = jnp.where(alive, jnp.where(row == 0, charges, 1.0), 0.0)
    masks = [jnp.where(m, 1.0, 0.0) for m in member_masks(device, live, sid)]
    return [weights[0], weights[4], weights[6], basis] + masks


def neutral_charges(pack, means):
    acc = jnp.zeros((8, ATOMS), f32)
    for slot, mean in enumerate(means):
        acc = acc + pack[48 + 8 * slot : 56 + 8 * slot] * mean
    return pack[40:41] - jnp.sum(acc, axis=0, keepdims=True)


def lane_iota(rows):
    return lax.broadcasted_iota(jnp.int32, (rows, LANES), 1)


def group_tile(c, part):
    lane = z_lane(c, part)
    return lane // LANES, lane % LANES


def to_messages(wave, roll):
    lanes = lane_iota(CY)
    here = [(lanes >= NK * g) & (lanes < NK * g + NK) for g in range(GROUPS)]
    out = []
    for c in range(N_COL):
        parts = []
        for part in range(2):
            tile, lane = group_tile(c, part)
            acc = jnp.zeros((CY, LANES), f32)
            for g in range(GROUPS):
                piece = wave[g * CY : (g + 1) * CY, tile * LANES : (tile + 1) * LANES]
                shift = (NK * g - lane) % LANES
                if shift:
                    piece = roll(piece, shift, 1)
                acc = jnp.where(here[g], piece, acc)
            parts.append(acc)
        out.append(jnp.concatenate(parts, axis=0))
    return out


def from_messages(message, roll):
    lanes = lane_iota(CY)
    here = [(lanes >= NK * g) & (lanes < NK * g + NK) for g in range(GROUPS)]
    out = []
    for g in range(GROUPS):
        wide = [jnp.zeros((CY, LANES), f32) for _ in range(3)]
        for c in range(N_COL):
            block = message(c)
            for part in range(2):
                tile, lane = group_tile(c, part)
                piece = block[part * CY : (part + 1) * CY]
                shift = (lane - NK * g) % LANES
                if shift:
                    piece = roll(piece, shift, 1)
                wide[tile] = jnp.where(here[lane // NK], piece, wide[tile])
        out.append(jnp.concatenate(wide, axis=1))
    return jnp.concatenate(out, axis=0)


def add_halo(blocks, roll, slant):
    lane = lane_iota(8)
    row = lax.broadcasted_iota(jnp.int32, (8, LANES), 0)
    out = [None] * N_COL
    for c in range(N_COL):
        after = (c + 1) % N_COL
        pair = []
        for part in range(2):
            low = slant(blocks[c][part][:8], 0)
            high = slant(roll(blocks[c][part][8:], 8 * NK, 1), 0)
            lines = jnp.zeros((8, LANES), f32)
            for h in range(3):
                first = NK * (XI + 2 - h) + NK * row
                take_low = (lane - first + 2 * LANES) % LANES < NK
                take_high = ((lane - first - 8 * NK + 3 * LANES) % LANES < NK) & (row < XI - 8)
                line = jnp.where(take_low, low, 0.0) + jnp.where(take_high, high, 0.0)
                lines = jnp.where(row == h, jnp.sum(line, axis=0, keepdims=True), lines)
            lines = slant(lines, LANES - NK * (XI + 2))
            main = blocks[after][part]
            pair.append(jnp.concatenate([main[:8] + lines, main[8:]], axis=0))
        out[after] = pair
    return out


def copy_halo(blocks, roll, slant):
    lane = lane_iota(8)
    out = []
    for c in range(N_COL):
        after = (c + 1) % N_COL
        pair = []
        for part in range(2):
            low, high = blocks[c][part][:8], blocks[c][part][8:]
            for h in range(3):
                line = jnp.broadcast_to(blocks[after][part][h : h + 1], (8, LANES))
                group = NK * (XI + 2 - h)
                here = (lane >= group) & (lane < group + NK)
                base = group - 15 * NK
                low = jnp.where(here, slant(roll(line, base % LANES, 1), 0), low)
                high = jnp.where(here, slant(line, base + 8 * NK), high)
            pair.append(jnp.concatenate([low, high], axis=0))
        out.append(pair)
    return out


def spread_to_z(neutral, pack, z_high, z_low, table, roll):
    x_rows = pack[0:16] * neutral
    y_rows = pack[16:32]
    y_edge = pack[32:40]
    plane = jnp.concatenate(
        [y_rows * x_rows[x : x + 1] for x in range(XI)]
        + [x_rows * y_edge[h : h + 1] for h in (2, 1, 0)],
        axis=0,
    )
    plane_high, plane_low = split(plane)
    grid = dot(plane_high, z_high, NT) + (dot(plane_low, z_high, NT) + dot(plane_high, z_low, NT))
    grid_high, grid_low = split(grid)
    wave = dot(grid_high, table[0]) + (dot(grid_low, table[0]) + dot(grid_high, table[1]))
    return to_messages(wave, roll)


def y_stage(x, table):
    high, low = split(x)
    half = table.shape[0] // 2
    both = dot(table, jnp.concatenate([high, low], axis=1))
    return both[:half, :LANES] + (both[:half, LANES:] + both[half:, :LANES])


def fft(values, sign):
    count = len(values)
    if count == 1:
        return values
    even = fft(values[0::2], sign)
    odd = fft(values[1::2], sign)
    out = [None] * count
    for k in range(count // 2):
        re, im = odd[k]
        if k == 0:
            pass
        elif 4 * k == count:
            re, im = (-sign * im, sign * re)
        else:
            angle = 2.0 * np.pi * k / count
            c, s = float(np.cos(angle)), float(sign * np.sin(angle))
            re, im = (re * c - im * s, re * s + im * c)
        er, ei = even[k]
        out[k] = (er + re, ei + im)
        out[k + count // 2] = (er - re, ei - im)
    return out


def x_turn(values, twiddle):
    out = []
    for k1, (re, im) in enumerate(values):
        cos, sin = twiddle(k1)
        out.append(jnp.concatenate([re * cos - im * sin, re * sin + im * cos], axis=1))
    return jnp.concatenate(out, axis=0)


def x_mix(wave, gain, mix):
    high, low = split(wave)
    spectrum = dot(high, mix[0]) + (dot(low, mix[0]) + dot(high, mix[1]))
    spectrum = spectrum * gain
    high, low = split(spectrum)
    return dot(high, mix[0], NT) + (dot(low, mix[0], NT) + dot(high, mix[1], NT))


def x_back(wave, twiddle):
    values = []
    for k1 in range(N_ROW):
        re = wave[k1 * 8 : (k1 + 1) * 8, :LANES]
        im = wave[k1 * 8 : (k1 + 1) * 8, LANES:]
        cos, sin = twiddle(k1)
        values.append((re * cos + im * sin, im * cos - re * sin))
    return fft(values, 1.0)


def gain_table(device, own, mirror, edge, roll):
    col = device % N_COL
    r = lax.broadcasted_iota(jnp.int32, (72, 128), 0)
    k = lax.broadcasted_iota(jnp.int32, (72, 128), 1)
    take_own = ((r % 8 < 7) & (k == r + 1)).astype(bf16)
    r = lax.broadcasted_iota(jnp.int32, (72, 64), 0)
    k = lax.broadcasted_iota(jnp.int32, (72, 64), 1)
    take_mirror = ((r >= 8) & (k == (8 - r // 8) * 8 + 7 - r % 8)).astype(bf16)
    r = lax.broadcasted_iota(jnp.int32, (72, NK), 0)
    k = lax.broadcasted_iota(jnp.int32, (72, NK), 1)
    take_edge = ((r % 8 == 7) & (k == r // 8)).astype(bf16)
    kx = lax.broadcasted_iota(jnp.int32, (N, N), 0)
    lane = lax.broadcasted_iota(jnp.int32, (N, N), 1)
    wave = lane // 8 + 32 * (lane % 8)
    order = (kx == wave).astype(bf16)
    reverse = (kx == (N - wave) % N).astype(bf16)

    def ordered(x, select, permutation):
        high, low = split(x)
        high = dot(select, high).astype(bf16)
        low = dot(select, low).astype(bf16)
        return dot(high, permutation) + dot(low, permutation)

    gain = ordered(own, take_own, order)
    gain = gain + ordered(mirror, take_mirror, reverse) + ordered(edge, take_edge, order)
    row = lax.broadcasted_iota(jnp.int32, (72, N), 0)
    gain = jnp.where((row >= 64) & (col >= 8), 0.0, gain) * (1.0 / (N * N * N))
    lanes = lane_iota(8)
    out = []
    for k1 in range(N_ROW):
        tile, lane = (k1 * 8) // LANES, (k1 * 8) % LANES
        acc = jnp.zeros((8, LANES), f32)
        for slot in range(NK):
            piece = gain[slot * 8 : (slot + 1) * 8, tile * LANES : (tile + 1) * LANES]
            shift = (slot * 8 - lane) % LANES
            if shift:
                piece = roll(piece, shift, 1)
            acc = jnp.where((lanes >= slot * 8) & (lanes < slot * 8 + 8), piece, acc)
        out.append(acc)
    return out


def interpolate(wave, neutral, pack, z_rows, z_slopes, table):
    x_rows, x_slopes, x_back, x_back_slopes, y_rows, y_slopes = [
        pack[16 * k : 16 * (k + 1)] for k in range(6)
    ]
    y_edge, y_edge_slopes = pack[96:104], pack[104:112]
    high, low = split(wave)
    grid = dot(high, table[0], NT) + (dot(low, table[0], NT) + dot(high, table[1], NT))
    grid_high, grid_low = split(grid)

    def sample(high, low):
        return dot(grid_high, high) + (dot(grid_low, high) + dot(grid_high, low))

    at = sample(*z_rows)
    at_slope = sample(*z_slopes)
    value = jnp.zeros((8, ATOMS), f32)
    grad_x, grad_y, grad_z = value, value, value

    def eight(x):
        return x[:8] + x[8:]

    for x in range(XI):
        main = at[x * CY : (x + 1) * CY]
        plain = eight(main * y_rows)
        turned = eight(main * y_slopes)
        risen = eight(at_slope[x * CY : (x + 1) * CY] * y_rows)
        value = value + plain * x_rows[x : x + 1]
        grad_x = grad_x + plain * x_slopes[x : x + 1]
        grad_y = grad_y + turned * x_rows[x : x + 1]
        grad_z = grad_z + risen * x_rows[x : x + 1]
    for h in range(3):
        rows = slice(MAIN + (2 - h) * CY, MAIN + (3 - h) * CY)
        plain = eight(at[rows] * x_back)
        weight = y_edge[h : h + 1]
        value = value + plain * weight
        grad_x = grad_x + eight(at[rows] * x_back_slopes) * weight
        grad_y = grad_y + plain * y_edge_slopes[h : h + 1]
        grad_z = grad_z + eight(at_slope[rows] * x_back) * weight

    def total(x):
        return jnp.sum(x, axis=0, keepdims=True)

    energy = 0.5 * neutral * total(value)
    force = [-neutral * total(g) for g in (grad_x, grad_y, grad_z)]
    return energy, force


def run_copies(pairs, sems):
    copies = [pltpu.make_async_copy(a, b, sems.at[i]) for i, (a, b) in enumerate(pairs)]
    for copy in copies:
        copy.start()
    return copies


def partial_kernel(dev, live, sid_hbm, charges_hbm, influence, out, edge, sid, charges, sems):
    copies = run_copies(
        [(sid_hbm, sid), (charges_hbm, charges), (influence.at[0:NK, 0], edge)], sems
    )
    copies[0].wait()
    copies[1].wait()
    row = partial_sums(dev[0], live[0], sid[...], charges[...])
    out[...] = jnp.broadcast_to(row, (N_COL, LANES))
    copies[2].wait()


def relay_kernel(dev, sums, edge, out):
    rows = relay_rows(dev[0] % N_COL, lambda c: sums[pl.ds(c, 1), :], pltpu.roll)
    sub = lax.broadcasted_iota(jnp.int32, (8, LANES), 0)
    rows = jnp.where(sub == 0, edge[8:9, :LANES], rows)
    rows = jnp.where(sub == 1, edge[8:9, LANES:], rows)
    first, second = edge[0:8, :LANES], edge[0:8, LANES:]
    for k in range(N_ROW):
        out[k * RELAY : k * RELAY + 8, :] = first
        out[k * RELAY + 8 : k * RELAY + 16, :] = second
        out[k * RELAY + 16 : k * RELAY + 24, :] = rows


def prefetch_kernel(
    dev, live, cells_hbm, fraction_hbm, sid_hbm, charges_hbm, own_hbm, z_tab, y_tab, turn_tab,
    own, z, y, turn, spread_pack, zh, zl, atom_pack_hbm, vh_hbm, vl_hbm,
    cells, fraction, sid, charges, atom_pack, vh, vl, sems,
):
    copies = run_copies(
        [
            (cells_hbm, cells),
            (fraction_hbm, fraction),
            (sid_hbm, sid),
            (charges_hbm, charges),
            (own_hbm, own),
            (z_tab, z),
            (y_tab, y),
            (turn_tab, turn),
        ],
        sems,
    )
    for copy in copies[:4]:
        copy.wait()
    z_cell = cells[2:3]
    vh[...], vl[...] = split(place_periodic(z_cell, spline_slopes(fraction[2:3])))
    x, y_cell, _ = local_cells(dev[0], cells[...])
    weights = atom_weights(x, y_cell, fraction[...])
    start = 0
    for rows in weights:
        atom_pack[start : start + rows.shape[0], :] = rows
        start += rows.shape[0]
    pairs = [(atom_pack, atom_pack_hbm), (vh, vh_hbm), (vl, vl_hbm)]
    leaving = [pltpu.make_async_copy(a, b, sems.at[8 + i]) for i, (a, b) in enumerate(pairs)]
    for copy in leaving:
        copy.start()
    start = 0
    for rows in spread_rows(dev[0], live[0], sid[...], charges[...], weights):
        spread_pack[start : start + rows.shape[0], :] = rows
        start += rows.shape[0]
    zh[...], zl[...] = split(place_periodic(z_cell, spline_values(fraction[2:3])))
    for copy in copies[4:] + leaving:
        copy.wait()


def local_cells(dev, cells):
    return (
        cells[0:1] - dev // N_COL * CX,
        cells[1:2] - dev % N_COL * CY,
        cells[2:3],
    )


def spread_kernel(dev, sums, pack, z_high, z_low, table, out, neutral_out):
    row = dev[0] // N_COL

    def row_of(dr, k):
        return sums[pl.ds((row + 2 * N_ROW + dr) % N_ROW * RELAY + 20 + k, 1), :]

    neutral = neutral_charges(pack, fragment_means(row_of, pltpu.roll))
    neutral_out[...] = neutral
    messages = spread_to_z(neutral, pack, z_high[...], z_low[...], table, pltpu.roll)
    for c, message in enumerate(messages):
        out[c] = message


def slant(x, shift):
    return pltpu.roll(x, shift, 1, stride=NK, stride_axis=0)


def pairs_of(x):
    return [[x[c, :CY], x[c, CY:]] for c in range(N_COL)]


def y_forward_kernel(x, table, out):
    blocks = add_halo(pairs_of(x), pltpu.roll, slant)
    y = y_stage(jnp.concatenate([b for pair in blocks for b in pair], axis=0), table[...])
    out[:, :, :LANES] = pltpu.roll(y[:N], N - 1, 0).reshape(N_ROW, 8, LANES)
    out[:, :, LANES:] = pltpu.roll(y[N:], N - 1, 0).reshape(N_ROW, 8, LANES)


def y_back_kernel(x, table, out):
    re = pltpu.roll(x[:, :, :LANES].reshape(N, LANES), 1, 0)
    im = -pltpu.roll(x[:, :, LANES:].reshape(N, LANES), 1, 0)
    pieces = []
    for c in range(N_COL):
        pieces += [re[c * CY : (c + 1) * CY], im[c * CY : (c + 1) * CY]]
    y = y_stage(jnp.concatenate(pieces, axis=0), table[...])
    blocks = [
        [y[c * CY : (c + 1) * CY], -y[N + c * CY : N + (c + 1) * CY]] for c in range(N_COL)
    ]
    for c, (re, im) in enumerate(copy_halo(blocks, pltpu.roll, slant)):
        out[c, :CY] = re
        out[c, CY:] = im


def gain_kernel(dev, own, mirror, sums, out):
    after = pl.multiple_of((dev[0] // N_COL + 1) % N_ROW * RELAY, 8)
    sent = sums[pl.ds(after, RELAY), :]
    edge = jnp.concatenate(
        [
            jnp.concatenate([sent[0:8], sent[16:17]], axis=0),
            jnp.concatenate([sent[8:16], sent[17:18]], axis=0),
        ],
        axis=1,
    )
    flat = own[...].reshape(128, N)
    pieces = gain_table(dev[0], flat, mirror[8:16].reshape(64, N), edge, pltpu.roll)
    for k1, piece in enumerate(pieces):
        out[k1 * 8 : (k1 + 1) * 8, :LANES] = piece
        out[k1 * 8 : (k1 + 1) * 8, LANES:] = piece


def x_kernel(x, gain, twiddle, mix, out):
    def factor(k1):
        return twiddle[k1, 0:1, :], twiddle[k1, 1:2, :]

    values = fft([(x[r, :, :LANES], x[r, :, LANES:]) for r in range(N_ROW)], -1.0)
    wave = x_mix(x_turn(values, factor), gain[...], mix)
    for r, (re, im) in enumerate(x_back(wave, factor)):
        out[r, :, :LANES] = re
        out[r, :, LANES:] = im


def atom_kernel(message, neutral, pack, zh, zl, vh, vl, table, force, energy):
    wave = from_messages(lambda c: message[c], pltpu.roll)
    e, g = interpolate(
        wave, neutral[...], pack, (zh[...], zl[...]), (vh[...], vl[...]), table
    )
    energy[...] = e
    for d in range(3):
        force[d : d + 1, :] = g[d]


KINDS = {"s": pltpu.SMEM, "v": pltpu.VMEM, "h": pltpu.HBM}


def call(kernel, outs, spaces, args, scratch=()):
    args = [
        pltpu.with_memory_space_constraint(x, pltpu.HBM) if k == "h" else x
        for k, x in zip(spaces, args)
    ]
    result = pl.pallas_call(
        kernel,
        out_shape=[
            pltpu.HBM(shape, dtype) if k == "h" else jax.ShapeDtypeStruct(shape, dtype)
            for k, shape, dtype in outs
        ],
        in_specs=[pl.BlockSpec(memory_space=KINDS[k]) for k in spaces],
        out_specs=[pl.BlockSpec(memory_space=KINDS[k]) for k, _, _ in outs],
        scratch_shapes=list(scratch),
        compiler_params=pltpu.CompilerParams(vmem_limit_bytes=16 << 20),
    )(*args)
    return result if len(outs) > 1 else result[0]


def sems(count):
    return pltpu.SemaphoreType.DMA((count,))


def swap(x, axis):
    return lax.all_to_all(x, axis, split_axis=0, concat_axis=0, tiled=True)


def body(charges, structure_id, live_count, cells, fraction, influence):
    dev = lax.axis_index(ALL).astype(jnp.int32).reshape(1)
    charges = charges.reshape(1, ATOMS)
    sid = structure_id.reshape(1, ATOMS)
    sums, edge = call(
        partial_kernel,
        [("v", (N_COL, LANES), f32), ("v", (NK, N), f32)],
        "sshhh",
        (dev, live_count, sid, charges, influence),
        [pltpu.VMEM((1, ATOMS), jnp.int32), pltpu.VMEM((1, ATOMS), f32), sems(3)],
    )
    sums = swap(sums.reshape(N_COL, 1, LANES), COL).reshape(N_COL, LANES)
    sums = call(relay_kernel, [("v", (RELAY * N_ROW, LANES), f32)], "svv", (dev, sums, edge))
    sums, mirror = lax.optimization_barrier((sums, influence))
    mirror = lax.ppermute(mirror, ALL, [(i, DEV - 1 - i) for i in range(DEV)])
    sums = swap(sums.reshape(N_ROW, RELAY, LANES), ROW).reshape(RELAY * N_ROW, LANES)
    twiddle, mix = x_tables()
    sources = (cells, fraction, sid, charges, influence, z_table(), y_table(), twiddle)
    half = ((N, ATOMS), bf16)
    own, z_tab, y_tab, twiddle, spread_pack, zh, zl, atom_pack, vh, vl = call(
        prefetch_kernel,
        [("v", x.shape, x.dtype) for x in sources[4:]]
        + [("v", (SPREAD_ROWS, ATOMS), f32), ("v",) + half, ("v",) + half]
        + [("h", (ATOM_ROWS, ATOMS), f32), ("h",) + half, ("h",) + half],
        "ss" + "h" * len(sources),
        (dev, live_count) + sources,
        [
            pltpu.VMEM((3, ATOMS), jnp.int32), pltpu.VMEM((3, ATOMS), f32),
            pltpu.VMEM((1, ATOMS), jnp.int32), pltpu.VMEM((1, ATOMS), f32),
            pltpu.VMEM((ATOM_ROWS, ATOMS), f32), pltpu.VMEM(*half), pltpu.VMEM(*half), sems(11),
        ],
    )
    gain = call(gain_kernel, [("v", (N, 2 * LANES), f32)], "svvv", (dev, own, mirror, sums))
    sums, gain = lax.optimization_barrier((sums, gain))
    messages, neutral = call(
        spread_kernel,
        [("v", (N_COL, ROWS, LANES), f32), ("v", (1, ATOMS), f32)],
        "svvvvv",
        (dev, sums, spread_pack, zh, zl, z_tab),
    )
    columns = swap(messages, COL)
    strip = [("v", (N_ROW, 8, 2 * LANES), f32)]
    rows = call(y_forward_kernel, strip, "vv", (columns, y_tab))
    rows = swap(rows, ROW)
    rows = call(x_kernel, strip, "vvvv", (rows, gain, twiddle, mix))
    rows = swap(rows, ROW)
    columns = call(y_back_kernel, [("v", (N_COL, ROWS, LANES), f32)], "vv", (rows, y_tab))
    columns = swap(columns, COL)
    forces, energy = call(
        atom_kernel,
        [("v", (3, ATOMS), f32), ("v", (1, ATOMS), f32)],
        "vvvvvvvv",
        (columns, neutral, atom_pack, zh, zl, vh, vl, z_tab),
    )
    return forces, energy.reshape(ATOMS)


def solution(mesh):
    torus = Mesh(mesh.devices.reshape(4, 8, 8, 2), ALL)
    placed = (P(ALL), P(ALL), P(ALL), P(None, ALL), P(None, ALL), P(COL, ROW, None))
    return jax.shard_map(
        body, mesh=torus, in_specs=placed, out_specs=(P(None, ALL), P(ALL)), check_vma=False
    )
```
